128 devices in a mesh: gx: 64 (over y, x, z_hi, core), gy: 2 (over z_lo).
Axes of the slice: x: 4, y: 4, z: 4 (z_hi: 2, z_lo: 2; z = z_hi * 2 + z_lo), core: 2. Of those that a mesh axis runs over, the one named last changes fastest.
Arguments:
- adjoint_in: float32 [3, 1024, 128, 256], P(None, 'gx', 'gy'), may hold values from -6 to 6
- checkpoints: bfloat16 [2, 16384, 3, 2048], P(None, ('gx', 'gy')), may hold values from -4 to 4
- send_owner: int32 [16384], P(('gx', 'gy')), may hold values from 0 to 127, as said below
- receive_rows: int32 [16384], P(('gx', 'gy')), may hold values from 0 to 255, as said below
- block_columns: int32 [4096, 8], P(('gx', 'gy')), may hold values from 0 to 35
- eddy_blocks: bfloat16 [8, 128, 128], replicated, may hold values from -0.1875 to 0.1875
- thrust: float32 [80], replicated, may hold values from 0.4 to 1
- yaw_angle: float32 [80], replicated, may hold values from -0.5 to 0.5
- turbine_place: float32 [3, 80], replicated, may hold values from 0 to 1
- turbine_tile: int32 [80], replicated, may hold values from 0 to 127
- fringe_rows: int32 [128], replicated, may hold values from 0 to 1023, as said below
Outputs:
- adjoint_out: float32 [3, 1024, 128, 256], P(None, 'gx', 'gy')
- control_gradient: float32 [2, 80], replicated
The draws below stay inside these ranges and needn't reach their ends.
Inputs may be any that keep to these rules, and one draw needn't show every extreme that they name: `send_owner`: each storage tile holds 128 slots; at most 2 of its slots name one owner, exactly 2 for some owners; every owner is named by 128 slots in all. `receive_rows`: for each owner the 128 entries name each row storage*2+rank of a slot sent to it exactly once. `fringe_rows`: distinct rows.
All inputs are finite; a program needn't handle non-finite values.
Results may differ from the reference program's by a relative error of at most 0.00086.
Values may be sent and summed in bfloat16 or wider, within the bound.
A program may use at most 128 MiB of HBM per device.

```python
import math
import jax
import jax.numpy as jnp
import numpy as np
from jax import lax

CX = 16
CY = 64
NZ = 256
PB = 128
KB = 8
STEPS = 2
CAP = 2
NTURB = 80
TILES = 128
NBLK = 128
BLK = 2048
NP = 32
NPE = 36
NX = 1024
NY = 128
NF = 128
N_GX = 64
N_GY = 2


def route_tables(key):
    base_key = jax.random.fold_in(key, 7)
    key_pattern, key_rotation, key_send, key_receive = jax.random.split(base_key, 4)
    tile_count = TILES
    levels = (jnp.arange(tile_count, dtype=jnp.int32) % 4 + 1) // 2
    pattern = jax.random.permutation(key_pattern, levels)
    rotation = jax.random.permutation(key_rotation, tile_count)
    owner_ids = jnp.arange(tile_count, dtype=jnp.int32)
    counts = pattern[(rotation[:, None] + owner_ids[None, :]) % tile_count]
    grid_rank = jnp.arange(CAP, dtype=jnp.int32)[None, None, :]
    usable = grid_rank < counts[:, :, None]
    slot_ids = owner_ids[None, :, None] * CAP + grid_rank
    sort_keys = jnp.where(usable, slot_ids, tile_count * CAP + slot_ids).reshape(tile_count, tile_count * CAP)
    ordering = jnp.argsort(sort_keys, axis=1, stable=True)[:, :NBLK]
    owners_sorted = (ordering // CAP).astype(jnp.int32)
    scores = jax.random.randint(key_send, (tile_count, NBLK), 0, 1 << 20) * NBLK + jnp.arange(NBLK, dtype=jnp.int32)[None, :]
    shuffle = jnp.argsort(scores, axis=1)
    send_owner = jnp.take_along_axis(owners_sorted, shuffle, axis=1).reshape(-1).astype(jnp.int32)
    usable_owner = jnp.transpose(usable, (1, 0, 2))
    row_ids = owner_ids[None, :, None] * CAP + grid_rank
    row_ids = jnp.broadcast_to(row_ids, (tile_count, tile_count, CAP))
    receive_keys = jnp.where(usable_owner, row_ids, tile_count * CAP + row_ids).reshape(tile_count, tile_count * CAP)
    receive_order = jnp.argsort(receive_keys, axis=1, stable=True)[:, :NBLK].astype(jnp.int32)
    receive_scores = jax.random.randint(key_receive, (tile_count, NBLK), 0, 1 << 20) * NBLK + jnp.arange(NBLK, dtype=jnp.int32)[None, :]
    receive_shuffle = jnp.argsort(receive_scores, axis=1)
    receive_rows = jnp.take_along_axis(receive_order, receive_shuffle, axis=1).reshape(-1).astype(jnp.int32)
    return (send_owner, receive_rows)


def draw_send_owner(key, part):
    return route_tables(key)[0]


def draw_receive_rows(key, part):
    return route_tables(key)[1]


def draw_fringe_rows(key, part):
    remaining = jax.random.permutation(jax.random.fold_in(key, 11), NX - 2)[:NF - 2] + 1
    return jnp.concatenate([jnp.array([NX - 1, 0], dtype=jnp.int32), remaining.astype(jnp.int32)])


def touch_ends(result, stream_key, low, largest):
    shape = result.shape
    index_at = [jax.random.randint(jax.random.fold_in(stream_key, axis), (), 0, shape[axis]) for axis in range(len(shape))]
    result = result.at[tuple(index_at)].set(low)
    longest = shape.index(max(shape))
    index_at[longest] = (index_at[longest] + 1) % shape[longest]
    return result.at[tuple(index_at)].set(largest)


def block_levels(stream_key, extent, shards, smallest, largest):
    def one(dim, blocks):
        draws = jax.random.uniform(jax.random.fold_in(jax.random.fold_in(stream_key, 6), dim), (blocks,), jnp.float32, smallest / len(shards), largest / len(shards))
        return jnp.repeat(jnp.exp(draws), extent[dim] // blocks).reshape((-1,) + (1,) * (len(extent) - dim - 1))

    factor_of = one(*shards[0])
    for cut in shards[1:]:
        factor_of = factor_of * one(*cut)
    return factor_of


def rank_bounds(count, lean):
    portions = [(1 << 20) // math.isqrt(rank ** lean) + 1 for rank in range(1, count + 1)]
    scale = 1 + sum(portions) // (1 << 30)
    return np.cumsum(np.array([max(1, weight // scale) for weight in portions]))


def ranked_ids(rng, shape, number_of, lean):
    listing = rank_bounds(number_of, lean)
    lot = jax.random.randint(jax.random.fold_in(rng, 1), shape, 0, int(listing[number_of - 1]))
    standing = jnp.searchsorted(jnp.asarray(listing, jnp.int32), lot, side="right")
    return jax.random.permutation(jax.random.fold_in(rng, 2), number_of)[standing].astype(jnp.int32)


def centred(rng, shape, width, most, shards=(), kind=jnp.bfloat16):
    loudness = block_levels(rng, shape, shards, -0.22, 0.18) if shards else 1.0
    entries = jax.random.normal(rng, shape, jnp.float32) * width * loudness
    return jnp.minimum(jnp.maximum(entries, -most), most).astype(kind)


def setup_inputs(seed: int = 0) -> dict:
    seeds = jax.random.split(jax.random.key(seed), 12)
    adjoint_in = centred(seeds[0], (3, NX, NY, NZ), 1.0, 6.0, ((1, 64), (2, 2)), jnp.float32)
    checkpoints = centred(seeds[1], (STEPS, TILES * NBLK, 3, BLK), 0.7, 4.0, ((1, 128),))
    send_owner = draw_send_owner(jax.random.fold_in(seeds[11], 71), 0)
    receive_rows = draw_receive_rows(jax.random.fold_in(seeds[11], 71), 0)
    block_columns = touch_ends(jax.random.randint(seeds[4], (TILES * NP, KB), 0, NPE), jax.random.fold_in(seeds[4], 1), 0, NPE - 1).astype(jnp.int32)
    eddy_blocks = centred(seeds[5], (KB, PB, PB), (KB * PB) ** -0.5, 0.1875)
    thrust = jnp.clip(jax.random.uniform(seeds[6], (NTURB,), jnp.float32, 0.4, 1.0), 0.4, 1.0)
    yaw_angle = jnp.clip(jax.random.uniform(seeds[7], (NTURB,), jnp.float32, -0.5, 0.5), -0.5, 0.5)
    turbine_place = jnp.clip(jax.random.uniform(seeds[8], (3, NTURB), jnp.float32, 0.0, 1.0), 0.0, 1.0)
    turbine_tile = touch_ends(ranked_ids(seeds[9], (NTURB,), TILES, 2), jax.random.fold_in(seeds[9], 3), 0, TILES - 1).astype(jnp.int32)
    fringe_rows = draw_fringe_rows(jax.random.fold_in(seeds[11], 71), 0)
    return {"adjoint_in": adjoint_in, "checkpoints": checkpoints, "send_owner": send_owner, "receive_rows": receive_rows, "block_columns": block_columns, "eddy_blocks": eddy_blocks, "thrust": thrust, "yaw_angle": yaw_angle, "turbine_place": turbine_place, "turbine_tile": turbine_tile, "fringe_rows": fringe_rows}


TIME_STEP = 0.25
BASE_VISC = 0.1
EDDY_COEF = 0.5
KERNEL_WIDTH = 1.5
FRINGE_KEEP = 0.5

def assemble(stored, send_owner, receive_rows):
    tile_count = N_GX * N_GY
    owners = send_owner.reshape(tile_count, NBLK)
    owner_ids = jnp.arange(tile_count, dtype=jnp.int32)
    onehot = (owners[:, :, None] == owner_ids[None, None, :]).astype(jnp.int32)
    slot_rank = lax.optimization_barrier(jnp.sum(jnp.cumsum(onehot, axis=1) * onehot, axis=2)) - 1
    sources = jnp.repeat(owner_ids, NBLK)
    slot_ids = jnp.arange(tile_count * NBLK, dtype=jnp.int32)
    slot_table = jnp.zeros((tile_count, tile_count, CAP), jnp.int32)
    slot_table = slot_table.at[sources, owners.reshape(-1), slot_rank.reshape(-1)].set(slot_ids)
    wanted = receive_rows.reshape(tile_count, NBLK)
    source_ids = wanted // CAP
    rank_ids = wanted % CAP
    picked = slot_table[source_ids, owner_ids[:, None], rank_ids]
    blocks = stored[picked.reshape(-1)]
    blocks = blocks.reshape(tile_count, NBLK, 3, BLK).transpose(0, 2, 1, 3)
    return blocks.reshape(N_GX, N_GY, 3, CX, CY, NZ)

def turbine_terms(tile_index, thrust, yaw_angle, turbine_place, turbine_tile, width_x, width_y, height):
    owned_mask = (turbine_tile == tile_index).astype(jnp.float32)
    spread = 2.0 * KERNEL_WIDTH * KERNEL_WIDTH
    along_x = jnp.exp(-(jnp.arange(width_x, dtype=jnp.float32)[None, :] - turbine_place[0][:, None] * width_x) ** 2 / spread)
    along_y = jnp.exp(-(jnp.arange(width_y, dtype=jnp.float32)[None, :] - turbine_place[1][:, None] * width_y) ** 2 / spread)
    along_z = jnp.exp(-(jnp.arange(height, dtype=jnp.float32)[None, :] - turbine_place[2][:, None] * (0.5 * height)) ** 2 / spread)
    plan_kernel = (along_x[:, :, None] * along_y[:, None, :]).reshape(along_x.shape[0], width_x * width_y)
    cosine = jnp.cos(yaw_angle)
    loading = owned_mask * thrust * cosine * cosine
    drag_field = jnp.dot((plan_kernel * loading[:, None]).T, along_z, precision=lax.Precision.HIGHEST)
    return (owned_mask, plan_kernel, along_z, drag_field.reshape(width_x, width_y, height))

def advance(extended, forward, columns, eddy_blocks, owned_mask, plan_kernel, along_z, drag_field, fringe_scale):
    center = extended[:, 1:-1, 1:-1, :]
    east_cells = extended[:, 2:, 1:-1, :]
    west_cells = extended[:, :-2, 1:-1, :]
    north_cells = extended[:, 1:-1, 2:, :]
    south_cells = extended[:, 1:-1, :-2, :]
    zero_plane = jnp.zeros_like(center[..., :1])
    upper_cells = jnp.concatenate([center[..., 1:], zero_plane], axis=3)
    lower_cells = jnp.concatenate([zero_plane, center[..., :-1]], axis=3)
    velocity = forward.astype(jnp.float32)
    laplace = east_cells + west_cells + north_cells + south_cells + upper_cells + lower_cells - 6.0 * center
    advect = 0.5 * (velocity[0] * (east_cells - west_cells) + velocity[1] * (north_cells - south_cells) + velocity[2] * (upper_cells - lower_cells))
    viscous = EDDY_COEF * jnp.sqrt(1.0 + lax.optimization_barrier(jnp.sum(velocity * velocity, axis=0)))
    components, width_x, width_y, height = center.shape
    z_blocks = height // PB
    planes = extended[:, :, 1:-1, :].astype(jnp.bfloat16)
    planes_x = planes.shape[1]
    patches = planes.reshape(components, planes_x, width_y, z_blocks, PB).transpose(1, 3, 0, 2, 4)
    patches = patches.reshape(planes_x * z_blocks, components, width_y, PB)
    gathered = patches[columns].astype(jnp.float32)
    product = jnp.einsum('pkcyz,kzw->pcyw', gathered, eddy_blocks.astype(jnp.float32), precision=lax.Precision.HIGHEST)
    product = product.reshape(width_x, z_blocks, components, width_y, PB).transpose(2, 0, 3, 1, 4)
    product = product.reshape(components, width_x, width_y, height)
    update = center + TIME_STEP * (advect + BASE_VISC * laplace + viscous * product)
    drag_term = TIME_STEP * drag_field * velocity[0] * center[0]
    update = update.at[0].add(-drag_term)
    update = update * fringe_scale[None, :, None, None]
    density = (velocity[0] * velocity[0] * center[0]).reshape(width_x * width_y, height)
    projected = jnp.dot(density, along_z.T, precision=lax.Precision.HIGHEST)
    gradient_part = owned_mask * lax.optimization_barrier(jnp.sum(plan_kernel.T * projected, axis=0))
    return (update, gradient_part)

def reference(adjoint_in, checkpoints, send_owner, receive_rows, block_columns, eddy_blocks, thrust, yaw_angle, turbine_place, turbine_tile, fringe_rows):
    tile_count = N_GX * N_GY
    adjoint = adjoint_in.reshape(3, N_GX, CX, N_GY, CY, NZ).transpose(1, 3, 0, 2, 4, 5)
    columns = block_columns.reshape(tile_count, CX * (NZ // PB), KB)
    rows_x = jnp.arange(NX, dtype=jnp.int32).reshape(N_GX, CX)
    fringe_hit = jnp.any(rows_x[:, :, None] == fringe_rows[None, None, :], axis=2)
    fringe_scale = jnp.where(fringe_hit, FRINGE_KEEP, 1.0).astype(jnp.float32)
    fringe_tiles = jnp.broadcast_to(fringe_scale[:, None, :], (N_GX, N_GY, CX)).reshape(tile_count, CX)
    tile_ids = jnp.arange(tile_count, dtype=jnp.int32)
    gradient_sum = jnp.zeros((NTURB,), jnp.float32)

    def one_tile(pieces):
        extended, forward, tile_columns, tile_index, tile_fringe = pieces
        owned_mask, plan_kernel, along_z, drag_field = turbine_terms(tile_index, thrust, yaw_angle, turbine_place, turbine_tile, CX, CY, NZ)
        return advance(extended, forward, tile_columns, eddy_blocks, owned_mask, plan_kernel, along_z, drag_field, tile_fringe)
    for step_index in range(STEPS):
        forward = assemble(checkpoints[STEPS - 1 - step_index], send_owner, receive_rows)
        west_plane = jnp.roll(adjoint[:, :, :, -1:], 1, axis=0)
        east_plane = jnp.roll(adjoint[:, :, :, :1], -1, axis=0)
        widened = jnp.concatenate([west_plane, adjoint, east_plane], axis=3)
        south_plane = jnp.roll(widened[:, :, :, :, -1:], 1, axis=1)
        north_plane = jnp.roll(widened[:, :, :, :, :1], -1, axis=1)
        extended = jnp.concatenate([south_plane, widened, north_plane], axis=4)
        extended = extended.reshape((tile_count,) + extended.shape[2:])
        forward = forward.reshape((tile_count,) + forward.shape[2:])
        updates, parts = lax.map(one_tile, (extended, forward, columns, tile_ids, fringe_tiles))
        adjoint = updates.reshape(N_GX, N_GY, 3, CX, CY, NZ)
        gradient_sum = gradient_sum + lax.optimization_barrier(jnp.sum(parts, axis=0))
    adjoint_out = adjoint.transpose(2, 0, 3, 1, 4, 5).reshape(3, NX, NY, NZ)
    cosine = jnp.cos(yaw_angle)
    sine = jnp.sin(yaw_angle)
    control_gradient = jnp.stack([-0.5 * TIME_STEP * cosine * cosine * gradient_sum, TIME_STEP * thrust * sine * cosine * gradient_sum])
    return (adjoint_out, control_gradient)
```

```python
import functools

import jax
import jax.numpy as jnp
from jax import lax
from jax.experimental import pallas as pl
from jax.experimental.pallas import tpu as pltpu
from jax.sharding import PartitionSpec as P

MESH = pl.DeviceIdType.MESH

PB = 128
KB = 8
CAP = 2
NZB = 2


TIME_STEP = 0.25
BASE_VISC = 0.1
EDDY_COEF = 0.5
KERNEL_WIDTH = 1.5
FRINGE_KEEP = 0.5


def padded(block, sides, width):
    for axis, dim in sides:
        count = lax.axis_size(axis)
        forward = [(i, i + 1) for i in range(count - 1)]
        forward.append((count - 1, 0))
        backward = [(target, source) for source, target in forward]
        low = lax.ppermute(
            lax.slice_in_dim(block, block.shape[dim] - width, None, axis=dim), axis, forward
        )
        high = lax.ppermute(lax.slice_in_dim(block, 0, width, axis=dim), axis, backward)
        block = jnp.concatenate([low, block, high], axis=dim)
    return block


def gather_sum_kernel(count_y, total, part_ref, out_ref, rows, send_sem, recv_sem):
    me = lax.axis_index("gx") * count_y + lax.axis_index("gy")

    def device(i):
        other = lax.rem(me + i, total)
        return (other // count_y, other % count_y)

    barrier = pltpu.get_barrier_semaphore()

    def greet(i, carry):
        pl.semaphore_signal(barrier, inc=1, device_id=device(i), device_id_type=MESH)
        return carry

    lax.fori_loop(1, total, greet, 0)
    pl.semaphore_wait(barrier, total - 1)
    rows[me] = part_ref[...]

    def send(i, carry):
        pltpu.make_async_remote_copy(
            src_ref=part_ref,
            dst_ref=rows.at[me],
            send_sem=send_sem,
            recv_sem=recv_sem,
            device_id=device(i),
            device_id_type=MESH,
        ).start()
        return carry

    lax.fori_loop(1, total, send, 0)
    everything = pltpu.make_async_remote_copy(
        src_ref=rows.at[pl.ds(0, total - 1)],
        dst_ref=rows.at[pl.ds(0, total - 1)],
        send_sem=send_sem,
        recv_sem=recv_sem,
        device_id=device(1),
        device_id_type=MESH,
    )
    everything.wait_send()
    everything.wait_recv()
    out_ref[...] = jnp.sum(rows[...], axis=0)


def gather_sum(part):
    count_y = lax.axis_size("gy")
    total = lax.axis_size("gx") * count_y
    width = part.shape[0]
    block = jnp.zeros((8, 128), jnp.float32).at[0, :width].set(part)
    summed = pl.pallas_call(
        functools.partial(gather_sum_kernel, count_y, total),
        out_shape=jax.ShapeDtypeStruct((8, 128), jnp.float32),
        in_specs=[pl.BlockSpec(memory_space=pltpu.VMEM)],
        out_specs=pl.BlockSpec(memory_space=pltpu.VMEM),
        scratch_shapes=[
            pltpu.VMEM((total, 8, 128), jnp.float32),
            pltpu.SemaphoreType.DMA(()),
            pltpu.SemaphoreType.DMA(()),
        ],
        compiler_params=pltpu.CompilerParams(collective_id=0, has_side_effects=True),
    )(block)
    return summed[0, :width]


def turbine_terms(
    tile_index, thrust, yaw_angle, turbine_place, turbine_tile, width_x, width_y, height
):
    owned_mask = (turbine_tile == tile_index).astype(jnp.float32)
    spread = 2.0 * KERNEL_WIDTH * KERNEL_WIDTH
    along_x = jnp.exp(
        -(
            (jnp.arange(width_x, dtype=jnp.float32)[None, :] - turbine_place[0][:, None] * width_x)
            ** 2
        )
        / spread
    )
    along_y = jnp.exp(
        -(
            (jnp.arange(width_y, dtype=jnp.float32)[None, :] - turbine_place[1][:, None] * width_y)
            ** 2
        )
        / spread
    )
    along_z = jnp.exp(
        -(
            (
                jnp.arange(height, dtype=jnp.float32)[None, :]
                - turbine_place[2][:, None] * (0.5 * height)
            )
            ** 2
        )
        / spread
    )
    plan_kernel = (along_x[:, :, None] * along_y[:, None, :]).reshape(
        along_x.shape[0], width_x * width_y
    )
    cosine = jnp.cos(yaw_angle)
    loading = owned_mask * thrust * cosine * cosine
    drag_field = jnp.dot(
        (plan_kernel * loading[:, None]).T, along_z, precision=lax.Precision.HIGHEST
    )
    return (owned_mask, plan_kernel, along_z, drag_field.reshape(width_x, width_y, height))


def block_selector(columns, width_x):
    count_in = (width_x + 2) * NZB
    picks = (columns[:, :, None] == jnp.arange(count_in, dtype=jnp.int32)[None, None, :]).astype(
        jnp.bfloat16
    )
    return picks.reshape(width_x, NZB, KB, width_x + 2, NZB)


def advance(
    extended,
    forward,
    selector,
    eddy_blocks,
    owned_mask,
    plan_kernel,
    along_z,
    drag_field,
    fringe_scale,
):
    center = extended[:, 1:-1, 1:-1, :]
    east_cells = extended[:, 2:, 1:-1, :]
    west_cells = extended[:, :-2, 1:-1, :]
    north_cells = extended[:, 1:-1, 2:, :]
    south_cells = extended[:, 1:-1, :-2, :]
    zero_plane = jnp.zeros_like(center[..., :1])
    upper_cells = jnp.concatenate([center[..., 1:], zero_plane], axis=3)
    lower_cells = jnp.concatenate([zero_plane, center[..., :-1]], axis=3)
    velocity = forward.astype(jnp.float32)
    laplace = (
        east_cells
        + west_cells
        + north_cells
        + south_cells
        + upper_cells
        + lower_cells
        - 6.0 * center
    )
    advect = 0.5 * (
        velocity[0] * (east_cells - west_cells)
        + velocity[1] * (north_cells - south_cells)
        + velocity[2] * (upper_cells - lower_cells)
    )
    viscous = EDDY_COEF * jnp.sqrt(1.0 + jnp.sum(velocity * velocity, axis=0))
    components, width_x, width_y, height = center.shape
    planes = extended[:, :, 1:-1, :].astype(jnp.bfloat16)
    planes = planes.reshape(components, width_x + 2, width_y, NZB, PB)
    picked = jnp.einsum(
        "xbkqc,aqycz->xbkayz", selector, planes, preferred_element_type=jnp.float32
    ).astype(jnp.bfloat16)
    product = jnp.einsum(
        "xbkayz,kzw->axybw", picked, eddy_blocks, preferred_element_type=jnp.float32
    )
    product = product.reshape(components, width_x, width_y, height)
    update = center + TIME_STEP * (advect + BASE_VISC * laplace + viscous * product)
    drag_term = TIME_STEP * drag_field * velocity[0] * center[0]
    first_only = (jnp.arange(components, dtype=jnp.int32) == 0).astype(jnp.float32)
    update = update - first_only[:, None, None, None] * drag_term[None]
    update = update * fringe_scale[None, :, None, None]
    density = (velocity[0] * velocity[0] * center[0]).reshape(width_x * width_y, height)
    projected = jnp.dot(density, along_z.T, precision=lax.Precision.HIGHEST)
    gradient_part = owned_mask * jnp.sum(plan_kernel.T * projected, axis=0)
    return (update, gradient_part)


def shards(
    adjoint_in,
    checkpoints,
    send_owner,
    receive_rows,
    block_columns,
    eddy_blocks,
    thrust,
    yaw_angle,
    turbine_place,
    turbine_tile,
    fringe_rows,
):
    count_x = lax.axis_size("gx")
    count_y = lax.axis_size("gy")
    tile_count = count_x * count_y
    tile_index = lax.axis_index("gx") * count_y + lax.axis_index("gy")
    components, width_x, width_y, height = adjoint_in.shape
    steps_total = checkpoints.shape[0]
    block_shape = checkpoints.shape[2:]
    owner_ids = jnp.arange(tile_count, dtype=jnp.int32)
    onehot = (send_owner[:, None] == owner_ids[None, :]).astype(jnp.int32)
    slot_rank = jnp.sum(jnp.cumsum(onehot, axis=0) * onehot, axis=1) - 1
    position = send_owner * CAP + slot_rank
    row_ids = jnp.arange(tile_count * CAP, dtype=jnp.int32)
    pack_table = (row_ids[:, None] == position[None, :]).astype(jnp.bfloat16)
    pick_table = (receive_rows[:, None] == row_ids[None, :]).astype(jnp.bfloat16)
    selector = block_selector(block_columns, width_x)
    rows_x = lax.axis_index("gx") * width_x + jnp.arange(width_x, dtype=jnp.int32)
    fringe_hit = jnp.any(rows_x[:, None] == fringe_rows[None, :], axis=1)
    fringe_scale = jnp.where(fringe_hit, FRINGE_KEEP, 1.0).astype(jnp.float32)
    owned_mask, plan_kernel, along_z, drag_field = turbine_terms(
        tile_index, thrust, yaw_angle, turbine_place, turbine_tile, width_x, width_y, height
    )
    adjoint = adjoint_in
    gradient_sum = jnp.zeros((thrust.shape[0],), jnp.float32)
    for step_index in range(steps_total):
        stored = checkpoints[steps_total - 1 - step_index]
        packed = jnp.einsum(
            "rs,scb->rcb", pack_table, stored, preferred_element_type=jnp.float32
        ).astype(jnp.bfloat16)
        arrived = lax.all_to_all(
            packed.reshape((tile_count, CAP) + block_shape),
            ("gx", "gy"),
            split_axis=0,
            concat_axis=0,
            tiled=True,
        )
        arrived = arrived.reshape((tile_count * CAP,) + block_shape)
        forward = jnp.einsum(
            "jr,rcb->cjb", pick_table, arrived, preferred_element_type=jnp.float32
        ).astype(jnp.bfloat16)
        forward = forward.reshape(components, width_x, width_y, height)
        extended = padded(adjoint, (("gx", 1), ("gy", 2)), 1)
        adjoint, gradient_part = advance(
            extended,
            forward,
            selector,
            eddy_blocks,
            owned_mask,
            plan_kernel,
            along_z,
            drag_field,
            fringe_scale,
        )
        gradient_sum = gradient_sum + gradient_part
    gradient_sum = gather_sum(gradient_sum)
    cosine = jnp.cos(yaw_angle)
    sine = jnp.sin(yaw_angle)
    control_gradient = jnp.stack(
        [
            -0.5 * TIME_STEP * cosine * cosine * gradient_sum,
            TIME_STEP * thrust * sine * cosine * gradient_sum,
        ]
    )
    return (adjoint, control_gradient)


def solution(mesh):
    return jax.shard_map(
        shards,
        mesh=mesh,
        in_specs=(
            P(None, "gx", "gy", None),
            P(None, ("gx", "gy"), None, None),
            P(("gx", "gy")),
            P(("gx", "gy")),
            P(("gx", "gy"), None),
            P(),
            P(),
            P(),
            P(),
            P(),
            P(),
        ),
        out_specs=(P(None, "gx", "gy", None), P()),
        check_vma=False,
    )
```

```python
import functools

import jax
import jax.numpy as jnp
from jax import lax
from jax.experimental import pallas as pl
from jax.experimental.pallas import tpu as pltpu
from jax.sharding import PartitionSpec as P

MESH = pl.DeviceIdType.MESH

PB = 128
KB = 8
CAP = 2
NZB = 2


TIME_STEP = 0.25
BASE_VISC = 0.1
EDDY_COEF = 0.5
KERNEL_WIDTH = 1.5
FRINGE_KEEP = 0.5


def gather_sum_kernel(count_y, total, part_ref, out_ref, rows, send_sem, recv_sem):
    me = lax.axis_index("gx") * count_y + lax.axis_index("gy")

    def device(i):
        other = lax.rem(me + i, total)
        return (other // count_y, other % count_y)

    barrier = pltpu.get_barrier_semaphore()

    def greet(i, carry):
        pl.semaphore_signal(barrier, inc=1, device_id=device(i), device_id_type=MESH)
        return carry

    lax.fori_loop(1, total, greet, 0)
    pl.semaphore_wait(barrier, total - 1)
    rows[me] = part_ref[...]

    def send(i, carry):
        pltpu.make_async_remote_copy(
            src_ref=part_ref,
            dst_ref=rows.at[me],
            send_sem=send_sem,
            recv_sem=recv_sem,
            device_id=device(i),
            device_id_type=MESH,
        ).start()
        return carry

    lax.fori_loop(1, total, send, 0)
    everything = pltpu.make_async_remote_copy(
        src_ref=rows.at[pl.ds(0, total - 1)],
        dst_ref=rows.at[pl.ds(0, total - 1)],
        send_sem=send_sem,
        recv_sem=recv_sem,
        device_id=device(1),
        device_id_type=MESH,
    )
    everything.wait_send()
    everything.wait_recv()
    out_ref[...] = jnp.sum(rows[...], axis=0)


def gather_sum(part):
    count_y = lax.axis_size("gy")
    total = lax.axis_size("gx") * count_y
    width = part.shape[0]
    block = jnp.zeros((8, 128), jnp.float32).at[0, :width].set(part)
    summed = pl.pallas_call(
        functools.partial(gather_sum_kernel, count_y, total),
        out_shape=jax.ShapeDtypeStruct((8, 128), jnp.float32),
        in_specs=[pl.BlockSpec(memory_space=pltpu.VMEM)],
        out_specs=pl.BlockSpec(memory_space=pltpu.VMEM),
        scratch_shapes=[
            pltpu.VMEM((total, 8, 128), jnp.float32),
            pltpu.SemaphoreType.DMA(()),
            pltpu.SemaphoreType.DMA(()),
        ],
        compiler_params=pltpu.CompilerParams(collective_id=0, has_side_effects=True),
    )(block)
    return summed[0, :width]


def turbine_terms(
    tile_index, thrust, yaw_angle, turbine_place, turbine_tile, width_x, width_y, height
):
    owned_mask = (turbine_tile == tile_index).astype(jnp.float32)
    spread = 2.0 * KERNEL_WIDTH * KERNEL_WIDTH
    along_x = jnp.exp(
        -(
            (jnp.arange(width_x, dtype=jnp.float32)[None, :] - turbine_place[0][:, None] * width_x)
            ** 2
        )
        / spread
    )
    along_y = jnp.exp(
        -(
            (jnp.arange(width_y, dtype=jnp.float32)[None, :] - turbine_place[1][:, None] * width_y)
            ** 2
        )
        / spread
    )
    along_z = jnp.exp(
        -(
            (
                jnp.arange(height, dtype=jnp.float32)[None, :]
                - turbine_place[2][:, None] * (0.5 * height)
            )
            ** 2
        )
        / spread
    )
    plan_kernel = (along_x[:, :, None] * along_y[:, None, :]).reshape(
        along_x.shape[0], width_x * width_y
    )
    cosine = jnp.cos(yaw_angle)
    loading = owned_mask * thrust * cosine * cosine
    drag_field = jnp.dot(
        (plan_kernel * loading[:, None]).T, along_z, precision=lax.Precision.HIGHEST
    )
    return (owned_mask, plan_kernel, along_z, drag_field.reshape(width_x, width_y, height))


def advance_kernel(
    cols_ref, fringe_ref, a_ref, w_ref, e_ref, s_ref, n_ref, u_ref, drag_ref, eddy_ref,
    out_ref, xq, prod,
):
    components, width_x, width_y, height = a_ref.shape
    half = height // NZB
    def fill(px, src):
        for zb in range(NZB):
            for c in range(components):
                xq[2 * px + zb, c * width_y : (c + 1) * width_y, :] = src[c, :, zb * half : (zb + 1) * half].astype(jnp.bfloat16)

    def fill_plane(x, carry):
        for zb in range(NZB):
            for c in range(components):
                xq[2 * (x + 1) + zb, c * width_y : (c + 1) * width_y, :] = a_ref[c, x, :, zb * half : (zb + 1) * half].astype(jnp.bfloat16)
        return carry

    for zb in range(NZB):
        for c in range(components):
            xq[zb, c * width_y : (c + 1) * width_y, :] = w_ref[c, 0, :, zb * half : (zb + 1) * half].astype(jnp.bfloat16)
            xq[2 * (width_x + 1) + zb, c * width_y : (c + 1) * width_y, :] = e_ref[c, 0, :, zb * half : (zb + 1) * half].astype(jnp.bfloat16)
    lax.fori_loop(0, width_x, fill_plane, 0)

    def eddy_block(p, carry):
        acc = jnp.zeros((components * width_y, half), jnp.float32)
        for k in range(KB):
            acc = acc + jnp.dot(xq[cols_ref[p, k]], eddy_ref[k], preferred_element_type=jnp.float32)
        prod[p] = acc
        return carry

    lax.fori_loop(0, width_x * NZB, eddy_block, 0)

    row = lax.broadcasted_iota(jnp.int32, (width_y, height), 0)
    lane = lax.broadcasted_iota(jnp.int32, (width_y, height), 1)

    def plane(x, carry):
        u0 = u_ref[0, x].astype(jnp.float32)
        u1 = u_ref[1, x].astype(jnp.float32)
        u2 = u_ref[2, x].astype(jnp.float32)
        viscous = EDDY_COEF * jnp.sqrt(1.0 + (u0 * u0 + u1 * u1 + u2 * u2))
        west_index = jnp.maximum(x - 1, 0)
        east_index = jnp.minimum(x + 1, width_x - 1)
        scale = fringe_ref[x]
        for c in range(components):
            center = a_ref[c, x]
            west = jnp.where(x == 0, w_ref[c, 0], a_ref[c, west_index])
            east = jnp.where(x == width_x - 1, e_ref[c, 0], a_ref[c, east_index])
            north = jnp.where(row == width_y - 1, jnp.broadcast_to(n_ref[c, x], (width_y, height)), pltpu.roll(center, width_y - 1, 0))
            south = jnp.where(row == 0, jnp.broadcast_to(s_ref[c, x], (width_y, height)), pltpu.roll(center, 1, 0))
            upper = jnp.where(lane == height - 1, 0.0, pltpu.roll(center, height - 1, 1))
            lower = jnp.where(lane == 0, 0.0, pltpu.roll(center, 1, 1))
            laplace = east + west + north + south + upper + lower - 6.0 * center
            advect = 0.5 * (u0 * (east - west) + u1 * (north - south) + u2 * (upper - lower))
            product = jnp.concatenate(
                [prod[2 * x + zb, c * width_y : (c + 1) * width_y, :] for zb in range(NZB)], axis=1
            )
            update = center + TIME_STEP * (advect + BASE_VISC * laplace + viscous * product)
            if c == 0:
                update = update - TIME_STEP * drag_ref[x] * u0 * center
            out_ref[c, x] = update * scale
        return carry

    lax.fori_loop(0, width_x, plane, 0)


def advance(adjoint, west, east, south, north, forward, columns, eddy_blocks, drag_field, fringe_scale):
    components, width_x, width_y, height = adjoint.shape
    vmem = pl.BlockSpec(memory_space=pltpu.VMEM)
    smem = pl.BlockSpec(memory_space=pltpu.SMEM)
    return pl.pallas_call(
        advance_kernel,
        out_shape=jax.ShapeDtypeStruct(adjoint.shape, jnp.float32),
        in_specs=[smem, smem] + [vmem] * 8,
        out_specs=vmem,
        scratch_shapes=[
            pltpu.VMEM(((width_x + 2) * NZB, components * width_y, height // NZB), jnp.bfloat16),
            pltpu.VMEM((width_x * NZB, components * width_y, height // NZB), jnp.float32),
        ],
        compiler_params=pltpu.CompilerParams(vmem_limit_bytes=48 * 1024 * 1024),
    )(columns, fringe_scale, adjoint, west, east, south, north, forward, drag_field, eddy_blocks)


def halo(block, axis, dim):
    count = lax.axis_size(axis)
    forward = [(i, (i + 1) % count) for i in range(count)]
    backward = [(target, source) for source, target in forward]
    low = lax.ppermute(lax.slice_in_dim(block, block.shape[dim] - 1, None, axis=dim), axis, forward)
    high = lax.ppermute(lax.slice_in_dim(block, 0, 1, axis=dim), axis, backward)
    return low, high


def gradient_terms(adjoint, forward, owned_mask, plan_kernel, along_z):
    components, width_x, width_y, height = adjoint.shape
    velocity = forward[0].astype(jnp.float32)
    density = (velocity * velocity * adjoint[0]).reshape(width_x * width_y, height)
    projected = jnp.dot(density, along_z.T, precision=lax.Precision.HIGHEST)
    return owned_mask * jnp.sum(plan_kernel.T * projected, axis=0)


def shards(
    adjoint_in,
    checkpoints,
    send_owner,
    receive_rows,
    block_columns,
    eddy_blocks,
    thrust,
    yaw_angle,
    turbine_place,
    turbine_tile,
    fringe_rows,
):
    count_x = lax.axis_size("gx")
    count_y = lax.axis_size("gy")
    tile_count = count_x * count_y
    tile_index = lax.axis_index("gx") * count_y + lax.axis_index("gy")
    components, width_x, width_y, height = adjoint_in.shape
    steps_total = checkpoints.shape[0]
    block_shape = checkpoints.shape[2:]
    owner_ids = jnp.arange(tile_count, dtype=jnp.int32)
    onehot = (send_owner[:, None] == owner_ids[None, :]).astype(jnp.int32)
    slot_rank = jnp.sum(jnp.cumsum(onehot, axis=0) * onehot, axis=1) - 1
    position = send_owner * CAP + slot_rank
    slots = send_owner.shape[0]
    source_slot = jnp.zeros((tile_count * CAP,), jnp.int32).at[position].set(
        jnp.arange(slots, dtype=jnp.int32)
    )
    rows_x = lax.axis_index("gx") * width_x + jnp.arange(width_x, dtype=jnp.int32)
    fringe_hit = jnp.any(rows_x[:, None] == fringe_rows[None, :], axis=1)
    fringe_scale = jnp.where(fringe_hit, FRINGE_KEEP, 1.0).astype(jnp.float32)
    owned_mask, plan_kernel, along_z, drag_field = turbine_terms(
        tile_index, thrust, yaw_angle, turbine_place, turbine_tile, width_x, width_y, height
    )
    adjoint = adjoint_in
    gradient_sum = jnp.zeros((thrust.shape[0],), jnp.float32)
    for step_index in range(steps_total):
        stored = checkpoints[steps_total - 1 - step_index]
        packed = jnp.take(stored, source_slot, axis=0)
        arrived = lax.all_to_all(
            packed.reshape((tile_count, CAP) + block_shape),
            ("gx", "gy"),
            split_axis=0,
            concat_axis=0,
            tiled=True,
        )
        arrived = arrived.reshape((tile_count * CAP,) + block_shape)
        blocks = jnp.take(arrived, receive_rows, axis=0)
        rows_per_block = block_shape[1] // height
        forward = blocks.reshape(width_x, width_y // rows_per_block, components, rows_per_block, height)
        forward = forward.transpose(2, 0, 1, 3, 4).reshape(components, width_x, width_y, height)
        west, east = halo(adjoint, "gx", 1)
        south, north = halo(adjoint, "gy", 2)
        gradient_sum = gradient_sum + gradient_terms(adjoint, forward, owned_mask, plan_kernel, along_z)
        adjoint = advance(
            adjoint, west, east, south, north, forward, block_columns, eddy_blocks, drag_field, fringe_scale
        )
    gradient_sum = gather_sum(gradient_sum)
    cosine = jnp.cos(yaw_angle)
    sine = jnp.sin(yaw_angle)
    control_gradient = jnp.stack(
        [
            -0.5 * TIME_STEP * cosine * cosine * gradient_sum,
            TIME_STEP * thrust * sine * cosine * gradient_sum,
        ]
    )
    return (adjoint, control_gradient)


def solution(mesh):
    return jax.shard_map(
        shards,
        mesh=mesh,
        in_specs=(
            P(None, "gx", "gy", None),
            P(None, ("gx", "gy"), None, None),
            P(("gx", "gy")),
            P(("gx", "gy")),
            P(("gx", "gy"), None),
            P(),
            P(),
            P(),
            P(),
            P(),
            P(),
        ),
        out_specs=(P(None, "gx", "gy", None), P()),
        check_vma=False,
    )
```

```python
import functools

import jax
import jax.numpy as jnp
from jax import lax
from jax.experimental import pallas as pl
from jax.experimental.pallas import tpu as pltpu
from jax.sharding import PartitionSpec as P

MESH = pl.DeviceIdType.MESH

PB = 128
KB = 8
CAP = 2
NZB = 2


TIME_STEP = 0.25
BASE_VISC = 0.1
EDDY_COEF = 0.5
KERNEL_WIDTH = 1.5
FRINGE_KEEP = 0.5


def gather_sum_kernel(count_y, total, part_ref, out_ref, rows, send_sem, recv_sem):
    me = lax.axis_index("gx") * count_y + lax.axis_index("gy")

    def device(i):
        other = lax.rem(me + i, total)
        return (other // count_y, other % count_y)

    barrier = pltpu.get_barrier_semaphore()

    def greet(i, carry):
        pl.semaphore_signal(barrier, inc=1, device_id=device(i), device_id_type=MESH)
        return carry

    lax.fori_loop(1, total, greet, 0)
    pl.semaphore_wait(barrier, total - 1)
    rows[me] = part_ref[...]

    def send(i, carry):
        pltpu.make_async_remote_copy(
            src_ref=part_ref,
            dst_ref=rows.at[me],
            send_sem=send_sem,
            recv_sem=recv_sem,
            device_id=device(i),
            device_id_type=MESH,
        ).start()
        return carry

    lax.fori_loop(1, total, send, 0)
    everything = pltpu.make_async_remote_copy(
        src_ref=rows.at[pl.ds(0, total - 1)],
        dst_ref=rows.at[pl.ds(0, total - 1)],
        send_sem=send_sem,
        recv_sem=recv_sem,
        device_id=device(1),
        device_id_type=MESH,
    )
    everything.wait_send()
    everything.wait_recv()
    out_ref[...] = jnp.sum(rows[...], axis=0)


def gather_sum(part):
    count_y = lax.axis_size("gy")
    total = lax.axis_size("gx") * count_y
    width = part.shape[0]
    block = jnp.zeros((8, 128), jnp.float32).at[0, :width].set(part)
    summed = pl.pallas_call(
        functools.partial(gather_sum_kernel, count_y, total),
        out_shape=jax.ShapeDtypeStruct((8, 128), jnp.float32),
        in_specs=[pl.BlockSpec(memory_space=pltpu.VMEM)],
        out_specs=pl.BlockSpec(memory_space=pltpu.VMEM),
        scratch_shapes=[
            pltpu.VMEM((total, 8, 128), jnp.float32),
            pltpu.SemaphoreType.DMA(()),
            pltpu.SemaphoreType.DMA(()),
        ],
        compiler_params=pltpu.CompilerParams(collective_id=0, has_side_effects=True),
    )(block)
    return summed[0, :width]


def turbine_terms(
    tile_index, thrust, yaw_angle, turbine_place, turbine_tile, width_x, width_y, height
):
    owned_mask = (turbine_tile == tile_index).astype(jnp.float32)
    spread = 2.0 * KERNEL_WIDTH * KERNEL_WIDTH
    along_x = jnp.exp(
        -(
            (jnp.arange(width_x, dtype=jnp.float32)[None, :] - turbine_place[0][:, None] * width_x)
            ** 2
        )
        / spread
    )
    along_y = jnp.exp(
        -(
            (jnp.arange(width_y, dtype=jnp.float32)[None, :] - turbine_place[1][:, None] * width_y)
            ** 2
        )
        / spread
    )
    along_z = jnp.exp(
        -(
            (
                jnp.arange(height, dtype=jnp.float32)[None, :]
                - turbine_place[2][:, None] * (0.5 * height)
            )
            ** 2
        )
        / spread
    )
    plan_kernel = (along_x[:, :, None] * along_y[:, None, :]).reshape(
        along_x.shape[0], width_x * width_y
    )
    cosine = jnp.cos(yaw_angle)
    loading = owned_mask * thrust * cosine * cosine
    drag_field = jnp.dot(
        (plan_kernel * loading[:, None]).T, along_z, precision=lax.Precision.HIGHEST
    )
    return (owned_mask, plan_kernel, along_z, drag_field.reshape(width_x, width_y, height))


def advance_kernel(
    cols_ref, fringe_ref, a_ref, w_ref, e_ref, s_ref, n_ref, u_ref, drag_ref, eddy_ref,
    out_ref, xq, prod,
):
    components, width_x, width_y, height = a_ref.shape
    half = height // NZB
    def fill(px, src):
        for zb in range(NZB):
            for c in range(components):
                xq[2 * px + zb, c * width_y : (c + 1) * width_y, :] = src[c, :, zb * half : (zb + 1) * half].astype(jnp.bfloat16)

    def fill_plane(x, carry):
        for zb in range(NZB):
            for c in range(components):
                xq[2 * (x + 1) + zb, c * width_y : (c + 1) * width_y, :] = a_ref[c, x, :, zb * half : (zb + 1) * half].astype(jnp.bfloat16)
        return carry

    for zb in range(NZB):
        for c in range(components):
            xq[zb, c * width_y : (c + 1) * width_y, :] = w_ref[c, 0, :, zb * half : (zb + 1) * half].astype(jnp.bfloat16)
            xq[2 * (width_x + 1) + zb, c * width_y : (c + 1) * width_y, :] = e_ref[c, 0, :, zb * half : (zb + 1) * half].astype(jnp.bfloat16)
    lax.fori_loop(0, width_x, fill_plane, 0)

    def eddy_block(p, carry):
        acc = jnp.zeros((components * width_y, half), jnp.float32)
        for k in range(KB):
            acc = acc + jnp.dot(xq[cols_ref[p, k]], eddy_ref[k], preferred_element_type=jnp.float32)
        prod[p] = acc
        return carry

    lax.fori_loop(0, width_x * NZB, eddy_block, 0)

    row = lax.broadcasted_iota(jnp.int32, (width_y, height), 0)
    lane = lax.broadcasted_iota(jnp.int32, (width_y, height), 1)

    def plane(x, carry):
        u0 = u_ref[0, x].astype(jnp.float32)
        u1 = u_ref[1, x].astype(jnp.float32)
        u2 = u_ref[2, x].astype(jnp.float32)
        viscous = EDDY_COEF * jnp.sqrt(1.0 + (u0 * u0 + u1 * u1 + u2 * u2))
        west_index = jnp.maximum(x - 1, 0)
        east_index = jnp.minimum(x + 1, width_x - 1)
        scale = fringe_ref[x]
        for c in range(components):
            center = a_ref[c, x]
            west = jnp.where(x == 0, w_ref[c, 0], a_ref[c, west_index])
            east = jnp.where(x == width_x - 1, e_ref[c, 0], a_ref[c, east_index])
            north = jnp.where(row == width_y - 1, jnp.broadcast_to(n_ref[c, x], (width_y, height)), pltpu.roll(center, width_y - 1, 0))
            south = jnp.where(row == 0, jnp.broadcast_to(s_ref[c, x], (width_y, height)), pltpu.roll(center, 1, 0))
            upper = jnp.where(lane == height - 1, 0.0, pltpu.roll(center, height - 1, 1))
            lower = jnp.where(lane == 0, 0.0, pltpu.roll(center, 1, 1))
            laplace = east + west + north + south + upper + lower - 6.0 * center
            advect = 0.5 * (u0 * (east - west) + u1 * (north - south) + u2 * (upper - lower))
            product = jnp.concatenate(
                [prod[2 * x + zb, c * width_y : (c + 1) * width_y, :] for zb in range(NZB)], axis=1
            )
            update = center + TIME_STEP * (advect + BASE_VISC * laplace + viscous * product)
            if c == 0:
                update = update - TIME_STEP * drag_ref[x] * u0 * center
            out_ref[c, x] = update * scale
        return carry

    lax.fori_loop(0, width_x, plane, 0)


def advance(adjoint, west, east, south, north, forward, columns, eddy_blocks, drag_field, fringe_scale):
    components, width_x, width_y, height = adjoint.shape
    vmem = pl.BlockSpec(memory_space=pltpu.VMEM)
    smem = pl.BlockSpec(memory_space=pltpu.SMEM)
    return pl.pallas_call(
        advance_kernel,
        out_shape=jax.ShapeDtypeStruct(adjoint.shape, jnp.float32),
        in_specs=[smem, smem] + [vmem] * 8,
        out_specs=vmem,
        scratch_shapes=[
            pltpu.VMEM(((width_x + 2) * NZB, components * width_y, height // NZB), jnp.bfloat16),
            pltpu.VMEM((width_x * NZB, components * width_y, height // NZB), jnp.float32),
        ],
        compiler_params=pltpu.CompilerParams(vmem_limit_bytes=48 * 1024 * 1024),
    )(columns, fringe_scale, adjoint, west, east, south, north, forward, drag_field, eddy_blocks)


def halo(block, axis, dim):
    count = lax.axis_size(axis)
    forward = [(i, (i + 1) % count) for i in range(count)]
    backward = [(target, source) for source, target in forward]
    low = lax.ppermute(lax.slice_in_dim(block, block.shape[dim] - 1, None, axis=dim), axis, forward)
    high = lax.ppermute(lax.slice_in_dim(block, 0, 1, axis=dim), axis, backward)
    return low, high


def gradient_terms(adjoint, forward, owned_mask, plan_kernel, along_z):
    components, width_x, width_y, height = adjoint.shape
    velocity = forward[0].astype(jnp.float32)
    density = (velocity * velocity * adjoint[0]).reshape(width_x * width_y, height)
    projected = jnp.dot(density, along_z.T, precision=lax.Precision.HIGHEST)
    return owned_mask * jnp.sum(plan_kernel.T * projected, axis=0)


def shards(
    adjoint_in,
    checkpoints,
    send_owner,
    receive_rows,
    block_columns,
    eddy_blocks,
    thrust,
    yaw_angle,
    turbine_place,
    turbine_tile,
    fringe_rows,
):
    count_x = lax.axis_size("gx")
    count_y = lax.axis_size("gy")
    tile_count = count_x * count_y
    tile_index = lax.axis_index("gx") * count_y + lax.axis_index("gy")
    components, width_x, width_y, height = adjoint_in.shape
    steps_total = checkpoints.shape[0]
    block_shape = checkpoints.shape[2:]
    owner_ids = jnp.arange(tile_count, dtype=jnp.int32)
    onehot = (send_owner[:, None] == owner_ids[None, :]).astype(jnp.int32)
    slot_rank = jnp.sum(jnp.cumsum(onehot, axis=0) * onehot, axis=1) - 1
    position = send_owner * CAP + slot_rank
    slots = send_owner.shape[0]
    row_ids = jnp.arange(tile_count * CAP, dtype=jnp.int32)
    pack_table = (row_ids[:, None] == position[None, :]).astype(jnp.bfloat16)
    pack_table = pack_table.reshape(tile_count, CAP, slots)
    pick_table = (receive_rows[:, None] == row_ids[None, :]).astype(jnp.bfloat16)
    pick_table = pick_table.reshape(receive_rows.shape[0], tile_count, CAP)
    rows_x = lax.axis_index("gx") * width_x + jnp.arange(width_x, dtype=jnp.int32)
    fringe_hit = jnp.any(rows_x[:, None] == fringe_rows[None, :], axis=1)
    fringe_scale = jnp.where(fringe_hit, FRINGE_KEEP, 1.0).astype(jnp.float32)
    owned_mask, plan_kernel, along_z, drag_field = turbine_terms(
        tile_index, thrust, yaw_angle, turbine_place, turbine_tile, width_x, width_y, height
    )
    adjoint = adjoint_in
    gradient_sum = jnp.zeros((thrust.shape[0],), jnp.float32)
    for step_index in range(steps_total):
        stored = checkpoints[steps_total - 1 - step_index]
        packed = jnp.einsum(
            "drs,scb->dcrb", pack_table, stored, preferred_element_type=jnp.float32
        ).astype(jnp.bfloat16)
        arrived = lax.all_to_all(packed, ("gx", "gy"), split_axis=0, concat_axis=0, tiled=True)
        forward = jnp.einsum(
            "jsr,scrb->cjb", pick_table, arrived, preferred_element_type=jnp.float32
        ).astype(jnp.bfloat16)
        forward = forward.reshape(components, width_x, width_y, height)
        west, east = halo(adjoint, "gx", 1)
        south, north = halo(adjoint, "gy", 2)
        gradient_sum = gradient_sum + gradient_terms(adjoint, forward, owned_mask, plan_kernel, along_z)
        adjoint = advance(
            adjoint, west, east, south, north, forward, block_columns, eddy_blocks, drag_field, fringe_scale
        )
    gradient_sum = gather_sum(gradient_sum)
    cosine = jnp.cos(yaw_angle)
    sine = jnp.sin(yaw_angle)
    control_gradient = jnp.stack(
        [
            -0.5 * TIME_STEP * cosine * cosine * gradient_sum,
            TIME_STEP * thrust * sine * cosine * gradient_sum,
        ]
    )
    return (adjoint, control_gradient)


def solution(mesh):
    return jax.shard_map(
        shards,
        mesh=mesh,
        in_specs=(
            P(None, "gx", "gy", None),
            P(None, ("gx", "gy"), None, None),
            P(("gx", "gy")),
            P(("gx", "gy")),
            P(("gx", "gy"), None),
            P(),
            P(),
            P(),
            P(),
            P(),
            P(),
        ),
        out_specs=(P(None, "gx", "gy", None), P()),
        check_vma=False,
    )
```

```python
import functools

import jax
import jax.numpy as jnp
from jax import lax
from jax.experimental import pallas as pl
from jax.experimental.pallas import tpu as pltpu
from jax.sharding import PartitionSpec as P

MESH = pl.DeviceIdType.MESH

PB = 128
KB = 8
CAP = 2
NZB = 2


TIME_STEP = 0.25
BASE_VISC = 0.1
EDDY_COEF = 0.5
KERNEL_WIDTH = 1.5
FRINGE_KEEP = 0.5


def gather_sum_kernel(count_y, group, part_ref, out_ref, near, far, sems):
    total = lax.axis_size("gx") * count_y
    groups = total // group
    me = lax.axis_index("gx") * count_y + lax.axis_index("gy")
    mine, base = me % group, me - me % group

    def near_device(i):
        other = base + lax.rem(mine + i, group)
        return (other // count_y, other % count_y)

    def far_device(i):
        other = lax.rem(me + i * group, total)
        return (other // count_y, other % count_y)

    barrier = pltpu.get_barrier_semaphore()

    def greet_near(i, carry):
        pl.semaphore_signal(barrier, inc=1, device_id=near_device(i), device_id_type=MESH)
        return carry

    def greet_far(i, carry):
        pl.semaphore_signal(barrier, inc=1, device_id=far_device(i), device_id_type=MESH)
        return carry

    lax.fori_loop(1, group, greet_near, 0)
    lax.fori_loop(1, groups, greet_far, 0)
    pl.semaphore_wait(barrier, group + groups - 2)

    near[mine] = part_ref[...]

    def send_near(i, carry):
        pltpu.make_async_remote_copy(
            src_ref=part_ref, dst_ref=near.at[mine], send_sem=sems.at[0], recv_sem=sems.at[1],
            device_id=near_device(i), device_id_type=MESH,
        ).start()
        return carry

    lax.fori_loop(1, group, send_near, 0)
    first = pltpu.make_async_remote_copy(
        src_ref=near.at[pl.ds(0, group - 1)], dst_ref=near.at[pl.ds(0, group - 1)],
        send_sem=sems.at[0], recv_sem=sems.at[1], device_id=near_device(1), device_id_type=MESH,
    )
    first.wait_send()
    first.wait_recv()
    far[me // group] = jnp.sum(near[...], axis=0)

    def send_far(i, carry):
        pltpu.make_async_remote_copy(
            src_ref=far.at[me // group], dst_ref=far.at[me // group], send_sem=sems.at[2], recv_sem=sems.at[3],
            device_id=far_device(i), device_id_type=MESH,
        ).start()
        return carry

    lax.fori_loop(1, groups, send_far, 0)
    second = pltpu.make_async_remote_copy(
        src_ref=far.at[pl.ds(0, groups - 1)], dst_ref=far.at[pl.ds(0, groups - 1)],
        send_sem=sems.at[2], recv_sem=sems.at[3], device_id=far_device(1), device_id_type=MESH,
    )
    second.wait_send()
    second.wait_recv()
    out_ref[...] = jnp.sum(far[...], axis=0)


def gather_sum(part):
    count_y = lax.axis_size("gy")
    total = lax.axis_size("gx") * count_y
    group = 8 if total % 8 == 0 and total > 8 else total // 2
    width = part.shape[0]
    block = jnp.zeros((8, 128), jnp.float32).at[0, :width].set(part)
    summed = pl.pallas_call(
        functools.partial(gather_sum_kernel, count_y, group),
        out_shape=jax.ShapeDtypeStruct((8, 128), jnp.float32),
        in_specs=[pl.BlockSpec(memory_space=pltpu.VMEM)],
        out_specs=pl.BlockSpec(memory_space=pltpu.VMEM),
        scratch_shapes=[
            pltpu.VMEM((group, 8, 128), jnp.float32),
            pltpu.VMEM((total // group, 8, 128), jnp.float32),
            pltpu.SemaphoreType.DMA((4,)),
        ],
        compiler_params=pltpu.CompilerParams(collective_id=0, has_side_effects=True),
    )(block)
    return summed[0, :width]


def turbine_terms(
    tile_index, thrust, yaw_angle, turbine_place, turbine_tile, width_x, width_y, height
):
    owned_mask = (turbine_tile == tile_index).astype(jnp.float32)
    spread = 2.0 * KERNEL_WIDTH * KERNEL_WIDTH
    along_x = jnp.exp(
        -(
            (jnp.arange(width_x, dtype=jnp.float32)[None, :] - turbine_place[0][:, None] * width_x)
            ** 2
        )
        / spread
    )
    along_y = jnp.exp(
        -(
            (jnp.arange(width_y, dtype=jnp.float32)[None, :] - turbine_place[1][:, None] * width_y)
            ** 2
        )
        / spread
    )
    along_z = jnp.exp(
        -(
            (
                jnp.arange(height, dtype=jnp.float32)[None, :]
                - turbine_place[2][:, None] * (0.5 * height)
            )
            ** 2
        )
        / spread
    )
    plan_kernel = (along_x[:, :, None] * along_y[:, None, :]).reshape(
        along_x.shape[0], width_x * width_y
    )
    cosine = jnp.cos(yaw_angle)
    loading = owned_mask * thrust * cosine * cosine
    drag_field = jnp.dot(
        (plan_kernel * loading[:, None]).T, along_z, precision=lax.Precision.HIGHEST
    )
    return (owned_mask, plan_kernel, along_z, drag_field.reshape(width_x, width_y, height))


def advance_kernel(
    cols_ref, fringe_ref, a_ref, w_ref, e_ref, s_ref, n_ref, u_ref, drag_ref, eddy_ref,
    out_ref, xq, prod,
):
    components, width_x, width_y, height = a_ref.shape
    half = height // NZB
    def fill(px, src):
        for zb in range(NZB):
            for c in range(components):
                xq[2 * px + zb, c * width_y : (c + 1) * width_y, :] = src[c, :, zb * half : (zb + 1) * half].astype(jnp.bfloat16)

    def fill_plane(x, carry):
        for zb in range(NZB):
            for c in range(components):
                xq[2 * (x + 1) + zb, c * width_y : (c + 1) * width_y, :] = a_ref[c, x, :, zb * half : (zb + 1) * half].astype(jnp.bfloat16)
        return carry

    for zb in range(NZB):
        for c in range(components):
            xq[zb, c * width_y : (c + 1) * width_y, :] = w_ref[c, 0, :, zb * half : (zb + 1) * half].astype(jnp.bfloat16)
            xq[2 * (width_x + 1) + zb, c * width_y : (c + 1) * width_y, :] = e_ref[c, 0, :, zb * half : (zb + 1) * half].astype(jnp.bfloat16)
    lax.fori_loop(0, width_x, fill_plane, 0)

    def eddy_block(p, carry):
        acc = jnp.zeros((components * width_y, half), jnp.float32)
        for k in range(KB):
            acc = acc + jnp.dot(xq[cols_ref[p, k]], eddy_ref[k], preferred_element_type=jnp.float32)
        prod[p] = acc
        return carry

    lax.fori_loop(0, width_x * NZB, eddy_block, 0)

    row = lax.broadcasted_iota(jnp.int32, (width_y, height), 0)
    lane = lax.broadcasted_iota(jnp.int32, (width_y, height), 1)

    def plane(x, carry):
        u0 = u_ref[0, x].astype(jnp.float32)
        u1 = u_ref[1, x].astype(jnp.float32)
        u2 = u_ref[2, x].astype(jnp.float32)
        viscous = EDDY_COEF * jnp.sqrt(1.0 + (u0 * u0 + u1 * u1 + u2 * u2))
        west_index = jnp.maximum(x - 1, 0)
        east_index = jnp.minimum(x + 1, width_x - 1)
        scale = fringe_ref[x]
        for c in range(components):
            center = a_ref[c, x]
            west = jnp.where(x == 0, w_ref[c, 0], a_ref[c, west_index])
            east = jnp.where(x == width_x - 1, e_ref[c, 0], a_ref[c, east_index])
            north = jnp.where(row == width_y - 1, jnp.broadcast_to(n_ref[c, x], (width_y, height)), pltpu.roll(center, width_y - 1, 0))
            south = jnp.where(row == 0, jnp.broadcast_to(s_ref[c, x], (width_y, height)), pltpu.roll(center, 1, 0))
            upper = jnp.where(lane == height - 1, 0.0, pltpu.roll(center, height - 1, 1))
            lower = jnp.where(lane == 0, 0.0, pltpu.roll(center, 1, 1))
            laplace = east + west + north + south + upper + lower - 6.0 * center
            advect = 0.5 * (u0 * (east - west) + u1 * (north - south) + u2 * (upper - lower))
            product = jnp.concatenate(
                [prod[2 * x + zb, c * width_y : (c + 1) * width_y, :] for zb in range(NZB)], axis=1
            )
            update = center + TIME_STEP * (advect + BASE_VISC * laplace + viscous * product)
            if c == 0:
                update = update - TIME_STEP * drag_ref[x] * u0 * center
            out_ref[c, x] = update * scale
        return carry

    lax.fori_loop(0, width_x, plane, 0)


def advance(adjoint, west, east, south, north, forward, columns, eddy_blocks, drag_field, fringe_scale):
    components, width_x, width_y, height = adjoint.shape
    vmem = pl.BlockSpec(memory_space=pltpu.VMEM)
    smem = pl.BlockSpec(memory_space=pltpu.SMEM)
    return pl.pallas_call(
        advance_kernel,
        out_shape=jax.ShapeDtypeStruct(adjoint.shape, jnp.float32),
        in_specs=[smem, smem] + [vmem] * 8,
        out_specs=vmem,
        scratch_shapes=[
            pltpu.VMEM(((width_x + 2) * NZB, components * width_y, height // NZB), jnp.bfloat16),
            pltpu.VMEM((width_x * NZB, components * width_y, height // NZB), jnp.float32),
        ],
        compiler_params=pltpu.CompilerParams(vmem_limit_bytes=48 * 1024 * 1024),
    )(columns, fringe_scale, adjoint, west, east, south, north, forward, drag_field, eddy_blocks)


def halo(block, axis, dim):
    count = lax.axis_size(axis)
    forward = [(i, (i + 1) % count) for i in range(count)]
    backward = [(target, source) for source, target in forward]
    low = lax.ppermute(lax.slice_in_dim(block, block.shape[dim] - 1, None, axis=dim), axis, forward)
    high = lax.ppermute(lax.slice_in_dim(block, 0, 1, axis=dim), axis, backward)
    return low, high


def gradient_terms(adjoint, forward, owned_mask, plan_kernel, along_z):
    components, width_x, width_y, height = adjoint.shape
    velocity = forward[0].astype(jnp.float32)
    density = (velocity * velocity * adjoint[0]).reshape(width_x * width_y, height)
    projected = jnp.dot(density, along_z.T, precision=lax.Precision.HIGHEST)
    return owned_mask * jnp.sum(plan_kernel.T * projected, axis=0)


def shards(
    adjoint_in,
    checkpoints,
    send_owner,
    receive_rows,
    block_columns,
    eddy_blocks,
    thrust,
    yaw_angle,
    turbine_place,
    turbine_tile,
    fringe_rows,
):
    count_x = lax.axis_size("gx")
    count_y = lax.axis_size("gy")
    tile_count = count_x * count_y
    tile_index = lax.axis_index("gx") * count_y + lax.axis_index("gy")
    components, width_x, width_y, height = adjoint_in.shape
    steps_total = checkpoints.shape[0]
    block_shape = checkpoints.shape[2:]
    owner_ids = jnp.arange(tile_count, dtype=jnp.int32)
    onehot = (send_owner[:, None] == owner_ids[None, :]).astype(jnp.int32)
    slot_rank = jnp.sum(jnp.cumsum(onehot, axis=0) * onehot, axis=1) - 1
    position = send_owner * CAP + slot_rank
    slots = send_owner.shape[0]
    row_ids = jnp.arange(tile_count * CAP, dtype=jnp.int32)
    pack_table = (row_ids[:, None] == position[None, :]).astype(jnp.bfloat16)
    pack_table = pack_table.reshape(tile_count, CAP, slots)
    pick_table = (receive_rows[:, None] == row_ids[None, :]).astype(jnp.bfloat16)
    pick_table = pick_table.reshape(receive_rows.shape[0], tile_count, CAP)
    rows_x = lax.axis_index("gx") * width_x + jnp.arange(width_x, dtype=jnp.int32)
    fringe_hit = jnp.any(rows_x[:, None] == fringe_rows[None, :], axis=1)
    fringe_scale = jnp.where(fringe_hit, FRINGE_KEEP, 1.0).astype(jnp.float32)
    owned_mask, plan_kernel, along_z, drag_field = turbine_terms(
        tile_index, thrust, yaw_angle, turbine_place, turbine_tile, width_x, width_y, height
    )
    adjoint = adjoint_in
    gradient_sum = jnp.zeros((thrust.shape[0],), jnp.float32)
    for step_index in range(steps_total):
        stored = checkpoints[steps_total - 1 - step_index]
        packed = jnp.einsum(
            "drs,scb->dcrb", pack_table, stored, preferred_element_type=jnp.float32
        ).astype(jnp.bfloat16)
        arrived = lax.all_to_all(packed, ("gx", "gy"), split_axis=0, concat_axis=0, tiled=True)
        forward = jnp.einsum(
            "jsr,scrb->cjb", pick_table, arrived, preferred_element_type=jnp.float32
        ).astype(jnp.bfloat16)
        forward = forward.reshape(components, width_x, width_y, height)
        west, east = halo(adjoint, "gx", 1)
        south, north = halo(adjoint, "gy", 2)
        gradient_sum = gradient_sum + gradient_terms(adjoint, forward, owned_mask, plan_kernel, along_z)
        adjoint = advance(
            adjoint, west, east, south, north, forward, block_columns, eddy_blocks, drag_field, fringe_scale
        )
    gradient_sum = gather_sum(gradient_sum)
    cosine = jnp.cos(yaw_angle)
    sine = jnp.sin(yaw_angle)
    control_gradient = jnp.stack(
        [
            -0.5 * TIME_STEP * cosine * cosine * gradient_sum,
            TIME_STEP * thrust * sine * cosine * gradient_sum,
        ]
    )
    return (adjoint, control_gradient)


def solution(mesh):
    return jax.shard_map(
        shards,
        mesh=mesh,
        in_specs=(
            P(None, "gx", "gy", None),
            P(None, ("gx", "gy"), None, None),
            P(("gx", "gy")),
            P(("gx", "gy")),
            P(("gx", "gy"), None),
            P(),
            P(),
            P(),
            P(),
            P(),
            P(),
        ),
        out_specs=(P(None, "gx", "gy", None), P()),
        check_vma=False,
    )
```

```python
import functools

import jax
import jax.numpy as jnp
from jax import lax
from jax.experimental import pallas as pl
from jax.experimental.pallas import tpu as pltpu
from jax.sharding import PartitionSpec as P

MESH = pl.DeviceIdType.MESH

PB = 128
KB = 8
CAP = 2
NZB = 2


TIME_STEP = 0.25
BASE_VISC = 0.1
EDDY_COEF = 0.5
KERNEL_WIDTH = 1.5
FRINGE_KEEP = 0.5


def turbine_terms(
    tile_index, thrust, yaw_angle, turbine_place, turbine_tile, width_x, width_y, height
):
    owned_mask = (turbine_tile == tile_index).astype(jnp.float32)
    spread = 2.0 * KERNEL_WIDTH * KERNEL_WIDTH
    along_x = jnp.exp(
        -(
            (jnp.arange(width_x, dtype=jnp.float32)[None, :] - turbine_place[0][:, None] * width_x)
            ** 2
        )
        / spread
    )
    along_y = jnp.exp(
        -(
            (jnp.arange(width_y, dtype=jnp.float32)[None, :] - turbine_place[1][:, None] * width_y)
            ** 2
        )
        / spread
    )
    along_z = jnp.exp(
        -(
            (
                jnp.arange(height, dtype=jnp.float32)[None, :]
                - turbine_place[2][:, None] * (0.5 * height)
            )
            ** 2
        )
        / spread
    )
    plan_kernel = (along_x[:, :, None] * along_y[:, None, :]).reshape(
        along_x.shape[0], width_x * width_y
    )
    cosine = jnp.cos(yaw_angle)
    loading = owned_mask * thrust * cosine * cosine
    drag_field = jnp.dot(
        (plan_kernel * loading[:, None]).T, along_z, precision=lax.Precision.HIGHEST
    )
    return (owned_mask, plan_kernel, along_z, drag_field.reshape(width_x, width_y, height))


def advance_kernel(count_y, group, exchange, *refs):
    if exchange:
        (cols_ref, fringe_ref, a_ref, w_ref, e_ref, s_ref, n_ref, u_ref, drag_ref, eddy_ref, part_ref,
         out_ref, sum_ref, xq, prod, near, far, sems) = refs
    else:
        (cols_ref, fringe_ref, a_ref, w_ref, e_ref, s_ref, n_ref, u_ref, drag_ref, eddy_ref,
         out_ref, xq, prod) = refs
    components, width_x, width_y, height = a_ref.shape
    if exchange:
        total = lax.axis_size("gx") * count_y
        groups = total // group
        me = lax.axis_index("gx") * count_y + lax.axis_index("gy")
        mine, base = me % group, me - me % group

        def near_device(i):
            other = base + lax.rem(mine + i, group)
            return (other // count_y, other % count_y)

        def far_device(i):
            other = lax.rem(me + i * group, total)
            return (other // count_y, other % count_y)

        barrier = pltpu.get_barrier_semaphore()

        def greet_near(i, carry):
            pl.semaphore_signal(barrier, inc=1, device_id=near_device(i), device_id_type=MESH)
            return carry

        def greet_far(i, carry):
            pl.semaphore_signal(barrier, inc=1, device_id=far_device(i), device_id_type=MESH)
            return carry

        lax.fori_loop(1, group, greet_near, 0)
        lax.fori_loop(1, groups, greet_far, 0)
        pl.semaphore_wait(barrier, group + groups - 2)
        near[mine] = part_ref[...]

        def send_near(i, carry):
            pltpu.make_async_remote_copy(
                src_ref=part_ref, dst_ref=near.at[mine], send_sem=sems.at[0], recv_sem=sems.at[1],
                device_id=near_device(i), device_id_type=MESH,
            ).start()
            return carry

        lax.fori_loop(1, group, send_near, 0)
    half = height // NZB
    def fill(px, src):
        for zb in range(NZB):
            for c in range(components):
                xq[2 * px + zb, c * width_y : (c + 1) * width_y, :] = src[c, :, zb * half : (zb + 1) * half].astype(jnp.bfloat16)

    def fill_plane(x, carry):
        for zb in range(NZB):
            for c in range(components):
                xq[2 * (x + 1) + zb, c * width_y : (c + 1) * width_y, :] = a_ref[c, x, :, zb * half : (zb + 1) * half].astype(jnp.bfloat16)
        return carry

    for zb in range(NZB):
        for c in range(components):
            xq[zb, c * width_y : (c + 1) * width_y, :] = w_ref[c, 0, :, zb * half : (zb + 1) * half].astype(jnp.bfloat16)
            xq[2 * (width_x + 1) + zb, c * width_y : (c + 1) * width_y, :] = e_ref[c, 0, :, zb * half : (zb + 1) * half].astype(jnp.bfloat16)
    lax.fori_loop(0, width_x, fill_plane, 0)

    def eddy_block(p, carry):
        acc = jnp.zeros((components * width_y, half), jnp.float32)
        for k in range(KB):
            acc = acc + jnp.dot(xq[cols_ref[p, k]], eddy_ref[k], preferred_element_type=jnp.float32)
        prod[p] = acc
        return carry

    lax.fori_loop(0, width_x * NZB, eddy_block, 0)
    if exchange:
        first = pltpu.make_async_remote_copy(
            src_ref=near.at[pl.ds(0, group - 1)], dst_ref=near.at[pl.ds(0, group - 1)],
            send_sem=sems.at[0], recv_sem=sems.at[1], device_id=near_device(1), device_id_type=MESH,
        )
        first.wait_send()
        first.wait_recv()
        far[me // group] = jnp.sum(near[...], axis=0)

        def send_far(i, carry):
            pltpu.make_async_remote_copy(
                src_ref=far.at[me // group], dst_ref=far.at[me // group], send_sem=sems.at[2],
                recv_sem=sems.at[3], device_id=far_device(i), device_id_type=MESH,
            ).start()
            return carry

        lax.fori_loop(1, groups, send_far, 0)

    row = lax.broadcasted_iota(jnp.int32, (width_y, height), 0)
    lane = lax.broadcasted_iota(jnp.int32, (width_y, height), 1)

    def plane(x, carry):
        u0 = u_ref[0, x].astype(jnp.float32)
        u1 = u_ref[1, x].astype(jnp.float32)
        u2 = u_ref[2, x].astype(jnp.float32)
        viscous = EDDY_COEF * jnp.sqrt(1.0 + (u0 * u0 + u1 * u1 + u2 * u2))
        west_index = jnp.maximum(x - 1, 0)
        east_index = jnp.minimum(x + 1, width_x - 1)
        scale = fringe_ref[x]
        for c in range(components):
            center = a_ref[c, x]
            west = jnp.where(x == 0, w_ref[c, 0], a_ref[c, west_index])
            east = jnp.where(x == width_x - 1, e_ref[c, 0], a_ref[c, east_index])
            north = jnp.where(row == width_y - 1, jnp.broadcast_to(n_ref[c, x], (width_y, height)), pltpu.roll(center, width_y - 1, 0))
            south = jnp.where(row == 0, jnp.broadcast_to(s_ref[c, x], (width_y, height)), pltpu.roll(center, 1, 0))
            upper = jnp.where(lane == height - 1, 0.0, pltpu.roll(center, height - 1, 1))
            lower = jnp.where(lane == 0, 0.0, pltpu.roll(center, 1, 1))
            laplace = east + west + north + south + upper + lower - 6.0 * center
            advect = 0.5 * (u0 * (east - west) + u1 * (north - south) + u2 * (upper - lower))
            product = jnp.concatenate(
                [prod[2 * x + zb, c * width_y : (c + 1) * width_y, :] for zb in range(NZB)], axis=1
            )
            update = center + TIME_STEP * (advect + BASE_VISC * laplace + viscous * product)
            if c == 0:
                update = update - TIME_STEP * drag_ref[x] * u0 * center
            out_ref[c, x] = update * scale
        return carry

    lax.fori_loop(0, width_x, plane, 0)
    if exchange:
        second = pltpu.make_async_remote_copy(
            src_ref=far.at[pl.ds(0, groups - 1)], dst_ref=far.at[pl.ds(0, groups - 1)],
            send_sem=sems.at[2], recv_sem=sems.at[3], device_id=far_device(1), device_id_type=MESH,
        )
        second.wait_send()
        second.wait_recv()
        sum_ref[...] = jnp.sum(far[...], axis=0)


def advance(adjoint, west, east, south, north, forward, columns, eddy_blocks, drag_field, fringe_scale, part=None):
    components, width_x, width_y, height = adjoint.shape
    vmem = pl.BlockSpec(memory_space=pltpu.VMEM)
    smem = pl.BlockSpec(memory_space=pltpu.SMEM)
    count_y = lax.axis_size("gy")
    total = lax.axis_size("gx") * count_y
    group = 8 if total % 8 == 0 and total > 8 else total // 2
    exchange = part is not None
    operands = [columns, fringe_scale, adjoint, west, east, south, north, forward, drag_field, eddy_blocks]
    out_shape = [jax.ShapeDtypeStruct(adjoint.shape, jnp.float32)]
    scratch = [
        pltpu.VMEM(((width_x + 2) * NZB, components * width_y, height // NZB), jnp.bfloat16),
        pltpu.VMEM((width_x * NZB, components * width_y, height // NZB), jnp.float32),
    ]
    params = dict(vmem_limit_bytes=48 * 1024 * 1024)
    if exchange:
        width = part.shape[0]
        operands.append(jnp.zeros((8, 128), jnp.float32).at[0, :width].set(part))
        out_shape.append(jax.ShapeDtypeStruct((8, 128), jnp.float32))
        scratch += [
            pltpu.VMEM((group, 8, 128), jnp.float32),
            pltpu.VMEM((total // group, 8, 128), jnp.float32),
            pltpu.SemaphoreType.DMA((4,)),
        ]
        params.update(collective_id=0, has_side_effects=True)
    results = pl.pallas_call(
        functools.partial(advance_kernel, count_y, group, exchange),
        out_shape=tuple(out_shape),
        in_specs=[smem, smem] + [vmem] * (len(operands) - 2),
        out_specs=tuple([vmem] * len(out_shape)),
        scratch_shapes=scratch,
        compiler_params=pltpu.CompilerParams(**params),
    )(*operands)
    if exchange:
        return results[0], results[1][0, :width]
    return results[0]


def halo(block, axis, dim):
    count = lax.axis_size(axis)
    forward = [(i, (i + 1) % count) for i in range(count)]
    backward = [(target, source) for source, target in forward]
    low = lax.ppermute(lax.slice_in_dim(block, block.shape[dim] - 1, None, axis=dim), axis, forward)
    high = lax.ppermute(lax.slice_in_dim(block, 0, 1, axis=dim), axis, backward)
    return low, high


def gradient_terms(adjoint, forward, owned_mask, plan_kernel, along_z):
    components, width_x, width_y, height = adjoint.shape
    velocity = forward[0].astype(jnp.float32)
    density = (velocity * velocity * adjoint[0]).reshape(width_x * width_y, height)
    projected = jnp.dot(density, along_z.T, precision=lax.Precision.HIGHEST)
    return owned_mask * jnp.sum(plan_kernel.T * projected, axis=0)


def shards(
    adjoint_in,
    checkpoints,
    send_owner,
    receive_rows,
    block_columns,
    eddy_blocks,
    thrust,
    yaw_angle,
    turbine_place,
    turbine_tile,
    fringe_rows,
):
    count_x = lax.axis_size("gx")
    count_y = lax.axis_size("gy")
    tile_count = count_x * count_y
    tile_index = lax.axis_index("gx") * count_y + lax.axis_index("gy")
    components, width_x, width_y, height = adjoint_in.shape
    steps_total = checkpoints.shape[0]
    block_shape = checkpoints.shape[2:]
    owner_ids = jnp.arange(tile_count, dtype=jnp.int32)
    onehot = (send_owner[:, None] == owner_ids[None, :]).astype(jnp.int32)
    slot_rank = jnp.sum(jnp.cumsum(onehot, axis=0) * onehot, axis=1) - 1
    position = send_owner * CAP + slot_rank
    slots = send_owner.shape[0]
    row_ids = jnp.arange(tile_count * CAP, dtype=jnp.int32)
    pack_table = (row_ids[:, None] == position[None, :]).astype(jnp.bfloat16)
    pack_table = pack_table.reshape(tile_count, CAP, slots)
    pick_table = (receive_rows[:, None] == row_ids[None, :]).astype(jnp.bfloat16)
    pick_table = pick_table.reshape(receive_rows.shape[0], tile_count, CAP)
    rows_x = lax.axis_index("gx") * width_x + jnp.arange(width_x, dtype=jnp.int32)
    fringe_hit = jnp.any(rows_x[:, None] == fringe_rows[None, :], axis=1)
    fringe_scale = jnp.where(fringe_hit, FRINGE_KEEP, 1.0).astype(jnp.float32)
    owned_mask, plan_kernel, along_z, drag_field = turbine_terms(
        tile_index, thrust, yaw_angle, turbine_place, turbine_tile, width_x, width_y, height
    )
    adjoint = adjoint_in
    gradient_sum = jnp.zeros((thrust.shape[0],), jnp.float32)
    for step_index in range(steps_total):
        stored = checkpoints[steps_total - 1 - step_index]
        packed = jnp.einsum(
            "drs,scb->dcrb", pack_table, stored, preferred_element_type=jnp.float32
        ).astype(jnp.bfloat16)
        arrived = lax.all_to_all(packed, ("gx", "gy"), split_axis=0, concat_axis=0, tiled=True)
        forward = jnp.einsum(
            "jsr,scrb->cjb", pick_table, arrived, preferred_element_type=jnp.float32
        ).astype(jnp.bfloat16)
        forward = forward.reshape(components, width_x, width_y, height)
        west, east = halo(adjoint, "gx", 1)
        south, north = halo(adjoint, "gy", 2)
        gradient_sum = gradient_sum + gradient_terms(adjoint, forward, owned_mask, plan_kernel, along_z)
        last = step_index == steps_total - 1
        stepped = advance(
            adjoint, west, east, south, north, forward, block_columns, eddy_blocks, drag_field, fringe_scale,
            gradient_sum if last else None,
        )
        if last:
            adjoint, gradient_sum = stepped
        else:
            adjoint = stepped
    cosine = jnp.cos(yaw_angle)
    sine = jnp.sin(yaw_angle)
    control_gradient = jnp.stack(
        [
            -0.5 * TIME_STEP * cosine * cosine * gradient_sum,
            TIME_STEP * thrust * sine * cosine * gradient_sum,
        ]
    )
    return (adjoint, control_gradient)


def solution(mesh):
    return jax.shard_map(
        shards,
        mesh=mesh,
        in_specs=(
            P(None, "gx", "gy", None),
            P(None, ("gx", "gy"), None, None),
            P(("gx", "gy")),
            P(("gx", "gy")),
            P(("gx", "gy"), None),
            P(),
            P(),
            P(),
            P(),
            P(),
            P(),
        ),
        out_specs=(P(None, "gx", "gy", None), P()),
        check_vma=False,
    )
```

```python
import functools

import jax
import jax.numpy as jnp
from jax import lax
from jax.experimental import pallas as pl
from jax.experimental.pallas import tpu as pltpu
from jax.sharding import PartitionSpec as P

MESH = pl.DeviceIdType.MESH

PB = 128
KB = 8
CAP = 2
NZB = 2


TIME_STEP = 0.25
BASE_VISC = 0.1
EDDY_COEF = 0.5
KERNEL_WIDTH = 1.5
FRINGE_KEEP = 0.5


def turbine_terms(
    tile_index, thrust, yaw_angle, turbine_place, turbine_tile, width_x, width_y, height
):
    owned_mask = (turbine_tile == tile_index).astype(jnp.float32)
    spread = 2.0 * KERNEL_WIDTH * KERNEL_WIDTH
    along_x = jnp.exp(
        -(
            (jnp.arange(width_x, dtype=jnp.float32)[None, :] - turbine_place[0][:, None] * width_x)
            ** 2
        )
        / spread
    )
    along_y = jnp.exp(
        -(
            (jnp.arange(width_y, dtype=jnp.float32)[None, :] - turbine_place[1][:, None] * width_y)
            ** 2
        )
        / spread
    )
    along_z = jnp.exp(
        -(
            (
                jnp.arange(height, dtype=jnp.float32)[None, :]
                - turbine_place[2][:, None] * (0.5 * height)
            )
            ** 2
        )
        / spread
    )
    plan_kernel = (along_x[:, :, None] * along_y[:, None, :]).reshape(
        along_x.shape[0], width_x * width_y
    )
    cosine = jnp.cos(yaw_angle)
    loading = owned_mask * thrust * cosine * cosine
    drag_field = jnp.dot(
        (plan_kernel * loading[:, None]).T, along_z, precision=lax.Precision.HIGHEST
    )
    return (owned_mask, plan_kernel, along_z, drag_field.reshape(width_x, width_y, height))


def advance_kernel(count_y, group, exchange, *refs):
    (cols_ref, fringe_ref, a_ref, w_ref, e_ref, s_ref, n_ref, u_ref, drag_ref, eddy_ref, pk_ref, azh_ref,
     prior_ref, out_ref, sum_ref, xq, prod) = refs[:17]
    components, width_x, width_y, height = a_ref.shape
    if exchange:
        near, far, sems = refs[17:]
        total = lax.axis_size("gx") * count_y
        groups = total // group
        me = lax.axis_index("gx") * count_y + lax.axis_index("gy")
        mine, base = me % group, me - me % group

        def near_device(i):
            other = base + lax.rem(mine + i, group)
            return (other // count_y, other % count_y)

        def far_device(i):
            other = lax.rem(me + i * group, total)
            return (other // count_y, other % count_y)

        barrier = pltpu.get_barrier_semaphore()

        def greet_near(i, carry):
            pl.semaphore_signal(barrier, inc=1, device_id=near_device(i), device_id_type=MESH)
            return carry

        def greet_far(i, carry):
            pl.semaphore_signal(barrier, inc=1, device_id=far_device(i), device_id_type=MESH)
            return carry

        lax.fori_loop(1, group, greet_near, 0)
        lax.fori_loop(1, groups, greet_far, 0)

    def turbine_plane(x, acc):
        velocity = u_ref[0, x].astype(jnp.float32)
        density = velocity * velocity * a_ref[0, x]
        projected = jnp.dot(
            density, azh_ref[...], precision=lax.Precision.HIGHEST, preferred_element_type=jnp.float32
        )
        return acc + pk_ref[x] * projected

    acc = lax.fori_loop(0, width_x, turbine_plane, jnp.zeros(pk_ref.shape[1:], jnp.float32))
    first_row = lax.broadcasted_iota(jnp.int32, prior_ref.shape, 0) == 0
    part = prior_ref[...] + jnp.where(first_row, jnp.sum(acc, axis=0, keepdims=True), 0.0)
    if exchange:
        pl.semaphore_wait(barrier, group + groups - 2)
        near[mine] = part

        def send_near(i, carry):
            pltpu.make_async_remote_copy(
                src_ref=near.at[mine], dst_ref=near.at[mine], send_sem=sems.at[0], recv_sem=sems.at[1],
                device_id=near_device(i), device_id_type=MESH,
            ).start()
            return carry

        lax.fori_loop(1, group, send_near, 0)
    else:
        sum_ref[...] = part

    half = height // NZB

    def fill_plane(x, carry):
        for zb in range(NZB):
            for c in range(components):
                xq[2 * (x + 1) + zb, c * width_y : (c + 1) * width_y, :] = a_ref[c, x, :, zb * half : (zb + 1) * half].astype(jnp.bfloat16)
        return carry

    for zb in range(NZB):
        for c in range(components):
            xq[zb, c * width_y : (c + 1) * width_y, :] = w_ref[c, 0, :, zb * half : (zb + 1) * half].astype(jnp.bfloat16)
            xq[2 * (width_x + 1) + zb, c * width_y : (c + 1) * width_y, :] = e_ref[c, 0, :, zb * half : (zb + 1) * half].astype(jnp.bfloat16)
    lax.fori_loop(0, width_x, fill_plane, 0)

    def eddy_block(p, carry):
        acc = jnp.zeros((components * width_y, half), jnp.float32)
        for k in range(KB):
            acc = acc + jnp.dot(xq[cols_ref[p, k]], eddy_ref[k], preferred_element_type=jnp.float32)
        prod[p] = acc
        return carry

    lax.fori_loop(0, width_x * NZB, eddy_block, 0)
    if exchange:
        first = pltpu.make_async_remote_copy(
            src_ref=near.at[pl.ds(0, group - 1)], dst_ref=near.at[pl.ds(0, group - 1)],
            send_sem=sems.at[0], recv_sem=sems.at[1], device_id=near_device(1), device_id_type=MESH,
        )
        first.wait_send()
        first.wait_recv()
        far[me // group] = jnp.sum(near[...], axis=0)

        def send_far(i, carry):
            pltpu.make_async_remote_copy(
                src_ref=far.at[me // group], dst_ref=far.at[me // group], send_sem=sems.at[2],
                recv_sem=sems.at[3], device_id=far_device(i), device_id_type=MESH,
            ).start()
            return carry

        lax.fori_loop(1, groups, send_far, 0)

    row = lax.broadcasted_iota(jnp.int32, (width_y, height), 0)
    lane = lax.broadcasted_iota(jnp.int32, (width_y, height), 1)

    def plane(x, carry):
        u0 = u_ref[0, x].astype(jnp.float32)
        u1 = u_ref[1, x].astype(jnp.float32)
        u2 = u_ref[2, x].astype(jnp.float32)
        viscous = EDDY_COEF * jnp.sqrt(1.0 + (u0 * u0 + u1 * u1 + u2 * u2))
        west_index = jnp.maximum(x - 1, 0)
        east_index = jnp.minimum(x + 1, width_x - 1)
        scale = fringe_ref[x]
        for c in range(components):
            center = a_ref[c, x]
            west = jnp.where(x == 0, w_ref[c, 0], a_ref[c, west_index])
            east = jnp.where(x == width_x - 1, e_ref[c, 0], a_ref[c, east_index])
            north = jnp.where(row == width_y - 1, jnp.broadcast_to(n_ref[c, x], (width_y, height)), pltpu.roll(center, width_y - 1, 0))
            south = jnp.where(row == 0, jnp.broadcast_to(s_ref[c, x], (width_y, height)), pltpu.roll(center, 1, 0))
            upper = jnp.where(lane == height - 1, 0.0, pltpu.roll(center, height - 1, 1))
            lower = jnp.where(lane == 0, 0.0, pltpu.roll(center, 1, 1))
            laplace = east + west + north + south + upper + lower - 6.0 * center
            advect = 0.5 * (u0 * (east - west) + u1 * (north - south) + u2 * (upper - lower))
            product = jnp.concatenate(
                [prod[2 * x + zb, c * width_y : (c + 1) * width_y, :] for zb in range(NZB)], axis=1
            )
            update = center + TIME_STEP * (advect + BASE_VISC * laplace + viscous * product)
            if c == 0:
                update = update - TIME_STEP * drag_ref[x] * u0 * center
            out_ref[c, x] = update * scale
        return carry

    lax.fori_loop(0, width_x, plane, 0)
    if exchange:
        second = pltpu.make_async_remote_copy(
            src_ref=far.at[pl.ds(0, groups - 1)], dst_ref=far.at[pl.ds(0, groups - 1)],
            send_sem=sems.at[2], recv_sem=sems.at[3], device_id=far_device(1), device_id_type=MESH,
        )
        second.wait_send()
        second.wait_recv()
        sum_ref[...] = jnp.sum(far[...], axis=0)


def advance(adjoint, west, east, south, north, forward, columns, eddy_blocks, drag_field, fringe_scale, turbine, prior, exchange):
    components, width_x, width_y, height = adjoint.shape
    vmem = pl.BlockSpec(memory_space=pltpu.VMEM)
    smem = pl.BlockSpec(memory_space=pltpu.SMEM)
    count_y = lax.axis_size("gy")
    total = lax.axis_size("gx") * count_y
    group = 8 if total % 8 == 0 and total > 8 else total // 2
    operands = [columns, fringe_scale, adjoint, west, east, south, north, forward, drag_field, eddy_blocks]
    operands += list(turbine) + [prior]
    out_shape = (jax.ShapeDtypeStruct(adjoint.shape, jnp.float32), jax.ShapeDtypeStruct(prior.shape, jnp.float32))
    scratch = [
        pltpu.VMEM(((width_x + 2) * NZB, components * width_y, height // NZB), jnp.bfloat16),
        pltpu.VMEM((width_x * NZB, components * width_y, height // NZB), jnp.float32),
    ]
    params = dict(vmem_limit_bytes=48 * 1024 * 1024)
    if exchange:
        scratch += [
            pltpu.VMEM((group,) + prior.shape, jnp.float32),
            pltpu.VMEM((total // group,) + prior.shape, jnp.float32),
            pltpu.SemaphoreType.DMA((4,)),
        ]
        params.update(collective_id=0, has_side_effects=True)
    return pl.pallas_call(
        functools.partial(advance_kernel, count_y, group, exchange),
        out_shape=out_shape,
        in_specs=[smem, smem] + [vmem] * (len(operands) - 2),
        out_specs=(vmem, vmem),
        scratch_shapes=scratch,
        compiler_params=pltpu.CompilerParams(**params),
    )(*operands)


def turbine_tables(owned_mask, plan_kernel, along_z, width_x, width_y):
    lanes = 128
    count = plan_kernel.shape[0]
    weights = (plan_kernel * owned_mask[:, None]).T.reshape(width_x, width_y, count)
    weights = jnp.zeros((width_x, width_y, lanes), jnp.float32).at[:, :, :count].set(weights)
    column = jnp.zeros((along_z.shape[1], lanes), jnp.float32).at[:, :count].set(along_z.T)
    return weights, column


def halo(block, axis, dim):
    count = lax.axis_size(axis)
    forward = [(i, (i + 1) % count) for i in range(count)]
    backward = [(target, source) for source, target in forward]
    low = lax.ppermute(lax.slice_in_dim(block, block.shape[dim] - 1, None, axis=dim), axis, forward)
    high = lax.ppermute(lax.slice_in_dim(block, 0, 1, axis=dim), axis, backward)
    return low, high


def shards(
    adjoint_in,
    checkpoints,
    send_owner,
    receive_rows,
    block_columns,
    eddy_blocks,
    thrust,
    yaw_angle,
    turbine_place,
    turbine_tile,
    fringe_rows,
):
    count_x = lax.axis_size("gx")
    count_y = lax.axis_size("gy")
    tile_count = count_x * count_y
    tile_index = lax.axis_index("gx") * count_y + lax.axis_index("gy")
    components, width_x, width_y, height = adjoint_in.shape
    steps_total = checkpoints.shape[0]
    block_shape = checkpoints.shape[2:]
    owner_ids = jnp.arange(tile_count, dtype=jnp.int32)
    onehot = (send_owner[:, None] == owner_ids[None, :]).astype(jnp.int32)
    slot_rank = jnp.sum(jnp.cumsum(onehot, axis=0) * onehot, axis=1) - 1
    position = send_owner * CAP + slot_rank
    slots = send_owner.shape[0]
    row_ids = jnp.arange(tile_count * CAP, dtype=jnp.int32)
    pack_table = (row_ids[:, None] == position[None, :]).astype(jnp.bfloat16)
    pack_table = pack_table.reshape(tile_count, CAP, slots)
    pick_table = (receive_rows[:, None] == row_ids[None, :]).astype(jnp.bfloat16)
    pick_table = pick_table.reshape(receive_rows.shape[0], tile_count, CAP)
    rows_x = lax.axis_index("gx") * width_x + jnp.arange(width_x, dtype=jnp.int32)
    fringe_hit = jnp.any(rows_x[:, None] == fringe_rows[None, :], axis=1)
    fringe_scale = jnp.where(fringe_hit, FRINGE_KEEP, 1.0).astype(jnp.float32)
    owned_mask, plan_kernel, along_z, drag_field = turbine_terms(
        tile_index, thrust, yaw_angle, turbine_place, turbine_tile, width_x, width_y, height
    )
    turbine = turbine_tables(owned_mask, plan_kernel, along_z, width_x, width_y)
    adjoint = adjoint_in
    gradient_block = jnp.zeros((8, 128), jnp.float32)
    for step_index in range(steps_total):
        stored = checkpoints[steps_total - 1 - step_index]
        packed = jnp.einsum(
            "drs,scb->dcrb", pack_table, stored, preferred_element_type=jnp.float32
        ).astype(jnp.bfloat16)
        arrived = lax.all_to_all(packed, ("gx", "gy"), split_axis=0, concat_axis=0, tiled=True)
        forward = jnp.einsum(
            "jsr,scrb->cjb", pick_table, arrived, preferred_element_type=jnp.float32
        ).astype(jnp.bfloat16)
        forward = forward.reshape(components, width_x, width_y, height)
        west, east = halo(adjoint, "gx", 1)
        south, north = halo(adjoint, "gy", 2)
        adjoint, gradient_block = advance(
            adjoint, west, east, south, north, forward, block_columns, eddy_blocks, drag_field, fringe_scale,
            turbine, gradient_block, step_index == steps_total - 1,
        )
    gradient_sum = gradient_block[0, : thrust.shape[0]]
    cosine = jnp.cos(yaw_angle)
    sine = jnp.sin(yaw_angle)
    control_gradient = jnp.stack(
        [
            -0.5 * TIME_STEP * cosine * cosine * gradient_sum,
            TIME_STEP * thrust * sine * cosine * gradient_sum,
        ]
    )
    return (adjoint, control_gradient)


def solution(mesh):
    return jax.shard_map(
        shards,
        mesh=mesh,
        in_specs=(
            P(None, "gx", "gy", None),
            P(None, ("gx", "gy"), None, None),
            P(("gx", "gy")),
            P(("gx", "gy")),
            P(("gx", "gy"), None),
            P(),
            P(),
            P(),
            P(),
            P(),
            P(),
        ),
        out_specs=(P(None, "gx", "gy", None), P()),
        check_vma=False,
    )
```

```python
import functools

import jax
import jax.numpy as jnp
from jax import lax
from jax.experimental import pallas as pl
from jax.experimental.pallas import tpu as pltpu
from jax.sharding import PartitionSpec as P

MESH = pl.DeviceIdType.MESH

PB = 128
KB = 8
CAP = 2
NZB = 2


TIME_STEP = 0.25
BASE_VISC = 0.1
EDDY_COEF = 0.5
KERNEL_WIDTH = 1.5
FRINGE_KEEP = 0.5


def turbine_terms(
    tile_index, thrust, yaw_angle, turbine_place, turbine_tile, width_x, width_y, height
):
    owned_mask = (turbine_tile == tile_index).astype(jnp.float32)
    spread = 2.0 * KERNEL_WIDTH * KERNEL_WIDTH
    along_x = jnp.exp(
        -(
            (jnp.arange(width_x, dtype=jnp.float32)[None, :] - turbine_place[0][:, None] * width_x)
            ** 2
        )
        / spread
    )
    along_y = jnp.exp(
        -(
            (jnp.arange(width_y, dtype=jnp.float32)[None, :] - turbine_place[1][:, None] * width_y)
            ** 2
        )
        / spread
    )
    along_z = jnp.exp(
        -(
            (
                jnp.arange(height, dtype=jnp.float32)[None, :]
                - turbine_place[2][:, None] * (0.5 * height)
            )
            ** 2
        )
        / spread
    )
    plan_kernel = (along_x[:, :, None] * along_y[:, None, :]).reshape(
        along_x.shape[0], width_x * width_y
    )
    cosine = jnp.cos(yaw_angle)
    loading = owned_mask * thrust * cosine * cosine
    drag_field = jnp.dot(
        (plan_kernel * loading[:, None]).T, along_z, precision=lax.Precision.HIGHEST
    )
    return (owned_mask, plan_kernel, along_z, drag_field.reshape(width_x, width_y, height))


def advance_kernel(count_y, group, exchange, *refs):
    (cols_ref, fringe_ref, a_ref, w_ref, e_ref, s_ref, n_ref, u_ref, drag_ref, eddy_ref, pk_ref, azh_ref,
     prior_ref, out_ref, sum_ref, xq, prod) = refs[:17]
    components, width_x, width_y, height = a_ref.shape
    if exchange:
        near, far, sems = refs[17:]
        total = lax.axis_size("gx") * count_y
        groups = total // group
        me = lax.axis_index("gx") * count_y + lax.axis_index("gy")
        mine, base = me % group, me - me % group

        def near_device(i):
            other = base + lax.rem(mine + i, group)
            return (other // count_y, other % count_y)

        def far_device(i):
            other = lax.rem(me + i * group, total)
            return (other // count_y, other % count_y)

        barrier = pltpu.get_barrier_semaphore()

        def greet_near(i, carry):
            pl.semaphore_signal(barrier, inc=1, device_id=near_device(i), device_id_type=MESH)
            return carry

        def greet_far(i, carry):
            pl.semaphore_signal(barrier, inc=1, device_id=far_device(i), device_id_type=MESH)
            return carry

        lax.fori_loop(1, group, greet_near, 0)
        lax.fori_loop(1, groups, greet_far, 0)

    def turbine_plane(x, acc):
        velocity = u_ref[0, x].astype(jnp.float32)
        density = velocity * velocity * a_ref[0, x]
        projected = jnp.dot(
            density, azh_ref[...], precision=lax.Precision.HIGHEST, preferred_element_type=jnp.float32
        )
        return acc + pk_ref[x] * projected

    acc = lax.fori_loop(0, width_x, turbine_plane, jnp.zeros(pk_ref.shape[1:], jnp.float32))
    first_row = lax.broadcasted_iota(jnp.int32, prior_ref.shape, 0) == 0
    part = prior_ref[...] + jnp.where(first_row, jnp.sum(acc, axis=0, keepdims=True), 0.0)
    if exchange:
        pl.semaphore_wait(barrier, group + groups - 2)
        near[mine] = part

        def send_near(i, carry):
            pltpu.make_async_remote_copy(
                src_ref=near.at[mine], dst_ref=near.at[mine], send_sem=sems.at[0], recv_sem=sems.at[1],
                device_id=near_device(i), device_id_type=MESH,
            ).start()
            return carry

        lax.fori_loop(1, group, send_near, 0)
    else:
        sum_ref[...] = part

    half = height // NZB

    def fill_plane(x, carry):
        for zb in range(NZB):
            for c in range(components):
                xq[2 * (x + 1) + zb, c * width_y : (c + 1) * width_y, :] = a_ref[c, x, :, zb * half : (zb + 1) * half].astype(jnp.bfloat16)
        return carry

    for zb in range(NZB):
        for c in range(components):
            xq[zb, c * width_y : (c + 1) * width_y, :] = w_ref[c, 0, :, zb * half : (zb + 1) * half].astype(jnp.bfloat16)
            xq[2 * (width_x + 1) + zb, c * width_y : (c + 1) * width_y, :] = e_ref[c, 0, :, zb * half : (zb + 1) * half].astype(jnp.bfloat16)
    lax.fori_loop(0, width_x, fill_plane, 0)

    def eddy_block(p, carry):
        acc = jnp.zeros((components * width_y, half), jnp.float32)
        for k in range(0, KB, 2):
            pair = jnp.concatenate([xq[cols_ref[p, k]], xq[cols_ref[p, k + 1]]], axis=1)
            acc = acc + jnp.dot(pair, eddy_ref[k // 2], preferred_element_type=jnp.float32)
        prod[p] = acc
        return carry

    lax.fori_loop(0, width_x * NZB, eddy_block, 0)
    if exchange:
        first = pltpu.make_async_remote_copy(
            src_ref=near.at[pl.ds(0, group - 1)], dst_ref=near.at[pl.ds(0, group - 1)],
            send_sem=sems.at[0], recv_sem=sems.at[1], device_id=near_device(1), device_id_type=MESH,
        )
        first.wait_send()
        first.wait_recv()
        far[me // group] = jnp.sum(near[...], axis=0)

        def send_far(i, carry):
            pltpu.make_async_remote_copy(
                src_ref=far.at[me // group], dst_ref=far.at[me // group], send_sem=sems.at[2],
                recv_sem=sems.at[3], device_id=far_device(i), device_id_type=MESH,
            ).start()
            return carry

        lax.fori_loop(1, groups, send_far, 0)

    row = lax.broadcasted_iota(jnp.int32, (width_y, height), 0)
    lane = lax.broadcasted_iota(jnp.int32, (width_y, height), 1)

    def plane(x, carry):
        u0 = u_ref[0, x].astype(jnp.float32)
        u1 = u_ref[1, x].astype(jnp.float32)
        u2 = u_ref[2, x].astype(jnp.float32)
        viscous = EDDY_COEF * jnp.sqrt(1.0 + (u0 * u0 + u1 * u1 + u2 * u2))
        west_index = jnp.maximum(x - 1, 0)
        east_index = jnp.minimum(x + 1, width_x - 1)
        scale = fringe_ref[x]
        for c in range(components):
            center = a_ref[c, x]
            west = jnp.where(x == 0, w_ref[c, 0], a_ref[c, west_index])
            east = jnp.where(x == width_x - 1, e_ref[c, 0], a_ref[c, east_index])
            north = jnp.where(row == width_y - 1, jnp.broadcast_to(n_ref[c, x], (width_y, height)), pltpu.roll(center, width_y - 1, 0))
            south = jnp.where(row == 0, jnp.broadcast_to(s_ref[c, x], (width_y, height)), pltpu.roll(center, 1, 0))
            upper = jnp.where(lane == height - 1, 0.0, pltpu.roll(center, height - 1, 1))
            lower = jnp.where(lane == 0, 0.0, pltpu.roll(center, 1, 1))
            laplace = east + west + north + south + upper + lower - 6.0 * center
            advect = 0.5 * (u0 * (east - west) + u1 * (north - south) + u2 * (upper - lower))
            product = jnp.concatenate(
                [prod[2 * x + zb, c * width_y : (c + 1) * width_y, :] for zb in range(NZB)], axis=1
            )
            update = center + TIME_STEP * (advect + BASE_VISC * laplace + viscous * product)
            if c == 0:
                update = update - TIME_STEP * drag_ref[x] * u0 * center
            out_ref[c, x] = update * scale
        return carry

    lax.fori_loop(0, width_x, plane, 0)
    if exchange:
        second = pltpu.make_async_remote_copy(
            src_ref=far.at[pl.ds(0, groups - 1)], dst_ref=far.at[pl.ds(0, groups - 1)],
            send_sem=sems.at[2], recv_sem=sems.at[3], device_id=far_device(1), device_id_type=MESH,
        )
        second.wait_send()
        second.wait_recv()
        sum_ref[...] = jnp.sum(far[...], axis=0)


def advance(adjoint, west, east, south, north, forward, columns, eddy_blocks, drag_field, fringe_scale, turbine, prior, exchange):
    components, width_x, width_y, height = adjoint.shape
    vmem = pl.BlockSpec(memory_space=pltpu.VMEM)
    smem = pl.BlockSpec(memory_space=pltpu.SMEM)
    count_y = lax.axis_size("gy")
    total = lax.axis_size("gx") * count_y
    group = 8 if total % 8 == 0 and total > 8 else total // 2
    paired = eddy_blocks.reshape(KB // 2, 2 * eddy_blocks.shape[1], eddy_blocks.shape[2])
    operands = [columns, fringe_scale, adjoint, west, east, south, north, forward, drag_field, paired]
    operands += list(turbine) + [prior]
    out_shape = (jax.ShapeDtypeStruct(adjoint.shape, jnp.float32), jax.ShapeDtypeStruct(prior.shape, jnp.float32))
    scratch = [
        pltpu.VMEM(((width_x + 2) * NZB, components * width_y, height // NZB), jnp.bfloat16),
        pltpu.VMEM((width_x * NZB, components * width_y, height // NZB), jnp.float32),
    ]
    params = dict(vmem_limit_bytes=48 * 1024 * 1024)
    if exchange:
        scratch += [
            pltpu.VMEM((group,) + prior.shape, jnp.float32),
            pltpu.VMEM((total // group,) + prior.shape, jnp.float32),
            pltpu.SemaphoreType.DMA((4,)),
        ]
        params.update(collective_id=0, has_side_effects=True)
    return pl.pallas_call(
        functools.partial(advance_kernel, count_y, group, exchange),
        out_shape=out_shape,
        in_specs=[smem, smem] + [vmem] * (len(operands) - 2),
        out_specs=(vmem, vmem),
        scratch_shapes=scratch,
        compiler_params=pltpu.CompilerParams(**params),
    )(*operands)


def turbine_tables(owned_mask, plan_kernel, along_z, width_x, width_y):
    lanes = 128
    count = plan_kernel.shape[0]
    weights = (plan_kernel * owned_mask[:, None]).T.reshape(width_x, width_y, count)
    weights = jnp.zeros((width_x, width_y, lanes), jnp.float32).at[:, :, :count].set(weights)
    column = jnp.zeros((along_z.shape[1], lanes), jnp.float32).at[:, :count].set(along_z.T)
    return weights, column


def halo(block, axis, dim):
    count = lax.axis_size(axis)
    forward = [(i, (i + 1) % count) for i in range(count)]
    backward = [(target, source) for source, target in forward]
    low = lax.ppermute(lax.slice_in_dim(block, block.shape[dim] - 1, None, axis=dim), axis, forward)
    high = lax.ppermute(lax.slice_in_dim(block, 0, 1, axis=dim), axis, backward)
    return low, high


def shards(
    adjoint_in,
    checkpoints,
    send_owner,
    receive_rows,
    block_columns,
    eddy_blocks,
    thrust,
    yaw_angle,
    turbine_place,
    turbine_tile,
    fringe_rows,
):
    count_x = lax.axis_size("gx")
    count_y = lax.axis_size("gy")
    tile_count = count_x * count_y
    tile_index = lax.axis_index("gx") * count_y + lax.axis_index("gy")
    components, width_x, width_y, height = adjoint_in.shape
    steps_total = checkpoints.shape[0]
    block_shape = checkpoints.shape[2:]
    owner_ids = jnp.arange(tile_count, dtype=jnp.int32)
    onehot = (send_owner[:, None] == owner_ids[None, :]).astype(jnp.int32)
    slot_rank = jnp.sum(jnp.cumsum(onehot, axis=0) * onehot, axis=1) - 1
    position = send_owner * CAP + slot_rank
    slots = send_owner.shape[0]
    row_ids = jnp.arange(tile_count * CAP, dtype=jnp.int32)
    pack_table = (row_ids[:, None] == position[None, :]).astype(jnp.bfloat16)
    pack_table = pack_table.reshape(tile_count, CAP, slots)
    pick_table = (receive_rows[:, None] == row_ids[None, :]).astype(jnp.bfloat16)
    pick_table = pick_table.reshape(receive_rows.shape[0], tile_count, CAP)
    rows_x = lax.axis_index("gx") * width_x + jnp.arange(width_x, dtype=jnp.int32)
    fringe_hit = jnp.any(rows_x[:, None] == fringe_rows[None, :], axis=1)
    fringe_scale = jnp.where(fringe_hit, FRINGE_KEEP, 1.0).astype(jnp.float32)
    owned_mask, plan_kernel, along_z, drag_field = turbine_terms(
        tile_index, thrust, yaw_angle, turbine_place, turbine_tile, width_x, width_y, height
    )
    turbine = turbine_tables(owned_mask, plan_kernel, along_z, width_x, width_y)
    adjoint = adjoint_in
    gradient_block = jnp.zeros((8, 128), jnp.float32)
    for step_index in range(steps_total):
        stored = checkpoints[steps_total - 1 - step_index]
        packed = jnp.einsum(
            "drs,scb->dcrb", pack_table, stored, preferred_element_type=jnp.float32
        ).astype(jnp.bfloat16)
        arrived = lax.all_to_all(packed, ("gx", "gy"), split_axis=0, concat_axis=0, tiled=True)
        forward = jnp.einsum(
            "jsr,scrb->cjb", pick_table, arrived, preferred_element_type=jnp.float32
        ).astype(jnp.bfloat16)
        forward = forward.reshape(components, width_x, width_y, height)
        west, east = halo(adjoint, "gx", 1)
        south, north = halo(adjoint, "gy", 2)
        adjoint, gradient_block = advance(
            adjoint, west, east, south, north, forward, block_columns, eddy_blocks, drag_field, fringe_scale,
            turbine, gradient_block, step_index == steps_total - 1,
        )
    gradient_sum = gradient_block[0, : thrust.shape[0]]
    cosine = jnp.cos(yaw_angle)
    sine = jnp.sin(yaw_angle)
    control_gradient = jnp.stack(
        [
            -0.5 * TIME_STEP * cosine * cosine * gradient_sum,
            TIME_STEP * thrust * sine * cosine * gradient_sum,
        ]
    )
    return (adjoint, control_gradient)


def solution(mesh):
    return jax.shard_map(
        shards,
        mesh=mesh,
        in_specs=(
            P(None, "gx", "gy", None),
            P(None, ("gx", "gy"), None, None),
            P(("gx", "gy")),
            P(("gx", "gy")),
            P(("gx", "gy"), None),
            P(),
            P(),
            P(),
            P(),
            P(),
            P(),
        ),
        out_specs=(P(None, "gx", "gy", None), P()),
        check_vma=False,
    )
```

```python
import functools

import jax
import jax.numpy as jnp
from jax import lax
from jax.experimental import pallas as pl
from jax.experimental.pallas import tpu as pltpu
from jax.sharding import PartitionSpec as P

MESH = pl.DeviceIdType.MESH

PB = 128
KB = 8
CAP = 2
NZB = 2


TIME_STEP = 0.25
BASE_VISC = 0.1
EDDY_COEF = 0.5
KERNEL_WIDTH = 1.5
FRINGE_KEEP = 0.5


def turbine_terms(
    tile_index, thrust, yaw_angle, turbine_place, turbine_tile, width_x, width_y, height
):
    owned_mask = (turbine_tile == tile_index).astype(jnp.float32)
    spread = 2.0 * KERNEL_WIDTH * KERNEL_WIDTH
    along_x = jnp.exp(
        -(
            (jnp.arange(width_x, dtype=jnp.float32)[None, :] - turbine_place[0][:, None] * width_x)
            ** 2
        )
        / spread
    )
    along_y = jnp.exp(
        -(
            (jnp.arange(width_y, dtype=jnp.float32)[None, :] - turbine_place[1][:, None] * width_y)
            ** 2
        )
        / spread
    )
    along_z = jnp.exp(
        -(
            (
                jnp.arange(height, dtype=jnp.float32)[None, :]
                - turbine_place[2][:, None] * (0.5 * height)
            )
            ** 2
        )
        / spread
    )
    plan_kernel = (along_x[:, :, None] * along_y[:, None, :]).reshape(
        along_x.shape[0], width_x * width_y
    )
    cosine = jnp.cos(yaw_angle)
    loading = owned_mask * thrust * cosine * cosine
    drag_field = jnp.dot(
        (plan_kernel * loading[:, None]).T, along_z, precision=lax.Precision.HIGHEST
    )
    return (owned_mask, plan_kernel, along_z, drag_field.reshape(width_x, width_y, height))


def advance_kernel(count_y, group, exchange, *refs):
    (cols_ref, fringe_ref, a_ref, w_ref, e_ref, s_ref, n_ref, u_ref, drag_ref, eddy_ref, pk_ref, azh_ref,
     prior_ref, out_ref, sum_ref, xq, prod) = refs[:17]
    components, width_x, width_y, height = a_ref.shape
    if exchange:
        near, far, sems = refs[17:]
        total = lax.axis_size("gx") * count_y
        groups = total // group
        me = lax.axis_index("gx") * count_y + lax.axis_index("gy")
        mine, base = me % group, me - me % group

        def near_device(i):
            other = base + lax.rem(mine + i, group)
            return (other // count_y, other % count_y)

        def far_device(i):
            other = lax.rem(me + i * group, total)
            return (other // count_y, other % count_y)

        barrier = pltpu.get_barrier_semaphore()

        def greet_near(i, carry):
            pl.semaphore_signal(barrier, inc=1, device_id=near_device(i), device_id_type=MESH)
            return carry

        def greet_far(i, carry):
            pl.semaphore_signal(barrier, inc=1, device_id=far_device(i), device_id_type=MESH)
            return carry

        lax.fori_loop(1, group, greet_near, 0)
        lax.fori_loop(1, groups, greet_far, 0)

    def turbine_plane(x, acc):
        velocity = u_ref[0, x].astype(jnp.float32)
        density = velocity * velocity * a_ref[0, x]
        projected = jnp.dot(
            density, azh_ref[...], precision=lax.Precision.HIGHEST, preferred_element_type=jnp.float32
        )
        return acc + pk_ref[x] * projected

    acc = lax.fori_loop(0, width_x, turbine_plane, jnp.zeros(pk_ref.shape[1:], jnp.float32))
    first_row = lax.broadcasted_iota(jnp.int32, prior_ref.shape, 0) == 0
    part = prior_ref[...] + jnp.where(first_row, jnp.sum(acc, axis=0, keepdims=True), 0.0)
    if exchange:
        pl.semaphore_wait(barrier, group + groups - 2)
        near[mine] = part

        def send_near(i, carry):
            pltpu.make_async_remote_copy(
                src_ref=near.at[mine], dst_ref=near.at[mine], send_sem=sems.at[0], recv_sem=sems.at[1],
                device_id=near_device(i), device_id_type=MESH,
            ).start()
            return carry

        lax.fori_loop(1, group, send_near, 0)
    else:
        sum_ref[...] = part

    half = height // NZB

    def fill_plane(x, carry):
        for zb in range(NZB):
            for c in range(components):
                xq[2 * (x + 1) + zb, c * width_y : (c + 1) * width_y, :] = a_ref[c, x, :, zb * half : (zb + 1) * half].astype(jnp.bfloat16)
        return carry

    for zb in range(NZB):
        for c in range(components):
            xq[zb, c * width_y : (c + 1) * width_y, :] = w_ref[c, 0, :, zb * half : (zb + 1) * half].astype(jnp.bfloat16)
            xq[2 * (width_x + 1) + zb, c * width_y : (c + 1) * width_y, :] = e_ref[c, 0, :, zb * half : (zb + 1) * half].astype(jnp.bfloat16)
    lax.fori_loop(0, width_x, fill_plane, 0)

    def eddy_block(p, carry):
        acc = jnp.zeros((components * width_y, half), jnp.float32)
        for k in range(0, KB, 2):
            pair = jnp.concatenate([xq[cols_ref[p, k]], xq[cols_ref[p, k + 1]]], axis=1)
            acc = acc + jnp.dot(pair, eddy_ref[k // 2], preferred_element_type=jnp.float32)
        prod[p] = acc
        return carry

    lax.fori_loop(0, width_x * NZB, eddy_block, 0)
    if exchange:
        first = pltpu.make_async_remote_copy(
            src_ref=near.at[pl.ds(0, group - 1)], dst_ref=near.at[pl.ds(0, group - 1)],
            send_sem=sems.at[0], recv_sem=sems.at[1], device_id=near_device(1), device_id_type=MESH,
        )
        first.wait_send()
        first.wait_recv()
        far[me // group] = jnp.sum(near[...], axis=0)

        def send_far(i, carry):
            pltpu.make_async_remote_copy(
                src_ref=far.at[me // group], dst_ref=far.at[me // group], send_sem=sems.at[2],
                recv_sem=sems.at[3], device_id=far_device(i), device_id_type=MESH,
            ).start()
            return carry

        lax.fori_loop(1, groups, send_far, 0)

    row = lax.broadcasted_iota(jnp.int32, (width_y, height), 0)
    lane = lax.broadcasted_iota(jnp.int32, (width_y, height), 1)

    def plane(x, west_of, east_of):
        u0 = u_ref[0, x].astype(jnp.float32)
        u1 = u_ref[1, x].astype(jnp.float32)
        u2 = u_ref[2, x].astype(jnp.float32)
        viscous = (TIME_STEP * EDDY_COEF) * jnp.sqrt(1.0 + (u0 * u0 + u1 * u1 + u2 * u2))
        diffuse = TIME_STEP * BASE_VISC
        carry_x, carry_y, carry_z = (0.5 * TIME_STEP) * u0, (0.5 * TIME_STEP) * u1, (0.5 * TIME_STEP) * u2
        east_weight, west_weight = diffuse + carry_x, diffuse - carry_x
        north_weight, south_weight = diffuse + carry_y, diffuse - carry_y
        upper_weight = jnp.where(lane == height - 1, 0.0, diffuse + carry_z)
        lower_weight = jnp.where(lane == 0, 0.0, diffuse - carry_z)
        centre_weight = 1.0 - 6.0 * diffuse
        drag = TIME_STEP * drag_ref[x] * u0
        scale = fringe_ref[x]
        for c in range(components):
            center = a_ref[c, x]
            north = jnp.where(row == width_y - 1, jnp.broadcast_to(n_ref[c, x], (width_y, height)), pltpu.roll(center, width_y - 1, 0))
            south = jnp.where(row == 0, jnp.broadcast_to(s_ref[c, x], (width_y, height)), pltpu.roll(center, 1, 0))
            product = jnp.concatenate(
                [prod[2 * x + zb, c * width_y : (c + 1) * width_y, :] for zb in range(NZB)], axis=1
            )
            update = (
                centre_weight * center
                + east_weight * east_of(c)
                + west_weight * west_of(c)
                + north_weight * north
                + south_weight * south
                + upper_weight * pltpu.roll(center, height - 1, 1)
                + lower_weight * pltpu.roll(center, 1, 1)
                + viscous * product
            )
            if c == 0:
                update = update - drag * center
            out_ref[c, x] = update * scale

    plane(0, lambda c: w_ref[c, 0], lambda c: a_ref[c, 1])

    def inner_plane(x, carry):
        plane(x, lambda c: a_ref[c, x - 1], lambda c: a_ref[c, x + 1])
        return carry

    lax.fori_loop(1, width_x - 1, inner_plane, 0)
    plane(width_x - 1, lambda c: a_ref[c, width_x - 2], lambda c: e_ref[c, 0])
    if exchange:
        second = pltpu.make_async_remote_copy(
            src_ref=far.at[pl.ds(0, groups - 1)], dst_ref=far.at[pl.ds(0, groups - 1)],
            send_sem=sems.at[2], recv_sem=sems.at[3], device_id=far_device(1), device_id_type=MESH,
        )
        second.wait_send()
        second.wait_recv()
        sum_ref[...] = jnp.sum(far[...], axis=0)


def advance(adjoint, west, east, south, north, forward, columns, eddy_blocks, drag_field, fringe_scale, turbine, prior, exchange):
    components, width_x, width_y, height = adjoint.shape
    vmem = pl.BlockSpec(memory_space=pltpu.VMEM)
    smem = pl.BlockSpec(memory_space=pltpu.SMEM)
    count_y = lax.axis_size("gy")
    total = lax.axis_size("gx") * count_y
    group = 8 if total % 8 == 0 and total > 8 else total // 2
    paired = eddy_blocks.reshape(KB // 2, 2 * eddy_blocks.shape[1], eddy_blocks.shape[2])
    operands = [columns, fringe_scale, adjoint, west, east, south, north, forward, drag_field, paired]
    operands += list(turbine) + [prior]
    out_shape = (jax.ShapeDtypeStruct(adjoint.shape, jnp.float32), jax.ShapeDtypeStruct(prior.shape, jnp.float32))
    scratch = [
        pltpu.VMEM(((width_x + 2) * NZB, components * width_y, height // NZB), jnp.bfloat16),
        pltpu.VMEM((width_x * NZB, components * width_y, height // NZB), jnp.float32),
    ]
    params = dict(vmem_limit_bytes=48 * 1024 * 1024)
    if exchange:
        scratch += [
            pltpu.VMEM((group,) + prior.shape, jnp.float32),
            pltpu.VMEM((total // group,) + prior.shape, jnp.float32),
            pltpu.SemaphoreType.DMA((4,)),
        ]
        params.update(collective_id=0, has_side_effects=True)
    return pl.pallas_call(
        functools.partial(advance_kernel, count_y, group, exchange),
        out_shape=out_shape,
        in_specs=[smem, smem] + [vmem] * (len(operands) - 2),
        out_specs=(vmem, vmem),
        scratch_shapes=scratch,
        compiler_params=pltpu.CompilerParams(**params),
    )(*operands)


def turbine_tables(owned_mask, plan_kernel, along_z, width_x, width_y):
    lanes = 128
    count = plan_kernel.shape[0]
    weights = (plan_kernel * owned_mask[:, None]).T.reshape(width_x, width_y, count)
    weights = jnp.zeros((width_x, width_y, lanes), jnp.float32).at[:, :, :count].set(weights)
    column = jnp.zeros((along_z.shape[1], lanes), jnp.float32).at[:, :count].set(along_z.T)
    return weights, column


def halo(block, axis, dim):
    count = lax.axis_size(axis)
    forward = [(i, (i + 1) % count) for i in range(count)]
    backward = [(target, source) for source, target in forward]
    low = lax.ppermute(lax.slice_in_dim(block, block.shape[dim] - 1, None, axis=dim), axis, forward)
    high = lax.ppermute(lax.slice_in_dim(block, 0, 1, axis=dim), axis, backward)
    return low, high


def shards(
    adjoint_in,
    checkpoints,
    send_owner,
    receive_rows,
    block_columns,
    eddy_blocks,
    thrust,
    yaw_angle,
    turbine_place,
    turbine_tile,
    fringe_rows,
):
    count_x = lax.axis_size("gx")
    count_y = lax.axis_size("gy")
    tile_count = count_x * count_y
    tile_index = lax.axis_index("gx") * count_y + lax.axis_index("gy")
    components, width_x, width_y, height = adjoint_in.shape
    steps_total = checkpoints.shape[0]
    block_shape = checkpoints.shape[2:]
    owner_ids = jnp.arange(tile_count, dtype=jnp.int32)
    onehot = (send_owner[:, None] == owner_ids[None, :]).astype(jnp.int32)
    slot_rank = jnp.sum(jnp.cumsum(onehot, axis=0) * onehot, axis=1) - 1
    position = send_owner * CAP + slot_rank
    slots = send_owner.shape[0]
    row_ids = jnp.arange(tile_count * CAP, dtype=jnp.int32)
    pack_table = (row_ids[:, None] == position[None, :]).astype(jnp.bfloat16)
    pack_table = pack_table.reshape(tile_count, CAP, slots)
    pick_table = (receive_rows[:, None] == row_ids[None, :]).astype(jnp.bfloat16)
    pick_table = pick_table.reshape(receive_rows.shape[0], tile_count, CAP)
    rows_x = lax.axis_index("gx") * width_x + jnp.arange(width_x, dtype=jnp.int32)
    fringe_hit = jnp.any(rows_x[:, None] == fringe_rows[None, :], axis=1)
    fringe_scale = jnp.where(fringe_hit, FRINGE_KEEP, 1.0).astype(jnp.float32)
    owned_mask, plan_kernel, along_z, drag_field = turbine_terms(
        tile_index, thrust, yaw_angle, turbine_place, turbine_tile, width_x, width_y, height
    )
    turbine = turbine_tables(owned_mask, plan_kernel, along_z, width_x, width_y)
    adjoint = adjoint_in
    gradient_block = jnp.zeros((8, 128), jnp.float32)
    for step_index in range(steps_total):
        stored = checkpoints[steps_total - 1 - step_index]
        packed = jnp.einsum(
            "drs,scb->dcrb", pack_table, stored, preferred_element_type=jnp.float32
        ).astype(jnp.bfloat16)
        arrived = lax.all_to_all(packed, ("gx", "gy"), split_axis=0, concat_axis=0, tiled=True)
        forward = jnp.einsum(
            "jsr,scrb->cjb", pick_table, arrived, preferred_element_type=jnp.float32
        ).astype(jnp.bfloat16)
        forward = forward.reshape(components, width_x, width_y, height)
        west, east = halo(adjoint, "gx", 1)
        south, north = halo(adjoint, "gy", 2)
        adjoint, gradient_block = advance(
            adjoint, west, east, south, north, forward, block_columns, eddy_blocks, drag_field, fringe_scale,
            turbine, gradient_block, step_index == steps_total - 1,
        )
    gradient_sum = gradient_block[0, : thrust.shape[0]]
    cosine = jnp.cos(yaw_angle)
    sine = jnp.sin(yaw_angle)
    control_gradient = jnp.stack(
        [
            -0.5 * TIME_STEP * cosine * cosine * gradient_sum,
            TIME_STEP * thrust * sine * cosine * gradient_sum,
        ]
    )
    return (adjoint, control_gradient)


def solution(mesh):
    return jax.shard_map(
        shards,
        mesh=mesh,
        in_specs=(
            P(None, "gx", "gy", None),
            P(None, ("gx", "gy"), None, None),
            P(("gx", "gy")),
            P(("gx", "gy")),
            P(("gx", "gy"), None),
            P(),
            P(),
            P(),
            P(),
            P(),
            P(),
        ),
        out_specs=(P(None, "gx", "gy", None), P()),
        check_vma=False,
    )
```

```python
import functools

import jax
import jax.numpy as jnp
from jax import lax
from jax.experimental import pallas as pl
from jax.experimental.pallas import tpu as pltpu
from jax.sharding import PartitionSpec as P

MESH = pl.DeviceIdType.MESH

PB = 128
KB = 8
CAP = 2
NZB = 2


TIME_STEP = 0.25
BASE_VISC = 0.1
EDDY_COEF = 0.5
KERNEL_WIDTH = 1.5
FRINGE_KEEP = 0.5


def turbine_terms(
    tile_index, thrust, yaw_angle, turbine_place, turbine_tile, width_x, width_y, height
):
    owned_mask = (turbine_tile == tile_index).astype(jnp.float32)
    spread = 2.0 * KERNEL_WIDTH * KERNEL_WIDTH
    along_x = jnp.exp(
        -(
            (jnp.arange(width_x, dtype=jnp.float32)[None, :] - turbine_place[0][:, None] * width_x)
            ** 2
        )
        / spread
    )
    along_y = jnp.exp(
        -(
            (jnp.arange(width_y, dtype=jnp.float32)[None, :] - turbine_place[1][:, None] * width_y)
            ** 2
        )
        / spread
    )
    along_z = jnp.exp(
        -(
            (
                jnp.arange(height, dtype=jnp.float32)[None, :]
                - turbine_place[2][:, None] * (0.5 * height)
            )
            ** 2
        )
        / spread
    )
    plan_kernel = (along_x[:, :, None] * along_y[:, None, :]).reshape(
        along_x.shape[0], width_x * width_y
    )
    cosine = jnp.cos(yaw_angle)
    loading = owned_mask * thrust * cosine * cosine
    drag_field = jnp.dot(
        (plan_kernel * loading[:, None]).T, along_z, precision=lax.Precision.HIGHEST
    )
    return (owned_mask, plan_kernel, along_z, drag_field.reshape(width_x, width_y, height))


def advance_kernel(count_y, group, exchange, *refs):
    (cols_ref, fringe_ref, a_ref, w_ref, e_ref, s_ref, n_ref, u_ref, drag_ref, eddy_ref, pk_ref, azh_ref,
     prior_ref, out_ref, sum_ref, xq, prod) = refs[:17]
    components, width_x, width_y, height = a_ref.shape
    if exchange:
        near, far, sems = refs[17:]
        total = lax.axis_size("gx") * count_y
        groups = total // group
        me = lax.axis_index("gx") * count_y + lax.axis_index("gy")
        mine, base = me % group, me - me % group

        def near_device(i):
            other = base + lax.rem(mine + i, group)
            return (other // count_y, other % count_y)

        def far_device(i):
            other = lax.rem(me + i * group, total)
            return (other // count_y, other % count_y)

        barrier = pltpu.get_barrier_semaphore()

        def greet_near(i, carry):
            pl.semaphore_signal(barrier, inc=1, device_id=near_device(i), device_id_type=MESH)
            return carry

        def greet_far(i, carry):
            pl.semaphore_signal(barrier, inc=1, device_id=far_device(i), device_id_type=MESH)
            return carry

        lax.fori_loop(1, group, greet_near, 0)
        lax.fori_loop(1, groups, greet_far, 0)

    def turbine_plane(x, acc):
        velocity = u_ref[0, x].astype(jnp.float32)
        density = velocity * velocity * a_ref[0, x]
        high = density.astype(jnp.bfloat16)
        low = (density - high.astype(jnp.float32)).astype(jnp.bfloat16)
        projected = (
            jnp.dot(high, azh_ref[0], preferred_element_type=jnp.float32)
            + jnp.dot(high, azh_ref[1], preferred_element_type=jnp.float32)
            + jnp.dot(low, azh_ref[0], preferred_element_type=jnp.float32)
        )
        return acc + pk_ref[x] * projected

    acc = lax.fori_loop(0, width_x, turbine_plane, jnp.zeros(pk_ref.shape[1:], jnp.float32))
    first_row = lax.broadcasted_iota(jnp.int32, prior_ref.shape, 0) == 0
    part = prior_ref[...] + jnp.where(first_row, jnp.sum(acc, axis=0, keepdims=True), 0.0)
    if exchange:
        pl.semaphore_wait(barrier, group + groups - 2)
        near[mine] = part

        def send_near(i, carry):
            pltpu.make_async_remote_copy(
                src_ref=near.at[mine], dst_ref=near.at[mine], send_sem=sems.at[0], recv_sem=sems.at[1],
                device_id=near_device(i), device_id_type=MESH,
            ).start()
            return carry

        lax.fori_loop(1, group, send_near, 0)
    else:
        sum_ref[...] = part

    half = height // NZB

    def fill_plane(x, carry):
        for zb in range(NZB):
            for c in range(components):
                xq[2 * (x + 1) + zb, c * width_y : (c + 1) * width_y, :] = a_ref[c, x, :, zb * half : (zb + 1) * half].astype(jnp.bfloat16)
        return carry

    for zb in range(NZB):
        for c in range(components):
            xq[zb, c * width_y : (c + 1) * width_y, :] = w_ref[c, 0, :, zb * half : (zb + 1) * half].astype(jnp.bfloat16)
            xq[2 * (width_x + 1) + zb, c * width_y : (c + 1) * width_y, :] = e_ref[c, 0, :, zb * half : (zb + 1) * half].astype(jnp.bfloat16)
    lax.fori_loop(0, width_x, fill_plane, 0)

    def eddy_block(p, carry):
        acc = jnp.zeros((components * width_y, half), jnp.float32)
        for k in range(0, KB, 2):
            pair = jnp.concatenate([xq[cols_ref[p, k]], xq[cols_ref[p, k + 1]]], axis=1)
            acc = acc + jnp.dot(pair, eddy_ref[k // 2], preferred_element_type=jnp.float32)
        prod[p] = acc
        return carry

    lax.fori_loop(0, width_x * NZB, eddy_block, 0)
    if exchange:
        first = pltpu.make_async_remote_copy(
            src_ref=near.at[pl.ds(0, group - 1)], dst_ref=near.at[pl.ds(0, group - 1)],
            send_sem=sems.at[0], recv_sem=sems.at[1], device_id=near_device(1), device_id_type=MESH,
        )
        first.wait_send()
        first.wait_recv()
        far[me // group] = jnp.sum(near[...], axis=0)

        def send_far(i, carry):
            pltpu.make_async_remote_copy(
                src_ref=far.at[me // group], dst_ref=far.at[me // group], send_sem=sems.at[2],
                recv_sem=sems.at[3], device_id=far_device(i), device_id_type=MESH,
            ).start()
            return carry

        lax.fori_loop(1, groups, send_far, 0)

    row = lax.broadcasted_iota(jnp.int32, (width_y, height), 0)
    lane = lax.broadcasted_iota(jnp.int32, (width_y, height), 1)

    def plane(x, west_of, east_of):
        u0 = u_ref[0, x].astype(jnp.float32)
        u1 = u_ref[1, x].astype(jnp.float32)
        u2 = u_ref[2, x].astype(jnp.float32)
        viscous = (TIME_STEP * EDDY_COEF) * jnp.sqrt(1.0 + (u0 * u0 + u1 * u1 + u2 * u2))
        diffuse = TIME_STEP * BASE_VISC
        carry_x, carry_y, carry_z = (0.5 * TIME_STEP) * u0, (0.5 * TIME_STEP) * u1, (0.5 * TIME_STEP) * u2
        east_weight, west_weight = diffuse + carry_x, diffuse - carry_x
        north_weight, south_weight = diffuse + carry_y, diffuse - carry_y
        upper_weight = jnp.where(lane == height - 1, 0.0, diffuse + carry_z)
        lower_weight = jnp.where(lane == 0, 0.0, diffuse - carry_z)
        centre_weight = 1.0 - 6.0 * diffuse
        drag = TIME_STEP * drag_ref[x] * u0
        scale = fringe_ref[x]
        for c in range(components):
            center = a_ref[c, x]
            north = jnp.where(row == width_y - 1, jnp.broadcast_to(n_ref[c, x], (width_y, height)), pltpu.roll(center, width_y - 1, 0))
            south = jnp.where(row == 0, jnp.broadcast_to(s_ref[c, x], (width_y, height)), pltpu.roll(center, 1, 0))
            product = jnp.concatenate(
                [prod[2 * x + zb, c * width_y : (c + 1) * width_y, :] for zb in range(NZB)], axis=1
            )
            update = (
                centre_weight * center
                + east_weight * east_of(c)
                + west_weight * west_of(c)
                + north_weight * north
                + south_weight * south
                + upper_weight * pltpu.roll(center, height - 1, 1)
                + lower_weight * pltpu.roll(center, 1, 1)
                + viscous * product
            )
            if c == 0:
                update = update - drag * center
            out_ref[c, x] = update * scale

    plane(0, lambda c: w_ref[c, 0], lambda c: a_ref[c, 1])

    def inner_plane(x, carry):
        plane(x, lambda c: a_ref[c, x - 1], lambda c: a_ref[c, x + 1])
        return carry

    lax.fori_loop(1, width_x - 1, inner_plane, 0)
    plane(width_x - 1, lambda c: a_ref[c, width_x - 2], lambda c: e_ref[c, 0])
    if exchange:
        second = pltpu.make_async_remote_copy(
            src_ref=far.at[pl.ds(0, groups - 1)], dst_ref=far.at[pl.ds(0, groups - 1)],
            send_sem=sems.at[2], recv_sem=sems.at[3], device_id=far_device(1), device_id_type=MESH,
        )
        second.wait_send()
        second.wait_recv()
        sum_ref[...] = jnp.sum(far[...], axis=0)


def advance(adjoint, west, east, south, north, forward, columns, eddy_blocks, drag_field, fringe_scale, turbine, prior, exchange):
    components, width_x, width_y, height = adjoint.shape
    vmem = pl.BlockSpec(memory_space=pltpu.VMEM)
    smem = pl.BlockSpec(memory_space=pltpu.SMEM)
    count_y = lax.axis_size("gy")
    total = lax.axis_size("gx") * count_y
    group = 8 if total % 8 == 0 and total > 8 else total // 2
    paired = eddy_blocks.reshape(KB // 2, 2 * eddy_blocks.shape[1], eddy_blocks.shape[2])
    operands = [columns, fringe_scale, adjoint, west, east, south, north, forward, drag_field, paired]
    operands += list(turbine) + [prior]
    out_shape = (jax.ShapeDtypeStruct(adjoint.shape, jnp.float32), jax.ShapeDtypeStruct(prior.shape, jnp.float32))
    scratch = [
        pltpu.VMEM(((width_x + 2) * NZB, components * width_y, height // NZB), jnp.bfloat16),
        pltpu.VMEM((width_x * NZB, components * width_y, height // NZB), jnp.float32),
    ]
    params = dict(vmem_limit_bytes=48 * 1024 * 1024)
    if exchange:
        scratch += [
            pltpu.VMEM((group,) + prior.shape, jnp.float32),
            pltpu.VMEM((total // group,) + prior.shape, jnp.float32),
            pltpu.SemaphoreType.DMA((4,)),
        ]
        params.update(collective_id=0, has_side_effects=True)
    return pl.pallas_call(
        functools.partial(advance_kernel, count_y, group, exchange),
        out_shape=out_shape,
        in_specs=[smem, smem] + [vmem] * (len(operands) - 2),
        out_specs=(vmem, vmem),
        scratch_shapes=scratch,
        compiler_params=pltpu.CompilerParams(**params),
    )(*operands)


def turbine_tables(owned_mask, plan_kernel, along_z, width_x, width_y):
    lanes = 128
    count = plan_kernel.shape[0]
    weights = (plan_kernel * owned_mask[:, None]).T.reshape(width_x, width_y, count)
    weights = jnp.zeros((width_x, width_y, lanes), jnp.float32).at[:, :, :count].set(weights)
    column = jnp.zeros((along_z.shape[1], lanes), jnp.float32).at[:, :count].set(along_z.T)
    high = lax.reduce_precision(column, exponent_bits=8, mantissa_bits=7)
    low = column - high
    return weights, jnp.stack([high, low]).astype(jnp.bfloat16)


def halo(block, axis, dim):
    count = lax.axis_size(axis)
    forward = [(i, (i + 1) % count) for i in range(count)]
    backward = [(target, source) for source, target in forward]
    low = lax.ppermute(lax.slice_in_dim(block, block.shape[dim] - 1, None, axis=dim), axis, forward)
    high = lax.ppermute(lax.slice_in_dim(block, 0, 1, axis=dim), axis, backward)
    return low, high


def shards(
    adjoint_in,
    checkpoints,
    send_owner,
    receive_rows,
    block_columns,
    eddy_blocks,
    thrust,
    yaw_angle,
    turbine_place,
    turbine_tile,
    fringe_rows,
):
    count_x = lax.axis_size("gx")
    count_y = lax.axis_size("gy")
    tile_count = count_x * count_y
    tile_index = lax.axis_index("gx") * count_y + lax.axis_index("gy")
    components, width_x, width_y, height = adjoint_in.shape
    steps_total = checkpoints.shape[0]
    block_shape = checkpoints.shape[2:]
    owner_ids = jnp.arange(tile_count, dtype=jnp.int32)
    onehot = (send_owner[:, None] == owner_ids[None, :]).astype(jnp.int32)
    slot_rank = jnp.sum(jnp.cumsum(onehot, axis=0) * onehot, axis=1) - 1
    position = send_owner * CAP + slot_rank
    slots = send_owner.shape[0]
    row_ids = jnp.arange(tile_count * CAP, dtype=jnp.int32)
    pack_table = (row_ids[:, None] == position[None, :]).astype(jnp.bfloat16)
    pack_table = pack_table.reshape(tile_count, CAP, slots)
    pick_table = (receive_rows[:, None] == row_ids[None, :]).astype(jnp.bfloat16)
    pick_table = pick_table.reshape(receive_rows.shape[0], tile_count, CAP)
    rows_x = lax.axis_index("gx") * width_x + jnp.arange(width_x, dtype=jnp.int32)
    fringe_hit = jnp.any(rows_x[:, None] == fringe_rows[None, :], axis=1)
    fringe_scale = jnp.where(fringe_hit, FRINGE_KEEP, 1.0).astype(jnp.float32)
    owned_mask, plan_kernel, along_z, drag_field = turbine_terms(
        tile_index, thrust, yaw_angle, turbine_place, turbine_tile, width_x, width_y, height
    )
    turbine = turbine_tables(owned_mask, plan_kernel, along_z, width_x, width_y)
    adjoint = adjoint_in
    gradient_block = jnp.zeros((8, 128), jnp.float32)
    for step_index in range(steps_total):
        stored = checkpoints[steps_total - 1 - step_index]
        packed = jnp.einsum(
            "drs,scb->dcrb", pack_table, stored, preferred_element_type=jnp.float32
        ).astype(jnp.bfloat16)
        arrived = lax.all_to_all(packed, ("gx", "gy"), split_axis=0, concat_axis=0, tiled=True)
        forward = jnp.einsum(
            "jsr,scrb->cjb", pick_table, arrived, preferred_element_type=jnp.float32
        ).astype(jnp.bfloat16)
        forward = forward.reshape(components, width_x, width_y, height)
        west, east = halo(adjoint, "gx", 1)
        south, north = halo(adjoint, "gy", 2)
        adjoint, gradient_block = advance(
            adjoint, west, east, south, north, forward, block_columns, eddy_blocks, drag_field, fringe_scale,
            turbine, gradient_block, step_index == steps_total - 1,
        )
    gradient_sum = gradient_block[0, : thrust.shape[0]]
    cosine = jnp.cos(yaw_angle)
    sine = jnp.sin(yaw_angle)
    control_gradient = jnp.stack(
        [
            -0.5 * TIME_STEP * cosine * cosine * gradient_sum,
            TIME_STEP * thrust * sine * cosine * gradient_sum,
        ]
    )
    return (adjoint, control_gradient)


def solution(mesh):
    return jax.shard_map(
        shards,
        mesh=mesh,
        in_specs=(
            P(None, "gx", "gy", None),
            P(None, ("gx", "gy"), None, None),
            P(("gx", "gy")),
            P(("gx", "gy")),
            P(("gx", "gy"), None),
            P(),
            P(),
            P(),
            P(),
            P(),
            P(),
        ),
        out_specs=(P(None, "gx", "gy", None), P()),
        check_vma=False,
    )
```

```python
import functools

import jax
import jax.numpy as jnp
from jax import lax
from jax.experimental import pallas as pl
from jax.experimental.pallas import tpu as pltpu
from jax.sharding import PartitionSpec as P

MESH = pl.DeviceIdType.MESH

PB = 128
KB = 8
CAP = 2
NZB = 2


TIME_STEP = 0.25
BASE_VISC = 0.1
EDDY_COEF = 0.5
KERNEL_WIDTH = 1.5
FRINGE_KEEP = 0.5


def turbine_terms(
    tile_index, thrust, yaw_angle, turbine_place, turbine_tile, width_x, width_y, height
):
    owned_mask = (turbine_tile == tile_index).astype(jnp.float32)
    spread = 2.0 * KERNEL_WIDTH * KERNEL_WIDTH
    along_x = jnp.exp(
        -(
            (jnp.arange(width_x, dtype=jnp.float32)[None, :] - turbine_place[0][:, None] * width_x)
            ** 2
        )
        / spread
    )
    along_y = jnp.exp(
        -(
            (jnp.arange(width_y, dtype=jnp.float32)[None, :] - turbine_place[1][:, None] * width_y)
            ** 2
        )
        / spread
    )
    along_z = jnp.exp(
        -(
            (
                jnp.arange(height, dtype=jnp.float32)[None, :]
                - turbine_place[2][:, None] * (0.5 * height)
            )
            ** 2
        )
        / spread
    )
    plan_kernel = (along_x[:, :, None] * along_y[:, None, :]).reshape(
        along_x.shape[0], width_x * width_y
    )
    cosine = jnp.cos(yaw_angle)
    loading = owned_mask * thrust * cosine * cosine
    drag_field = jnp.dot(
        (plan_kernel * loading[:, None]).T, along_z, precision=lax.Precision.HIGHEST
    )
    return (owned_mask, plan_kernel, along_z, drag_field.reshape(width_x, width_y, height))


def advance_kernel(count_y, group, exchange, *refs):
    (cols_ref, fringe_ref, a_ref, w_ref, e_ref, s_ref, n_ref, u_ref, drag_ref, eddy_ref, pk_ref, azh_ref,
     prior_ref, out_ref, sum_ref, first_plane, last_plane, first_row, last_row, xq, prod) = refs[:21]
    components, width_x, width_y, height = a_ref.shape
    if exchange:
        near, far, sems = refs[21:]
        total = lax.axis_size("gx") * count_y
        groups = total // group
        me = lax.axis_index("gx") * count_y + lax.axis_index("gy")
        mine, base = me % group, me - me % group

        def near_device(i):
            other = base + lax.rem(mine + i, group)
            return (other // count_y, other % count_y)

        def far_device(i):
            other = lax.rem(me + i * group, total)
            return (other // count_y, other % count_y)

        barrier = pltpu.get_barrier_semaphore()

        def greet_near(i, carry):
            pl.semaphore_signal(barrier, inc=1, device_id=near_device(i), device_id_type=MESH)
            return carry

        def greet_far(i, carry):
            pl.semaphore_signal(barrier, inc=1, device_id=far_device(i), device_id_type=MESH)
            return carry

        lax.fori_loop(1, group, greet_near, 0)
        lax.fori_loop(1, groups, greet_far, 0)

    def turbine_plane(x, acc):
        velocity = u_ref[0, x].astype(jnp.float32)
        density = velocity * velocity * a_ref[0, x]
        high = density.astype(jnp.bfloat16)
        low = (density - high.astype(jnp.float32)).astype(jnp.bfloat16)
        projected = (
            jnp.dot(high, azh_ref[0], preferred_element_type=jnp.float32)
            + jnp.dot(high, azh_ref[1], preferred_element_type=jnp.float32)
            + jnp.dot(low, azh_ref[0], preferred_element_type=jnp.float32)
        )
        return acc + pk_ref[x] * projected

    acc = lax.fori_loop(0, width_x, turbine_plane, jnp.zeros(pk_ref.shape[1:], jnp.float32))
    leading_row = lax.broadcasted_iota(jnp.int32, prior_ref.shape, 0) == 0
    part = prior_ref[...] + jnp.where(leading_row, jnp.sum(acc, axis=0, keepdims=True), 0.0)
    if exchange:
        pl.semaphore_wait(barrier, group + groups - 2)
        near[mine] = part

        def send_near(i, carry):
            pltpu.make_async_remote_copy(
                src_ref=near.at[mine], dst_ref=near.at[mine], send_sem=sems.at[0], recv_sem=sems.at[1],
                device_id=near_device(i), device_id_type=MESH,
            ).start()
            return carry

        lax.fori_loop(1, group, send_near, 0)
    else:
        sum_ref[...] = part

    half = height // NZB

    def fill_plane(x, carry):
        for zb in range(NZB):
            for c in range(components):
                xq[2 * (x + 1) + zb, c * width_y : (c + 1) * width_y, :] = a_ref[c, x, :, zb * half : (zb + 1) * half].astype(jnp.bfloat16)
        return carry

    for zb in range(NZB):
        for c in range(components):
            xq[zb, c * width_y : (c + 1) * width_y, :] = w_ref[c, 0, :, zb * half : (zb + 1) * half].astype(jnp.bfloat16)
            xq[2 * (width_x + 1) + zb, c * width_y : (c + 1) * width_y, :] = e_ref[c, 0, :, zb * half : (zb + 1) * half].astype(jnp.bfloat16)
    lax.fori_loop(0, width_x, fill_plane, 0)

    def eddy_block(p, carry):
        acc = jnp.zeros((components * width_y, half), jnp.float32)
        for k in range(0, KB, 2):
            pair = jnp.concatenate([xq[cols_ref[p, k]], xq[cols_ref[p, k + 1]]], axis=1)
            acc = acc + jnp.dot(pair, eddy_ref[k // 2], preferred_element_type=jnp.float32)
        prod[p] = acc
        return carry

    lax.fori_loop(0, width_x * NZB, eddy_block, 0)
    if exchange:
        first = pltpu.make_async_remote_copy(
            src_ref=near.at[pl.ds(0, group - 1)], dst_ref=near.at[pl.ds(0, group - 1)],
            send_sem=sems.at[0], recv_sem=sems.at[1], device_id=near_device(1), device_id_type=MESH,
        )
        first.wait_send()
        first.wait_recv()
        far[me // group] = jnp.sum(near[...], axis=0)

        def send_far(i, carry):
            pltpu.make_async_remote_copy(
                src_ref=far.at[me // group], dst_ref=far.at[me // group], send_sem=sems.at[2],
                recv_sem=sems.at[3], device_id=far_device(i), device_id_type=MESH,
            ).start()
            return carry

        lax.fori_loop(1, groups, send_far, 0)

    row = lax.broadcasted_iota(jnp.int32, (width_y, height), 0)
    lane = lax.broadcasted_iota(jnp.int32, (width_y, height), 1)

    def plane(x, west_of, east_of):
        u0 = u_ref[0, x].astype(jnp.float32)
        u1 = u_ref[1, x].astype(jnp.float32)
        u2 = u_ref[2, x].astype(jnp.float32)
        viscous = (TIME_STEP * EDDY_COEF) * jnp.sqrt(1.0 + (u0 * u0 + u1 * u1 + u2 * u2))
        diffuse = TIME_STEP * BASE_VISC
        carry_x, carry_y, carry_z = (0.5 * TIME_STEP) * u0, (0.5 * TIME_STEP) * u1, (0.5 * TIME_STEP) * u2
        east_weight, west_weight = diffuse + carry_x, diffuse - carry_x
        north_weight, south_weight = diffuse + carry_y, diffuse - carry_y
        upper_weight = jnp.where(lane == height - 1, 0.0, diffuse + carry_z)
        lower_weight = jnp.where(lane == 0, 0.0, diffuse - carry_z)
        centre_weight = 1.0 - 6.0 * diffuse
        drag = TIME_STEP * drag_ref[x] * u0
        scale = fringe_ref[x]
        for c in range(components):
            center = a_ref[c, x]
            north = jnp.where(row == width_y - 1, jnp.broadcast_to(n_ref[c, x], (width_y, height)), pltpu.roll(center, width_y - 1, 0))
            south = jnp.where(row == 0, jnp.broadcast_to(s_ref[c, x], (width_y, height)), pltpu.roll(center, 1, 0))
            product = jnp.concatenate(
                [prod[2 * x + zb, c * width_y : (c + 1) * width_y, :] for zb in range(NZB)], axis=1
            )
            update = (
                centre_weight * center
                + east_weight * east_of(c)
                + west_weight * west_of(c)
                + north_weight * north
                + south_weight * south
                + upper_weight * pltpu.roll(center, height - 1, 1)
                + lower_weight * pltpu.roll(center, 1, 1)
                + viscous * product
            )
            if c == 0:
                update = update - drag * center
            final = update * scale
            out_ref[c, x] = final
            first_row[c, x] = final[0:1, :]
            last_row[c, x] = final[width_y - 1 :, :]
            if isinstance(x, int) and x == 0:
                first_plane[c, 0] = final
            if isinstance(x, int) and x == width_x - 1:
                last_plane[c, 0] = final

    plane(0, lambda c: w_ref[c, 0], lambda c: a_ref[c, 1])

    def inner_plane(x, carry):
        plane(x, lambda c: a_ref[c, x - 1], lambda c: a_ref[c, x + 1])
        return carry

    lax.fori_loop(1, width_x - 1, inner_plane, 0)
    plane(width_x - 1, lambda c: a_ref[c, width_x - 2], lambda c: e_ref[c, 0])
    if exchange:
        second = pltpu.make_async_remote_copy(
            src_ref=far.at[pl.ds(0, groups - 1)], dst_ref=far.at[pl.ds(0, groups - 1)],
            send_sem=sems.at[2], recv_sem=sems.at[3], device_id=far_device(1), device_id_type=MESH,
        )
        second.wait_send()
        second.wait_recv()
        sum_ref[...] = jnp.sum(far[...], axis=0)


def advance(adjoint, west, east, south, north, forward, columns, eddy_blocks, drag_field, fringe_scale, turbine, prior, exchange):
    components, width_x, width_y, height = adjoint.shape
    vmem = pl.BlockSpec(memory_space=pltpu.VMEM)
    smem = pl.BlockSpec(memory_space=pltpu.SMEM)
    count_y = lax.axis_size("gy")
    total = lax.axis_size("gx") * count_y
    group = 8 if total % 8 == 0 and total > 8 else total // 2
    paired = eddy_blocks.reshape(KB // 2, 2 * eddy_blocks.shape[1], eddy_blocks.shape[2])
    operands = [columns, fringe_scale, adjoint, west, east, south, north, forward, drag_field, paired]
    operands += list(turbine) + [prior]
    out_shape = (
        jax.ShapeDtypeStruct(adjoint.shape, jnp.float32),
        jax.ShapeDtypeStruct(prior.shape, jnp.float32),
        jax.ShapeDtypeStruct((components, 1, width_y, height), jnp.float32),
        jax.ShapeDtypeStruct((components, 1, width_y, height), jnp.float32),
        jax.ShapeDtypeStruct((components, width_x, 1, height), jnp.float32),
        jax.ShapeDtypeStruct((components, width_x, 1, height), jnp.float32),
    )
    scratch = [
        pltpu.VMEM(((width_x + 2) * NZB, components * width_y, height // NZB), jnp.bfloat16),
        pltpu.VMEM((width_x * NZB, components * width_y, height // NZB), jnp.float32),
    ]
    params = dict(vmem_limit_bytes=48 * 1024 * 1024)
    if exchange:
        scratch += [
            pltpu.VMEM((group,) + prior.shape, jnp.float32),
            pltpu.VMEM((total // group,) + prior.shape, jnp.float32),
            pltpu.SemaphoreType.DMA((4,)),
        ]
        params.update(collective_id=0, has_side_effects=True)
    return pl.pallas_call(
        functools.partial(advance_kernel, count_y, group, exchange),
        out_shape=out_shape,
        in_specs=[smem, smem] + [vmem] * (len(operands) - 2),
        out_specs=tuple([vmem] * len(out_shape)),
        scratch_shapes=scratch,
        compiler_params=pltpu.CompilerParams(**params),
    )(*operands)


def turbine_tables(owned_mask, plan_kernel, along_z, width_x, width_y):
    lanes = 128
    count = plan_kernel.shape[0]
    weights = (plan_kernel * owned_mask[:, None]).T.reshape(width_x, width_y, count)
    weights = jnp.zeros((width_x, width_y, lanes), jnp.float32).at[:, :, :count].set(weights)
    column = jnp.zeros((along_z.shape[1], lanes), jnp.float32).at[:, :count].set(along_z.T)
    high = lax.reduce_precision(column, exponent_bits=8, mantissa_bits=7)
    low = column - high
    return weights, jnp.stack([high, low]).astype(jnp.bfloat16)


def halo(first, last, axis):
    count = lax.axis_size(axis)
    forward = [(i, (i + 1) % count) for i in range(count)]
    backward = [(target, source) for source, target in forward]
    return lax.ppermute(last, axis, forward), lax.ppermute(first, axis, backward)


def shards(
    adjoint_in,
    checkpoints,
    send_owner,
    receive_rows,
    block_columns,
    eddy_blocks,
    thrust,
    yaw_angle,
    turbine_place,
    turbine_tile,
    fringe_rows,
):
    count_x = lax.axis_size("gx")
    count_y = lax.axis_size("gy")
    tile_count = count_x * count_y
    tile_index = lax.axis_index("gx") * count_y + lax.axis_index("gy")
    components, width_x, width_y, height = adjoint_in.shape
    steps_total = checkpoints.shape[0]
    block_shape = checkpoints.shape[2:]
    owner_ids = jnp.arange(tile_count, dtype=jnp.int32)
    onehot = (send_owner[:, None] == owner_ids[None, :]).astype(jnp.int32)
    slot_rank = jnp.sum(jnp.cumsum(onehot, axis=0) * onehot, axis=1) - 1
    position = send_owner * CAP + slot_rank
    slots = send_owner.shape[0]
    row_ids = jnp.arange(tile_count * CAP, dtype=jnp.int32)
    pack_table = (row_ids[:, None] == position[None, :]).astype(jnp.bfloat16)
    pack_table = pack_table.reshape(tile_count, CAP, slots)
    pick_table = (receive_rows[:, None] == row_ids[None, :]).astype(jnp.bfloat16)
    pick_table = pick_table.reshape(receive_rows.shape[0], tile_count, CAP)
    rows_x = lax.axis_index("gx") * width_x + jnp.arange(width_x, dtype=jnp.int32)
    fringe_hit = jnp.any(rows_x[:, None] == fringe_rows[None, :], axis=1)
    fringe_scale = jnp.where(fringe_hit, FRINGE_KEEP, 1.0).astype(jnp.float32)
    owned_mask, plan_kernel, along_z, drag_field = turbine_terms(
        tile_index, thrust, yaw_angle, turbine_place, turbine_tile, width_x, width_y, height
    )
    turbine = turbine_tables(owned_mask, plan_kernel, along_z, width_x, width_y)
    adjoint = adjoint_in
    gradient_block = jnp.zeros((8, 128), jnp.float32)
    edges = (
        (adjoint[:, :1], adjoint[:, -1:]),
        (adjoint[:, :, :1], adjoint[:, :, -1:]),
    )
    for step_index in range(steps_total):
        stored = checkpoints[steps_total - 1 - step_index]
        packed = jnp.einsum(
            "drs,scb->dcrb", pack_table, stored, preferred_element_type=jnp.float32
        ).astype(jnp.bfloat16)
        arrived = lax.all_to_all(packed, ("gx", "gy"), split_axis=0, concat_axis=0, tiled=True)
        forward = jnp.einsum(
            "jsr,scrb->cjb", pick_table, arrived, preferred_element_type=jnp.float32
        ).astype(jnp.bfloat16)
        forward = forward.reshape(components, width_x, width_y, height)
        west, east = halo(*edges[0], "gx")
        south, north = halo(*edges[1], "gy")
        adjoint, gradient_block, first_plane, last_plane, first_row, last_row = advance(
            adjoint, west, east, south, north, forward, block_columns, eddy_blocks, drag_field, fringe_scale,
            turbine, gradient_block, step_index == steps_total - 1,
        )
        edges = ((first_plane, last_plane), (first_row, last_row))
    gradient_sum = gradient_block[0, : thrust.shape[0]]
    cosine = jnp.cos(yaw_angle)
    sine = jnp.sin(yaw_angle)
    control_gradient = jnp.stack(
        [
            -0.5 * TIME_STEP * cosine * cosine * gradient_sum,
            TIME_STEP * thrust * sine * cosine * gradient_sum,
        ]
    )
    return (adjoint, control_gradient)


def solution(mesh):
    return jax.shard_map(
        shards,
        mesh=mesh,
        in_specs=(
            P(None, "gx", "gy", None),
            P(None, ("gx", "gy"), None, None),
            P(("gx", "gy")),
            P(("gx", "gy")),
            P(("gx", "gy"), None),
            P(),
            P(),
            P(),
            P(),
            P(),
            P(),
        ),
        out_specs=(P(None, "gx", "gy", None), P()),
        check_vma=False,
    )
```

```python
import functools

import jax
import jax.numpy as jnp
from jax import lax
from jax.experimental import pallas as pl
from jax.experimental.pallas import tpu as pltpu
from jax.sharding import PartitionSpec as P

MESH = pl.DeviceIdType.MESH

PB = 128
KB = 8
CAP = 2
NZB = 2


TIME_STEP = 0.25
BASE_VISC = 0.1
EDDY_COEF = 0.5
KERNEL_WIDTH = 1.5
FRINGE_KEEP = 0.5


def turbine_terms(
    tile_index, thrust, yaw_angle, turbine_place, turbine_tile, width_x, width_y, height
):
    owned_mask = (turbine_tile == tile_index).astype(jnp.float32)
    spread = 2.0 * KERNEL_WIDTH * KERNEL_WIDTH
    along_x = jnp.exp(
        -(
            (jnp.arange(width_x, dtype=jnp.float32)[None, :] - turbine_place[0][:, None] * width_x)
            ** 2
        )
        / spread
    )
    along_y = jnp.exp(
        -(
            (jnp.arange(width_y, dtype=jnp.float32)[None, :] - turbine_place[1][:, None] * width_y)
            ** 2
        )
        / spread
    )
    along_z = jnp.exp(
        -(
            (
                jnp.arange(height, dtype=jnp.float32)[None, :]
                - turbine_place[2][:, None] * (0.5 * height)
            )
            ** 2
        )
        / spread
    )
    plan_kernel = (along_x[:, :, None] * along_y[:, None, :]).reshape(
        along_x.shape[0], width_x * width_y
    )
    cosine = jnp.cos(yaw_angle)
    loading = owned_mask * thrust * cosine * cosine
    drag_field = jnp.dot(
        (plan_kernel * loading[:, None]).T, along_z, precision=lax.Precision.HIGHEST
    )
    return (owned_mask, plan_kernel, along_z, drag_field.reshape(width_x, width_y, height))


def advance_kernel(count_y, group, exchange, *refs):
    (cols_ref, fringe_ref, a_ref, w_ref, e_ref, s_ref, n_ref, u_ref, drag_ref, eddy_ref, pk_ref, azh_ref,
     prior_ref, out_ref, sum_ref, first_plane, last_plane, first_row, last_row, xq, prod) = refs[:21]
    components, width_x, width_y, height = a_ref.shape
    if exchange:
        near, far, sems = refs[21:]
        total = lax.axis_size("gx") * count_y
        groups = total // group
        me = lax.axis_index("gx") * count_y + lax.axis_index("gy")
        mine, base = me % group, me - me % group

        def near_device(i):
            other = base + lax.rem(mine + i, group)
            return (other // count_y, other % count_y)

        def far_device(i):
            other = lax.rem(me + i * group, total)
            return (other // count_y, other % count_y)

        barrier = pltpu.get_barrier_semaphore()

        def greet_near(i, carry):
            pl.semaphore_signal(barrier, inc=1, device_id=near_device(i), device_id_type=MESH)
            return carry

        def greet_far(i, carry):
            pl.semaphore_signal(barrier, inc=1, device_id=far_device(i), device_id_type=MESH)
            return carry

        lax.fori_loop(1, group, greet_near, 0)
        lax.fori_loop(1, groups, greet_far, 0)

    def turbine_plane(x, acc):
        velocity = u_ref[0, x].astype(jnp.float32)
        density = velocity * velocity * a_ref[0, x]
        high = density.astype(jnp.bfloat16)
        low = (density - high.astype(jnp.float32)).astype(jnp.bfloat16)
        projected = (
            jnp.dot(high, azh_ref[0], preferred_element_type=jnp.float32)
            + jnp.dot(high, azh_ref[1], preferred_element_type=jnp.float32)
            + jnp.dot(low, azh_ref[0], preferred_element_type=jnp.float32)
        )
        return acc + pk_ref[x] * projected

    acc = lax.fori_loop(0, width_x, turbine_plane, jnp.zeros(pk_ref.shape[1:], jnp.float32))
    leading_row = lax.broadcasted_iota(jnp.int32, prior_ref.shape, 0) == 0
    part = prior_ref[...] + jnp.where(leading_row, jnp.sum(acc, axis=0, keepdims=True), 0.0)
    if exchange:
        pl.semaphore_wait(barrier, group + groups - 2)
        near[mine] = part

        def send_near(i, carry):
            pltpu.make_async_remote_copy(
                src_ref=near.at[mine], dst_ref=near.at[mine], send_sem=sems.at[0], recv_sem=sems.at[1],
                device_id=near_device(i), device_id_type=MESH,
            ).start()
            return carry

        lax.fori_loop(1, group, send_near, 0)
    else:
        sum_ref[...] = part

    half = height // NZB

    def fill_plane(x, carry):
        for zb in range(NZB):
            for c in range(components):
                xq[2 * (x + 1) + zb, c * width_y : (c + 1) * width_y, :] = a_ref[c, x, :, zb * half : (zb + 1) * half].astype(jnp.bfloat16)
        return carry

    for zb in range(NZB):
        for c in range(components):
            xq[zb, c * width_y : (c + 1) * width_y, :] = w_ref[c, 0, :, zb * half : (zb + 1) * half].astype(jnp.bfloat16)
            xq[2 * (width_x + 1) + zb, c * width_y : (c + 1) * width_y, :] = e_ref[c, 0, :, zb * half : (zb + 1) * half].astype(jnp.bfloat16)
    lax.fori_loop(0, width_x, fill_plane, 0)

    def eddy_block(p, carry):
        acc = jnp.zeros((components * width_y, half), jnp.float32)
        for k in range(0, KB, 2):
            pair = jnp.concatenate([xq[cols_ref[p, k]], xq[cols_ref[p, k + 1]]], axis=1)
            acc = acc + jnp.dot(pair, eddy_ref[k // 2], preferred_element_type=jnp.float32)
        prod[p] = acc
        return carry

    lax.fori_loop(0, width_x * NZB, eddy_block, 0)
    if exchange:
        first = pltpu.make_async_remote_copy(
            src_ref=near.at[pl.ds(0, group - 1)], dst_ref=near.at[pl.ds(0, group - 1)],
            send_sem=sems.at[0], recv_sem=sems.at[1], device_id=near_device(1), device_id_type=MESH,
        )
        first.wait_send()
        first.wait_recv()
        far[me // group] = jnp.sum(near[...], axis=0)

        def send_far(i, carry):
            pltpu.make_async_remote_copy(
                src_ref=far.at[me // group], dst_ref=far.at[me // group], send_sem=sems.at[2],
                recv_sem=sems.at[3], device_id=far_device(i), device_id_type=MESH,
            ).start()
            return carry

        lax.fori_loop(1, groups, send_far, 0)

    row = lax.broadcasted_iota(jnp.int32, (width_y, height), 0)
    lane = lax.broadcasted_iota(jnp.int32, (width_y, height), 1)

    def plane(x, west_of, east_of):
        u0 = u_ref[0, x].astype(jnp.float32)
        u1 = u_ref[1, x].astype(jnp.float32)
        u2 = u_ref[2, x].astype(jnp.float32)
        viscous = (TIME_STEP * EDDY_COEF) * jnp.sqrt(1.0 + (u0 * u0 + u1 * u1 + u2 * u2))
        diffuse = TIME_STEP * BASE_VISC
        carry_x, carry_y, carry_z = (0.5 * TIME_STEP) * u0, (0.5 * TIME_STEP) * u1, (0.5 * TIME_STEP) * u2
        east_weight, west_weight = diffuse + carry_x, diffuse - carry_x
        north_weight, south_weight = diffuse + carry_y, diffuse - carry_y
        upper_weight = jnp.where(lane == height - 1, 0.0, diffuse + carry_z)
        lower_weight = jnp.where(lane == 0, 0.0, diffuse - carry_z)
        centre_weight = 1.0 - 6.0 * diffuse
        drag = TIME_STEP * drag_ref[x] * u0
        scale = fringe_ref[x]
        for c in range(components):
            center = a_ref[c, x]
            north = jnp.where(row == width_y - 1, jnp.broadcast_to(n_ref[c, x], (width_y, height)), pltpu.roll(center, width_y - 1, 0))
            south = jnp.where(row == 0, jnp.broadcast_to(s_ref[c, x], (width_y, height)), pltpu.roll(center, 1, 0))
            product = jnp.concatenate(
                [prod[2 * x + zb, c * width_y : (c + 1) * width_y, :] for zb in range(NZB)], axis=1
            )
            update = (
                centre_weight * center
                + east_weight * east_of(c)
                + west_weight * west_of(c)
                + north_weight * north
                + south_weight * south
                + upper_weight * pltpu.roll(center, height - 1, 1)
                + lower_weight * pltpu.roll(center, 1, 1)
                + viscous * product
            )
            if c == 0:
                update = update - drag * center
            final = update * scale
            out_ref[c, x] = final
            first_row[c, x] = final[0:1, :]
            last_row[c, x] = final[width_y - 1 :, :]
            if isinstance(x, int) and x == 0:
                first_plane[c, 0] = final
            if isinstance(x, int) and x == width_x - 1:
                last_plane[c, 0] = final

    plane(0, lambda c: w_ref[c, 0], lambda c: a_ref[c, 1])

    def inner_plane(x, carry):
        plane(x, lambda c: a_ref[c, x - 1], lambda c: a_ref[c, x + 1])
        return carry

    lax.fori_loop(1, width_x - 1, inner_plane, 0)
    plane(width_x - 1, lambda c: a_ref[c, width_x - 2], lambda c: e_ref[c, 0])
    if exchange:
        second = pltpu.make_async_remote_copy(
            src_ref=far.at[pl.ds(0, groups - 1)], dst_ref=far.at[pl.ds(0, groups - 1)],
            send_sem=sems.at[2], recv_sem=sems.at[3], device_id=far_device(1), device_id_type=MESH,
        )
        second.wait_send()
        second.wait_recv()
        sum_ref[...] = jnp.sum(far[...], axis=0)


def advance(adjoint, west, east, south, north, forward, columns, eddy_blocks, drag_field, fringe_scale, turbine, prior, exchange):
    components, width_x, width_y, height = adjoint.shape
    vmem = pl.BlockSpec(memory_space=pltpu.VMEM)
    smem = pl.BlockSpec(memory_space=pltpu.SMEM)
    count_y = lax.axis_size("gy")
    total = lax.axis_size("gx") * count_y
    group = 8 if total % 8 == 0 and total > 8 else total // 2
    paired = eddy_blocks.reshape(KB // 2, 2 * eddy_blocks.shape[1], eddy_blocks.shape[2])
    operands = [columns, fringe_scale, adjoint, west, east, south, north, forward, drag_field, paired]
    operands += list(turbine) + [prior]
    out_shape = (
        jax.ShapeDtypeStruct(adjoint.shape, jnp.float32),
        jax.ShapeDtypeStruct(prior.shape, jnp.float32),
        jax.ShapeDtypeStruct((components, 1, width_y, height), jnp.float32),
        jax.ShapeDtypeStruct((components, 1, width_y, height), jnp.float32),
        jax.ShapeDtypeStruct((components, width_x, 1, height), jnp.float32),
        jax.ShapeDtypeStruct((components, width_x, 1, height), jnp.float32),
    )
    scratch = [
        pltpu.VMEM(((width_x + 2) * NZB, components * width_y, height // NZB), jnp.bfloat16),
        pltpu.VMEM((width_x * NZB, components * width_y, height // NZB), jnp.float32),
    ]
    params = dict(vmem_limit_bytes=48 * 1024 * 1024)
    if exchange:
        scratch += [
            pltpu.VMEM((group,) + prior.shape, jnp.float32),
            pltpu.VMEM((total // group,) + prior.shape, jnp.float32),
            pltpu.SemaphoreType.DMA((4,)),
        ]
        params.update(collective_id=0, has_side_effects=True)
    return pl.pallas_call(
        functools.partial(advance_kernel, count_y, group, exchange),
        out_shape=out_shape,
        in_specs=[smem, smem] + [vmem] * (len(operands) - 2),
        out_specs=tuple([vmem] * len(out_shape)),
        scratch_shapes=scratch,
        compiler_params=pltpu.CompilerParams(**params),
    )(*operands)


def turbine_tables(owned_mask, plan_kernel, along_z, width_x, width_y):
    lanes = 128
    count = plan_kernel.shape[0]
    weights = (plan_kernel * owned_mask[:, None]).T.reshape(width_x, width_y, count)
    weights = jnp.zeros((width_x, width_y, lanes), jnp.float32).at[:, :, :count].set(weights)
    column = jnp.zeros((along_z.shape[1], lanes), jnp.float32).at[:, :count].set(along_z.T)
    high = lax.reduce_precision(column, exponent_bits=8, mantissa_bits=7)
    low = column - high
    return weights, jnp.stack([high, low]).astype(jnp.bfloat16)


def halo_kernel(count_x, count_y, first_plane, last_plane, first_row, last_row, west, east, south, north, send, recv):
    gx, gy = lax.axis_index("gx"), lax.axis_index("gy")
    ahead_x, behind_x = lax.rem(gx + 1, count_x), lax.rem(gx + count_x - 1, count_x)
    ahead_y, behind_y = lax.rem(gy + 1, count_y), lax.rem(gy + count_y - 1, count_y)
    peers = [(ahead_x, gy), (behind_x, gy), (gx, ahead_y)]
    if count_y > 2:
        peers.append((gx, behind_y))
    barrier = pltpu.get_barrier_semaphore()
    for peer in peers:
        pl.semaphore_signal(barrier, inc=1, device_id=peer, device_id_type=MESH)
    pl.semaphore_wait(barrier, len(peers))
    routes = [
        (last_plane, west, (ahead_x, gy)),
        (first_plane, east, (behind_x, gy)),
        (last_row, south, (gx, ahead_y)),
        (first_row, north, (gx, behind_y)),
    ]
    copies = []
    for index, (source, target, peer) in enumerate(routes):
        copy = pltpu.make_async_remote_copy(
            src_ref=source, dst_ref=target, send_sem=send.at[index], recv_sem=recv.at[index],
            device_id=peer, device_id_type=MESH,
        )
        copy.start()
        copies.append(copy)
    for copy in copies:
        copy.wait()


def halos(edges, call):
    (first_plane, last_plane), (first_row, last_row) = edges
    vmem = pl.BlockSpec(memory_space=pltpu.VMEM)
    planes = jax.ShapeDtypeStruct(first_plane.shape, jnp.float32)
    rows = jax.ShapeDtypeStruct(first_row.shape, jnp.float32)
    return pl.pallas_call(
        functools.partial(halo_kernel, lax.axis_size("gx"), lax.axis_size("gy")),
        out_shape=(planes, planes, rows, rows),
        in_specs=[vmem] * 4,
        out_specs=(vmem,) * 4,
        scratch_shapes=[pltpu.SemaphoreType.DMA((4,)), pltpu.SemaphoreType.DMA((4,))],
        compiler_params=pltpu.CompilerParams(collective_id=1 + call, has_side_effects=True),
    )(first_plane, last_plane, first_row, last_row)


def shards(
    adjoint_in,
    checkpoints,
    send_owner,
    receive_rows,
    block_columns,
    eddy_blocks,
    thrust,
    yaw_angle,
    turbine_place,
    turbine_tile,
    fringe_rows,
):
    count_x = lax.axis_size("gx")
    count_y = lax.axis_size("gy")
    tile_count = count_x * count_y
    tile_index = lax.axis_index("gx") * count_y + lax.axis_index("gy")
    components, width_x, width_y, height = adjoint_in.shape
    steps_total = checkpoints.shape[0]
    block_shape = checkpoints.shape[2:]
    owner_ids = jnp.arange(tile_count, dtype=jnp.int32)
    onehot = (send_owner[:, None] == owner_ids[None, :]).astype(jnp.int32)
    slot_rank = jnp.sum(jnp.cumsum(onehot, axis=0) * onehot, axis=1) - 1
    position = send_owner * CAP + slot_rank
    slots = send_owner.shape[0]
    row_ids = jnp.arange(tile_count * CAP, dtype=jnp.int32)
    pack_table = (row_ids[:, None] == position[None, :]).astype(jnp.bfloat16)
    pack_table = pack_table.reshape(tile_count, CAP, slots)
    pick_table = (receive_rows[:, None] == row_ids[None, :]).astype(jnp.bfloat16)
    pick_table = pick_table.reshape(receive_rows.shape[0], tile_count, CAP)
    rows_x = lax.axis_index("gx") * width_x + jnp.arange(width_x, dtype=jnp.int32)
    fringe_hit = jnp.any(rows_x[:, None] == fringe_rows[None, :], axis=1)
    fringe_scale = jnp.where(fringe_hit, FRINGE_KEEP, 1.0).astype(jnp.float32)
    owned_mask, plan_kernel, along_z, drag_field = turbine_terms(
        tile_index, thrust, yaw_angle, turbine_place, turbine_tile, width_x, width_y, height
    )
    turbine = turbine_tables(owned_mask, plan_kernel, along_z, width_x, width_y)
    adjoint = adjoint_in
    gradient_block = jnp.zeros((8, 128), jnp.float32)
    edges = (
        (adjoint[:, :1], adjoint[:, -1:]),
        (adjoint[:, :, :1], adjoint[:, :, -1:]),
    )
    for step_index in range(steps_total):
        stored = checkpoints[steps_total - 1 - step_index]
        packed = jnp.einsum(
            "drs,scb->dcrb", pack_table, stored, preferred_element_type=jnp.float32
        ).astype(jnp.bfloat16)
        arrived = lax.all_to_all(packed, ("gx", "gy"), split_axis=0, concat_axis=0, tiled=True)
        forward = jnp.einsum(
            "jsr,scrb->cjb", pick_table, arrived, preferred_element_type=jnp.float32
        ).astype(jnp.bfloat16)
        forward = forward.reshape(components, width_x, width_y, height)
        west, east, south, north = halos(edges, step_index)
        adjoint, gradient_block, first_plane, last_plane, first_row, last_row = advance(
            adjoint, west, east, south, north, forward, block_columns, eddy_blocks, drag_field, fringe_scale,
            turbine, gradient_block, step_index == steps_total - 1,
        )
        edges = ((first_plane, last_plane), (first_row, last_row))
    gradient_sum = gradient_block[0, : thrust.shape[0]]
    cosine = jnp.cos(yaw_angle)
    sine = jnp.sin(yaw_angle)
    control_gradient = jnp.stack(
        [
            -0.5 * TIME_STEP * cosine * cosine * gradient_sum,
            TIME_STEP * thrust * sine * cosine * gradient_sum,
        ]
    )
    return (adjoint, control_gradient)


def solution(mesh):
    return jax.shard_map(
        shards,
        mesh=mesh,
        in_specs=(
            P(None, "gx", "gy", None),
            P(None, ("gx", "gy"), None, None),
            P(("gx", "gy")),
            P(("gx", "gy")),
            P(("gx", "gy"), None),
            P(),
            P(),
            P(),
            P(),
            P(),
            P(),
        ),
        out_specs=(P(None, "gx", "gy", None), P()),
        check_vma=False,
    )
```

```python
import functools

import jax
import jax.numpy as jnp
from jax import lax
from jax.experimental import pallas as pl
from jax.experimental.pallas import tpu as pltpu
from jax.sharding import PartitionSpec as P

MESH = pl.DeviceIdType.MESH

PB = 128
KB = 8
CAP = 2
NZB = 2


TIME_STEP = 0.25
BASE_VISC = 0.1
EDDY_COEF = 0.5
KERNEL_WIDTH = 1.5
FRINGE_KEEP = 0.5


def turbine_terms(
    tile_index, thrust, yaw_angle, turbine_place, turbine_tile, width_x, width_y, height
):
    owned_mask = (turbine_tile == tile_index).astype(jnp.float32)
    spread = 2.0 * KERNEL_WIDTH * KERNEL_WIDTH
    along_x = jnp.exp(
        -(
            (jnp.arange(width_x, dtype=jnp.float32)[None, :] - turbine_place[0][:, None] * width_x)
            ** 2
        )
        / spread
    )
    along_y = jnp.exp(
        -(
            (jnp.arange(width_y, dtype=jnp.float32)[None, :] - turbine_place[1][:, None] * width_y)
            ** 2
        )
        / spread
    )
    along_z = jnp.exp(
        -(
            (
                jnp.arange(height, dtype=jnp.float32)[None, :]
                - turbine_place[2][:, None] * (0.5 * height)
            )
            ** 2
        )
        / spread
    )
    plan_kernel = (along_x[:, :, None] * along_y[:, None, :]).reshape(
        along_x.shape[0], width_x * width_y
    )
    cosine = jnp.cos(yaw_angle)
    loading = owned_mask * thrust * cosine * cosine
    drag_field = jnp.dot(
        (plan_kernel * loading[:, None]).T, along_z, precision=lax.Precision.HIGHEST
    )
    return (owned_mask, plan_kernel, along_z, drag_field.reshape(width_x, width_y, height))


def advance_kernel(count_y, group, exchange, *refs):
    (cols_ref, fringe_ref, a_ref, w_ref, e_ref, s_ref, n_ref, u_ref, drag_ref, eddy_ref, pk_ref, azh_ref,
     prior_ref, out_ref, sum_ref, first_plane, last_plane, first_row, last_row, xq, prod) = refs[:21]
    components, width_x, width_y, height = a_ref.shape
    if exchange:
        near, far, sems = refs[21:]
        total = lax.axis_size("gx") * count_y
        groups = total // group
        me = lax.axis_index("gx") * count_y + lax.axis_index("gy")
        mine, base = me % group, me - me % group

        def near_device(i):
            other = base + lax.rem(mine + i, group)
            return (other // count_y, other % count_y)

        def far_device(i):
            other = lax.rem(me + i * group, total)
            return (other // count_y, other % count_y)

        barrier = pltpu.get_barrier_semaphore()

        def greet_near(i, carry):
            pl.semaphore_signal(barrier, inc=1, device_id=near_device(i), device_id_type=MESH)
            return carry

        def greet_far(i, carry):
            pl.semaphore_signal(barrier, inc=1, device_id=far_device(i), device_id_type=MESH)
            return carry

        lax.fori_loop(1, group, greet_near, 0)
        lax.fori_loop(1, groups, greet_far, 0)

    def turbine_plane(x, acc):
        velocity = u_ref[0, x].astype(jnp.float32)
        density = velocity * velocity * a_ref[0, x]
        high = density.astype(jnp.bfloat16)
        low = (density - high.astype(jnp.float32)).astype(jnp.bfloat16)
        projected = (
            jnp.dot(high, azh_ref[0], preferred_element_type=jnp.float32)
            + jnp.dot(high, azh_ref[1], preferred_element_type=jnp.float32)
            + jnp.dot(low, azh_ref[0], preferred_element_type=jnp.float32)
        )
        return acc + pk_ref[x] * projected

    acc = lax.fori_loop(0, width_x, turbine_plane, jnp.zeros(pk_ref.shape[1:], jnp.float32))
    leading_row = lax.broadcasted_iota(jnp.int32, prior_ref.shape, 0) == 0
    part = prior_ref[...] + jnp.where(leading_row, jnp.sum(acc, axis=0, keepdims=True), 0.0)
    half = height // NZB

    def fill_plane(x, carry):
        for zb in range(NZB):
            for c in range(components):
                xq[2 * (x + 1) + zb, c * width_y : (c + 1) * width_y, :] = a_ref[c, x, :, zb * half : (zb + 1) * half].astype(jnp.bfloat16)
        return carry

    for zb in range(NZB):
        for c in range(components):
            xq[zb, c * width_y : (c + 1) * width_y, :] = w_ref[c, 0, :, zb * half : (zb + 1) * half].astype(jnp.bfloat16)
            xq[2 * (width_x + 1) + zb, c * width_y : (c + 1) * width_y, :] = e_ref[c, 0, :, zb * half : (zb + 1) * half].astype(jnp.bfloat16)
    lax.fori_loop(0, width_x, fill_plane, 0)
    if exchange:
        pl.semaphore_wait(barrier, group + groups - 2)
        near[mine] = part

        def send_near(i, carry):
            pltpu.make_async_remote_copy(
                src_ref=near.at[mine], dst_ref=near.at[mine], send_sem=sems.at[0], recv_sem=sems.at[1],
                device_id=near_device(i), device_id_type=MESH,
            ).start()
            return carry

        lax.fori_loop(1, group, send_near, 0)
    else:
        sum_ref[...] = part

    def eddy_block(p, carry):
        acc = jnp.zeros((components * width_y, half), jnp.float32)
        for k in range(0, KB, 2):
            pair = jnp.concatenate([xq[cols_ref[p, k]], xq[cols_ref[p, k + 1]]], axis=1)
            acc = acc + jnp.dot(pair, eddy_ref[k // 2], preferred_element_type=jnp.float32)
        prod[p] = acc
        return carry

    lax.fori_loop(0, width_x * NZB, eddy_block, 0)
    if exchange:
        first = pltpu.make_async_remote_copy(
            src_ref=near.at[pl.ds(0, group - 1)], dst_ref=near.at[pl.ds(0, group - 1)],
            send_sem=sems.at[0], recv_sem=sems.at[1], device_id=near_device(1), device_id_type=MESH,
        )
        first.wait_send()
        first.wait_recv()
        far[me // group] = jnp.sum(near[...], axis=0)

        def send_far(i, carry):
            pltpu.make_async_remote_copy(
                src_ref=far.at[me // group], dst_ref=far.at[me // group], send_sem=sems.at[2],
                recv_sem=sems.at[3], device_id=far_device(i), device_id_type=MESH,
            ).start()
            return carry

        lax.fori_loop(1, groups, send_far, 0)

    row = lax.broadcasted_iota(jnp.int32, (width_y, height), 0)
    lane = lax.broadcasted_iota(jnp.int32, (width_y, height), 1)

    def plane(x, west_of, east_of):
        u0 = u_ref[0, x].astype(jnp.float32)
        u1 = u_ref[1, x].astype(jnp.float32)
        u2 = u_ref[2, x].astype(jnp.float32)
        viscous = (TIME_STEP * EDDY_COEF) * jnp.sqrt(1.0 + (u0 * u0 + u1 * u1 + u2 * u2))
        diffuse = TIME_STEP * BASE_VISC
        carry_x, carry_y, carry_z = (0.5 * TIME_STEP) * u0, (0.5 * TIME_STEP) * u1, (0.5 * TIME_STEP) * u2
        east_weight, west_weight = diffuse + carry_x, diffuse - carry_x
        north_weight, south_weight = diffuse + carry_y, diffuse - carry_y
        upper_weight = jnp.where(lane == height - 1, 0.0, diffuse + carry_z)
        lower_weight = jnp.where(lane == 0, 0.0, diffuse - carry_z)
        centre_weight = 1.0 - 6.0 * diffuse
        drag = TIME_STEP * drag_ref[x] * u0
        scale = fringe_ref[x]
        for c in range(components):
            center = a_ref[c, x]
            north = jnp.where(row == width_y - 1, jnp.broadcast_to(n_ref[c, x], (width_y, height)), pltpu.roll(center, width_y - 1, 0))
            south = jnp.where(row == 0, jnp.broadcast_to(s_ref[c, x], (width_y, height)), pltpu.roll(center, 1, 0))
            product = jnp.concatenate(
                [prod[2 * x + zb, c * width_y : (c + 1) * width_y, :] for zb in range(NZB)], axis=1
            )
            update = (
                centre_weight * center
                + east_weight * east_of(c)
                + west_weight * west_of(c)
                + north_weight * north
                + south_weight * south
                + upper_weight * pltpu.roll(center, height - 1, 1)
                + lower_weight * pltpu.roll(center, 1, 1)
                + viscous * product
            )
            if c == 0:
                update = update - drag * center
            final = update * scale
            out_ref[c, x] = final
            first_row[c, x] = final[0:1, :]
            last_row[c, x] = final[width_y - 1 :, :]
            if isinstance(x, int) and x == 0:
                first_plane[c, 0] = final
            if isinstance(x, int) and x == width_x - 1:
                last_plane[c, 0] = final

    plane(0, lambda c: w_ref[c, 0], lambda c: a_ref[c, 1])

    def inner_plane(x, carry):
        plane(x, lambda c: a_ref[c, x - 1], lambda c: a_ref[c, x + 1])
        return carry

    lax.fori_loop(1, width_x - 1, inner_plane, 0)
    plane(width_x - 1, lambda c: a_ref[c, width_x - 2], lambda c: e_ref[c, 0])
    if exchange:
        second = pltpu.make_async_remote_copy(
            src_ref=far.at[pl.ds(0, groups - 1)], dst_ref=far.at[pl.ds(0, groups - 1)],
            send_sem=sems.at[2], recv_sem=sems.at[3], device_id=far_device(1), device_id_type=MESH,
        )
        second.wait_send()
        second.wait_recv()
        sum_ref[...] = jnp.sum(far[...], axis=0)


def advance(adjoint, west, east, south, north, forward, columns, eddy_blocks, drag_field, fringe_scale, turbine, prior, exchange):
    components, width_x, width_y, height = adjoint.shape
    vmem = pl.BlockSpec(memory_space=pltpu.VMEM)
    smem = pl.BlockSpec(memory_space=pltpu.SMEM)
    count_y = lax.axis_size("gy")
    total = lax.axis_size("gx") * count_y
    group = 8 if total % 8 == 0 and total > 8 else total // 2
    paired = eddy_blocks.reshape(KB // 2, 2 * eddy_blocks.shape[1], eddy_blocks.shape[2])
    operands = [columns, fringe_scale, adjoint, west, east, south, north, forward, drag_field, paired]
    operands += list(turbine) + [prior]
    out_shape = (
        jax.ShapeDtypeStruct(adjoint.shape, jnp.float32),
        jax.ShapeDtypeStruct(prior.shape, jnp.float32),
        jax.ShapeDtypeStruct((components, 1, width_y, height), jnp.float32),
        jax.ShapeDtypeStruct((components, 1, width_y, height), jnp.float32),
        jax.ShapeDtypeStruct((components, width_x, 1, height), jnp.float32),
        jax.ShapeDtypeStruct((components, width_x, 1, height), jnp.float32),
    )
    scratch = [
        pltpu.VMEM(((width_x + 2) * NZB, components * width_y, height // NZB), jnp.bfloat16),
        pltpu.VMEM((width_x * NZB, components * width_y, height // NZB), jnp.float32),
    ]
    params = dict(vmem_limit_bytes=48 * 1024 * 1024)
    if exchange:
        scratch += [
            pltpu.VMEM((group,) + prior.shape, jnp.float32),
            pltpu.VMEM((total // group,) + prior.shape, jnp.float32),
            pltpu.SemaphoreType.DMA((4,)),
        ]
        params.update(collective_id=0, has_side_effects=True)
    return pl.pallas_call(
        functools.partial(advance_kernel, count_y, group, exchange),
        out_shape=out_shape,
        in_specs=[smem, smem] + [vmem] * (len(operands) - 2),
        out_specs=tuple([vmem] * len(out_shape)),
        scratch_shapes=scratch,
        compiler_params=pltpu.CompilerParams(**params),
    )(*operands)


def turbine_tables(owned_mask, plan_kernel, along_z, width_x, width_y):
    lanes = 128
    count = plan_kernel.shape[0]
    weights = (plan_kernel * owned_mask[:, None]).T.reshape(width_x, width_y, count)
    weights = jnp.zeros((width_x, width_y, lanes), jnp.float32).at[:, :, :count].set(weights)
    column = jnp.zeros((along_z.shape[1], lanes), jnp.float32).at[:, :count].set(along_z.T)
    high = lax.reduce_precision(column, exponent_bits=8, mantissa_bits=7)
    low = column - high
    return weights, jnp.stack([high, low]).astype(jnp.bfloat16)


def halo(first, last, axis):
    count = lax.axis_size(axis)
    forward = [(i, (i + 1) % count) for i in range(count)]
    backward = [(target, source) for source, target in forward]
    return lax.ppermute(last, axis, forward), lax.ppermute(first, axis, backward)


def shards(
    adjoint_in,
    checkpoints,
    send_owner,
    receive_rows,
    block_columns,
    eddy_blocks,
    thrust,
    yaw_angle,
    turbine_place,
    turbine_tile,
    fringe_rows,
):
    count_x = lax.axis_size("gx")
    count_y = lax.axis_size("gy")
    tile_count = count_x * count_y
    tile_index = lax.axis_index("gx") * count_y + lax.axis_index("gy")
    components, width_x, width_y, height = adjoint_in.shape
    steps_total = checkpoints.shape[0]
    block_shape = checkpoints.shape[2:]
    owner_ids = jnp.arange(tile_count, dtype=jnp.int32)
    onehot = (send_owner[:, None] == owner_ids[None, :]).astype(jnp.int32)
    slot_rank = jnp.sum(jnp.cumsum(onehot, axis=0) * onehot, axis=1) - 1
    position = send_owner * CAP + slot_rank
    slots = send_owner.shape[0]
    row_ids = jnp.arange(tile_count * CAP, dtype=jnp.int32)
    pack_table = (row_ids[:, None] == position[None, :]).astype(jnp.bfloat16)
    pack_table = pack_table.reshape(tile_count, CAP, slots)
    pick_table = (receive_rows[:, None] == row_ids[None, :]).astype(jnp.bfloat16)
    pick_table = pick_table.reshape(receive_rows.shape[0], tile_count, CAP)
    rows_x = lax.axis_index("gx") * width_x + jnp.arange(width_x, dtype=jnp.int32)
    fringe_hit = jnp.any(rows_x[:, None] == fringe_rows[None, :], axis=1)
    fringe_scale = jnp.where(fringe_hit, FRINGE_KEEP, 1.0).astype(jnp.float32)
    owned_mask, plan_kernel, along_z, drag_field = turbine_terms(
        tile_index, thrust, yaw_angle, turbine_place, turbine_tile, width_x, width_y, height
    )
    turbine = turbine_tables(owned_mask, plan_kernel, along_z, width_x, width_y)
    adjoint = adjoint_in
    gradient_block = jnp.zeros((8, 128), jnp.float32)
    edges = (
        (adjoint[:, :1], adjoint[:, -1:]),
        (adjoint[:, :, :1], adjoint[:, :, -1:]),
    )
    for step_index in range(steps_total):
        stored = checkpoints[steps_total - 1 - step_index]
        packed = jnp.einsum(
            "drs,scb->dcrb", pack_table, stored, preferred_element_type=jnp.float32
        ).astype(jnp.bfloat16)
        arrived = lax.all_to_all(packed, ("gx", "gy"), split_axis=0, concat_axis=0, tiled=True)
        forward = jnp.einsum(
            "jsr,scrb->cjb", pick_table, arrived, preferred_element_type=jnp.float32
        ).astype(jnp.bfloat16)
        forward = forward.reshape(components, width_x, width_y, height)
        west, east = halo(*edges[0], "gx")
        south, north = halo(*edges[1], "gy")
        adjoint, gradient_block, first_plane, last_plane, first_row, last_row = advance(
            adjoint, west, east, south, north, forward, block_columns, eddy_blocks, drag_field, fringe_scale,
            turbine, gradient_block, step_index == steps_total - 1,
        )
        edges = ((first_plane, last_plane), (first_row, last_row))
    gradient_sum = gradient_block[0, : thrust.shape[0]]
    cosine = jnp.cos(yaw_angle)
    sine = jnp.sin(yaw_angle)
    control_gradient = jnp.stack(
        [
            -0.5 * TIME_STEP * cosine * cosine * gradient_sum,
            TIME_STEP * thrust * sine * cosine * gradient_sum,
        ]
    )
    return (adjoint, control_gradient)


def solution(mesh):
    return jax.shard_map(
        shards,
        mesh=mesh,
        in_specs=(
            P(None, "gx", "gy", None),
            P(None, ("gx", "gy"), None, None),
            P(("gx", "gy")),
            P(("gx", "gy")),
            P(("gx", "gy"), None),
            P(),
            P(),
            P(),
            P(),
            P(),
            P(),
        ),
        out_specs=(P(None, "gx", "gy", None), P()),
        check_vma=False,
    )
```

```python
import functools

import jax
import jax.numpy as jnp
from jax import lax
from jax.experimental import pallas as pl
from jax.experimental.pallas import tpu as pltpu
from jax.sharding import PartitionSpec as P

MESH = pl.DeviceIdType.MESH

PB = 128
KB = 8
CAP = 2
NZB = 2


TIME_STEP = 0.25
BASE_VISC = 0.1
EDDY_COEF = 0.5
KERNEL_WIDTH = 1.5
FRINGE_KEEP = 0.5


def turbine_terms(
    tile_index, thrust, yaw_angle, turbine_place, turbine_tile, width_x, width_y, height
):
    owned_mask = (turbine_tile == tile_index).astype(jnp.float32)
    spread = 2.0 * KERNEL_WIDTH * KERNEL_WIDTH
    along_x = jnp.exp(
        -(
            (jnp.arange(width_x, dtype=jnp.float32)[None, :] - turbine_place[0][:, None] * width_x)
            ** 2
        )
        / spread
    )
    along_y = jnp.exp(
        -(
            (jnp.arange(width_y, dtype=jnp.float32)[None, :] - turbine_place[1][:, None] * width_y)
            ** 2
        )
        / spread
    )
    along_z = jnp.exp(
        -(
            (
                jnp.arange(height, dtype=jnp.float32)[None, :]
                - turbine_place[2][:, None] * (0.5 * height)
            )
            ** 2
        )
        / spread
    )
    plan_kernel = (along_x[:, :, None] * along_y[:, None, :]).reshape(
        along_x.shape[0], width_x * width_y
    )
    cosine = jnp.cos(yaw_angle)
    loading = owned_mask * thrust * cosine * cosine
    drag_field = jnp.dot(
        (plan_kernel * loading[:, None]).T, along_z, precision=lax.Precision.HIGHEST
    )
    return (owned_mask, plan_kernel, along_z, drag_field.reshape(width_x, width_y, height))


def advance_kernel(count_y, group, exchange, *refs):
    (cols_ref, fringe_ref, a_ref, w_ref, e_ref, s_ref, n_ref, u_ref, drag_ref, eddy_ref, pk_ref, azh_ref,
     prior_ref, out_ref, sum_ref, first_plane, last_plane, first_row, last_row, xq, prod) = refs[:21]
    components, width_x, width_y, height = a_ref.shape
    if exchange:
        near, far, sems = refs[21:]
        total = lax.axis_size("gx") * count_y
        groups = total // group
        me = lax.axis_index("gx") * count_y + lax.axis_index("gy")
        mine, base = me % group, me - me % group

        def near_device(i):
            other = base + lax.rem(mine + i, group)
            return (other // count_y, other % count_y)

        def far_device(i):
            other = lax.rem(me + i * group, total)
            return (other // count_y, other % count_y)

        barrier = pltpu.get_barrier_semaphore()

        def greet_near(i, carry):
            pl.semaphore_signal(barrier, inc=1, device_id=near_device(i), device_id_type=MESH)
            return carry

        def greet_far(i, carry):
            pl.semaphore_signal(barrier, inc=1, device_id=far_device(i), device_id_type=MESH)
            return carry

        lax.fori_loop(1, group, greet_near, 0)
        lax.fori_loop(1, groups, greet_far, 0)

    def turbine_plane(x, acc):
        velocity = u_ref[0, x].astype(jnp.float32)
        density = velocity * velocity * a_ref[0, x]
        high = density.astype(jnp.bfloat16)
        low = (density - high.astype(jnp.float32)).astype(jnp.bfloat16)
        projected = (
            jnp.dot(high, azh_ref[0], preferred_element_type=jnp.float32)
            + jnp.dot(high, azh_ref[1], preferred_element_type=jnp.float32)
            + jnp.dot(low, azh_ref[0], preferred_element_type=jnp.float32)
        )
        return acc + pk_ref[x] * projected

    acc = lax.fori_loop(0, width_x, turbine_plane, jnp.zeros(pk_ref.shape[1:], jnp.float32))
    leading_row = lax.broadcasted_iota(jnp.int32, prior_ref.shape, 0) == 0
    part = prior_ref[...] + jnp.where(leading_row, jnp.sum(acc, axis=0, keepdims=True), 0.0)
    if exchange:
        pl.semaphore_wait(barrier, group + groups - 2)
        near[mine] = part

        def send_near(i, carry):
            pltpu.make_async_remote_copy(
                src_ref=near.at[mine], dst_ref=near.at[mine], send_sem=sems.at[0], recv_sem=sems.at[1],
                device_id=near_device(i), device_id_type=MESH,
            ).start()
            return carry

        lax.fori_loop(1, group, send_near, 0)
    else:
        sum_ref[...] = part

    half = height // NZB

    def fill_plane(x, carry):
        for zb in range(NZB):
            for c in range(components):
                xq[2 * (x + 1) + zb, c * width_y : (c + 1) * width_y, :] = a_ref[c, x, :, zb * half : (zb + 1) * half].astype(jnp.bfloat16)
        return carry

    for zb in range(NZB):
        for c in range(components):
            xq[zb, c * width_y : (c + 1) * width_y, :] = w_ref[c, 0, :, zb * half : (zb + 1) * half].astype(jnp.bfloat16)
            xq[2 * (width_x + 1) + zb, c * width_y : (c + 1) * width_y, :] = e_ref[c, 0, :, zb * half : (zb + 1) * half].astype(jnp.bfloat16)
    lax.fori_loop(0, width_x, fill_plane, 0)

    def eddy_block(p, carry):
        acc = jnp.zeros((components * width_y, half), jnp.float32)
        for k in range(0, KB, 2):
            pair = jnp.concatenate([xq[cols_ref[p, k]], xq[cols_ref[p, k + 1]]], axis=1)
            acc = acc + jnp.dot(pair, eddy_ref[k // 2], preferred_element_type=jnp.float32)
        prod[p] = acc
        return carry

    lax.fori_loop(0, width_x * NZB, eddy_block, 0)
    if exchange:
        first = pltpu.make_async_remote_copy(
            src_ref=near.at[pl.ds(0, group - 1)], dst_ref=near.at[pl.ds(0, group - 1)],
            send_sem=sems.at[0], recv_sem=sems.at[1], device_id=near_device(1), device_id_type=MESH,
        )
        first.wait_send()
        first.wait_recv()
        far[me // group] = jnp.sum(near[...], axis=0)

        def send_far(i, carry):
            pltpu.make_async_remote_copy(
                src_ref=far.at[me // group], dst_ref=far.at[me // group], send_sem=sems.at[2],
                recv_sem=sems.at[3], device_id=far_device(i), device_id_type=MESH,
            ).start()
            return carry

        lax.fori_loop(1, groups, send_far, 0)

    row = lax.broadcasted_iota(jnp.int32, (width_y, height), 0)
    lane = lax.broadcasted_iota(jnp.int32, (width_y, height), 1)

    def plane(x, west_of, east_of):
        u0 = u_ref[0, x].astype(jnp.float32)
        u1 = u_ref[1, x].astype(jnp.float32)
        u2 = u_ref[2, x].astype(jnp.float32)
        viscous = (TIME_STEP * EDDY_COEF) * jnp.sqrt(1.0 + (u0 * u0 + u1 * u1 + u2 * u2))
        diffuse = TIME_STEP * BASE_VISC
        carry_x, carry_y, carry_z = (0.5 * TIME_STEP) * u0, (0.5 * TIME_STEP) * u1, (0.5 * TIME_STEP) * u2
        east_weight, west_weight = diffuse + carry_x, diffuse - carry_x
        north_weight, south_weight = diffuse + carry_y, diffuse - carry_y
        upper_weight = jnp.where(lane == height - 1, 0.0, diffuse + carry_z)
        lower_weight = jnp.where(lane == 0, 0.0, diffuse - carry_z)
        centre_weight = 1.0 - 6.0 * diffuse
        drag = TIME_STEP * drag_ref[x] * u0
        scale = fringe_ref[x]
        for c in range(components):
            center = a_ref[c, x]
            north = jnp.where(row == width_y - 1, jnp.broadcast_to(n_ref[c, x], (width_y, height)), pltpu.roll(center, width_y - 1, 0))
            south = jnp.where(row == 0, jnp.broadcast_to(s_ref[c, x], (width_y, height)), pltpu.roll(center, 1, 0))
            product = jnp.concatenate(
                [prod[2 * x + zb, c * width_y : (c + 1) * width_y, :] for zb in range(NZB)], axis=1
            )
            update = (
                centre_weight * center
                + east_weight * east_of(c)
                + west_weight * west_of(c)
                + north_weight * north
                + south_weight * south
                + upper_weight * pltpu.roll(center, height - 1, 1)
                + lower_weight * pltpu.roll(center, 1, 1)
                + viscous * product
            )
            if c == 0:
                update = update - drag * center
            final = update * scale
            out_ref[c, x] = final
            first_row[c, x] = final[0:1, :]
            last_row[c, x] = final[width_y - 1 :, :]
            if isinstance(x, int) and x == 0:
                first_plane[c, 0] = final
            if isinstance(x, int) and x == width_x - 1:
                last_plane[c, 0] = final

    plane(0, lambda c: w_ref[c, 0], lambda c: a_ref[c, 1])

    def inner_plane(x, carry):
        plane(x, lambda c: a_ref[c, x - 1], lambda c: a_ref[c, x + 1])
        return carry

    lax.fori_loop(1, width_x - 1, inner_plane, 0)
    plane(width_x - 1, lambda c: a_ref[c, width_x - 2], lambda c: e_ref[c, 0])
    if exchange:
        second = pltpu.make_async_remote_copy(
            src_ref=far.at[pl.ds(0, groups - 1)], dst_ref=far.at[pl.ds(0, groups - 1)],
            send_sem=sems.at[2], recv_sem=sems.at[3], device_id=far_device(1), device_id_type=MESH,
        )
        second.wait_send()
        second.wait_recv()
        sum_ref[...] = jnp.sum(far[...], axis=0)


def advance(adjoint, west, east, south, north, forward, columns, eddy_blocks, drag_field, fringe_scale, turbine, prior, exchange):
    components, width_x, width_y, height = adjoint.shape
    vmem = pl.BlockSpec(memory_space=pltpu.VMEM)
    smem = pl.BlockSpec(memory_space=pltpu.SMEM)
    count_y = lax.axis_size("gy")
    total = lax.axis_size("gx") * count_y
    group = 8 if total % 8 == 0 and total > 8 else total // 2
    paired = eddy_blocks.reshape(KB // 2, 2 * eddy_blocks.shape[1], eddy_blocks.shape[2])
    operands = [columns, fringe_scale, adjoint, west, east, south, north, forward, drag_field, paired]
    operands += list(turbine) + [prior]
    out_shape = (
        jax.ShapeDtypeStruct(adjoint.shape, jnp.float32),
        jax.ShapeDtypeStruct(prior.shape, jnp.float32),
        jax.ShapeDtypeStruct((components, 1, width_y, height), jnp.float32),
        jax.ShapeDtypeStruct((components, 1, width_y, height), jnp.float32),
        jax.ShapeDtypeStruct((components, width_x, 1, height), jnp.float32),
        jax.ShapeDtypeStruct((components, width_x, 1, height), jnp.float32),
    )
    scratch = [
        pltpu.VMEM(((width_x + 2) * NZB, components * width_y, height // NZB), jnp.bfloat16),
        pltpu.VMEM((width_x * NZB, components * width_y, height // NZB), jnp.float32),
    ]
    params = dict(vmem_limit_bytes=48 * 1024 * 1024)
    if exchange:
        scratch += [
            pltpu.VMEM((group,) + prior.shape, jnp.float32),
            pltpu.VMEM((total // group,) + prior.shape, jnp.float32),
            pltpu.SemaphoreType.DMA((4,)),
        ]
        params.update(collective_id=0, has_side_effects=True)
    return pl.pallas_call(
        functools.partial(advance_kernel, count_y, group, exchange),
        out_shape=out_shape,
        in_specs=[smem, smem] + [vmem] * (len(operands) - 2),
        out_specs=tuple([vmem] * len(out_shape)),
        scratch_shapes=scratch,
        compiler_params=pltpu.CompilerParams(**params),
    )(*operands)


def turbine_tables(owned_mask, plan_kernel, along_z, width_x, width_y):
    lanes = 128
    count = plan_kernel.shape[0]
    weights = (plan_kernel * owned_mask[:, None]).T.reshape(width_x, width_y, count)
    weights = jnp.zeros((width_x, width_y, lanes), jnp.float32).at[:, :, :count].set(weights)
    column = jnp.zeros((along_z.shape[1], lanes), jnp.float32).at[:, :count].set(along_z.T)
    high = lax.reduce_precision(column, exponent_bits=8, mantissa_bits=7)
    low = column - high
    return weights, jnp.stack([high, low]).astype(jnp.bfloat16)


def halo(first, last, axis):
    count = lax.axis_size(axis)
    forward = [(i, (i + 1) % count) for i in range(count)]
    backward = [(target, source) for source, target in forward]
    return lax.ppermute(last, axis, forward), lax.ppermute(first, axis, backward)


def shards(
    adjoint_in,
    checkpoints,
    send_owner,
    receive_rows,
    block_columns,
    eddy_blocks,
    thrust,
    yaw_angle,
    turbine_place,
    turbine_tile,
    fringe_rows,
):
    count_x = lax.axis_size("gx")
    count_y = lax.axis_size("gy")
    tile_count = count_x * count_y
    tile_index = lax.axis_index("gx") * count_y + lax.axis_index("gy")
    components, width_x, width_y, height = adjoint_in.shape
    steps_total = checkpoints.shape[0]
    block_shape = checkpoints.shape[2:]
    owner_ids = jnp.arange(tile_count, dtype=jnp.int32)
    onehot = (send_owner[:, None] == owner_ids[None, :]).astype(jnp.int32)
    slot_rank = jnp.sum(jnp.cumsum(onehot, axis=0) * onehot, axis=1) - 1
    position = send_owner * CAP + slot_rank
    slots = send_owner.shape[0]
    row_ids = jnp.arange(tile_count * CAP, dtype=jnp.int32)
    pack_table = (row_ids[:, None] == position[None, :]).astype(jnp.bfloat16)
    pack_table = pack_table.reshape(tile_count, CAP, slots)
    pick_table = (receive_rows[:, None] == row_ids[None, :]).astype(jnp.bfloat16)
    pick_table = pick_table.reshape(receive_rows.shape[0], tile_count, CAP)
    rows_x = lax.axis_index("gx") * width_x + jnp.arange(width_x, dtype=jnp.int32)
    fringe_hit = jnp.any(rows_x[:, None] == fringe_rows[None, :], axis=1)
    fringe_scale = jnp.where(fringe_hit, FRINGE_KEEP, 1.0).astype(jnp.float32)
    owned_mask, plan_kernel, along_z, drag_field = turbine_terms(
        tile_index, thrust, yaw_angle, turbine_place, turbine_tile, width_x, width_y, height
    )
    turbine = turbine_tables(owned_mask, plan_kernel, along_z, width_x, width_y)
    adjoint = adjoint_in
    gradient_block = jnp.zeros((8, 128), jnp.float32)
    edges = (
        (adjoint[:, :1], adjoint[:, -1:]),
        (adjoint[:, :, :1], adjoint[:, :, -1:]),
    )
    for step_index in range(steps_total):
        stored = checkpoints[steps_total - 1 - step_index]
        packed = jnp.einsum(
            "drs,scb->dcrb", pack_table, stored, preferred_element_type=jnp.float32
        ).astype(jnp.bfloat16)
        arrived = lax.all_to_all(packed, ("gx", "gy"), split_axis=0, concat_axis=0, tiled=True)
        forward = jnp.einsum(
            "scrb,jsr->cjb", arrived, pick_table, preferred_element_type=jnp.float32
        )
        forward = forward.reshape(components, width_x, width_y, height).astype(jnp.bfloat16)
        west, east = halo(*edges[0], "gx")
        south, north = halo(*edges[1], "gy")
        adjoint, gradient_block, first_plane, last_plane, first_row, last_row = advance(
            adjoint, west, east, south, north, forward, block_columns, eddy_blocks, drag_field, fringe_scale,
            turbine, gradient_block, step_index == steps_total - 1,
        )
        edges = ((first_plane, last_plane), (first_row, last_row))
    gradient_sum = gradient_block[0, : thrust.shape[0]]
    cosine = jnp.cos(yaw_angle)
    sine = jnp.sin(yaw_angle)
    control_gradient = jnp.stack(
        [
            -0.5 * TIME_STEP * cosine * cosine * gradient_sum,
            TIME_STEP * thrust * sine * cosine * gradient_sum,
        ]
    )
    return (adjoint, control_gradient)


def solution(mesh):
    return jax.shard_map(
        shards,
        mesh=mesh,
        in_specs=(
            P(None, "gx", "gy", None),
            P(None, ("gx", "gy"), None, None),
            P(("gx", "gy")),
            P(("gx", "gy")),
            P(("gx", "gy"), None),
            P(),
            P(),
            P(),
            P(),
            P(),
            P(),
        ),
        out_specs=(P(None, "gx", "gy", None), P()),
        check_vma=False,
    )
```

```python
import functools

import jax
import jax.numpy as jnp
from jax import lax
from jax.experimental import pallas as pl
from jax.experimental.pallas import tpu as pltpu
from jax.sharding import PartitionSpec as P

MESH = pl.DeviceIdType.MESH

PB = 128
KB = 8
CAP = 2
NZB = 2


TIME_STEP = 0.25
BASE_VISC = 0.1
EDDY_COEF = 0.5
KERNEL_WIDTH = 1.5
FRINGE_KEEP = 0.5


def turbine_terms(
    tile_index, thrust, yaw_angle, turbine_place, turbine_tile, width_x, width_y, height
):
    owned_mask = (turbine_tile == tile_index).astype(jnp.float32)
    spread = 2.0 * KERNEL_WIDTH * KERNEL_WIDTH
    along_x = jnp.exp(
        -(
            (jnp.arange(width_x, dtype=jnp.float32)[None, :] - turbine_place[0][:, None] * width_x)
            ** 2
        )
        / spread
    )
    along_y = jnp.exp(
        -(
            (jnp.arange(width_y, dtype=jnp.float32)[None, :] - turbine_place[1][:, None] * width_y)
            ** 2
        )
        / spread
    )
    along_z = jnp.exp(
        -(
            (
                jnp.arange(height, dtype=jnp.float32)[None, :]
                - turbine_place[2][:, None] * (0.5 * height)
            )
            ** 2
        )
        / spread
    )
    plan_kernel = (along_x[:, :, None] * along_y[:, None, :]).reshape(
        along_x.shape[0], width_x * width_y
    )
    cosine = jnp.cos(yaw_angle)
    loading = owned_mask * thrust * cosine * cosine
    drag_field = jnp.dot(
        (plan_kernel * loading[:, None]).T, along_z, precision=lax.Precision.HIGHEST
    )
    return (owned_mask, plan_kernel, along_z, drag_field.reshape(width_x, width_y, height))


def advance_kernel(count_y, group, exchange, *refs):
    (cols_ref, fringe_ref, a_ref, w_ref, e_ref, s_ref, n_ref, u_ref, drag_ref, eddy_ref, pk_ref, azh_ref,
     prior_ref, out_ref, sum_ref, first_plane, last_plane, first_row, last_row, xq, prod) = refs[:21]
    components, width_x, width_y, height = a_ref.shape
    if exchange:
        near, far, sems = refs[21:]
        total = lax.axis_size("gx") * count_y
        groups = total // group
        me = lax.axis_index("gx") * count_y + lax.axis_index("gy")
        mine, base = me % group, me - me % group

        def near_device(i):
            other = base + lax.rem(mine + i, group)
            return (other // count_y, other % count_y)

        def far_device(i):
            other = lax.rem(me + i * group, total)
            return (other // count_y, other % count_y)

        barrier = pltpu.get_barrier_semaphore()

        def greet_near(i, carry):
            pl.semaphore_signal(barrier, inc=1, device_id=near_device(i), device_id_type=MESH)
            return carry

        def greet_far(i, carry):
            pl.semaphore_signal(barrier, inc=1, device_id=far_device(i), device_id_type=MESH)
            return carry

        lax.fori_loop(1, group, greet_near, 0)
        lax.fori_loop(1, groups, greet_far, 0)

    def turbine_plane(x, acc):
        velocity = u_ref[0, x].astype(jnp.float32)
        density = velocity * velocity * a_ref[0, x]
        high = density.astype(jnp.bfloat16)
        low = (density - high.astype(jnp.float32)).astype(jnp.bfloat16)
        projected = (
            jnp.dot(high, azh_ref[0], preferred_element_type=jnp.float32)
            + jnp.dot(high, azh_ref[1], preferred_element_type=jnp.float32)
            + jnp.dot(low, azh_ref[0], preferred_element_type=jnp.float32)
        )
        return acc + pk_ref[x] * projected

    acc = lax.fori_loop(0, width_x, turbine_plane, jnp.zeros(pk_ref.shape[1:], jnp.float32))
    leading_row = lax.broadcasted_iota(jnp.int32, prior_ref.shape, 0) == 0
    part = prior_ref[...] + jnp.where(leading_row, jnp.sum(acc, axis=0, keepdims=True), 0.0)
    if exchange:
        pl.semaphore_wait(barrier, group + groups - 2)
        near[mine] = part

        def send_near(i, carry):
            pltpu.make_async_remote_copy(
                src_ref=near.at[mine], dst_ref=near.at[mine], send_sem=sems.at[0], recv_sem=sems.at[1],
                device_id=near_device(i), device_id_type=MESH,
            ).start()
            return carry

        lax.fori_loop(1, group, send_near, 0)
    else:
        sum_ref[...] = part

    half = height // NZB

    def fill_plane(x, carry):
        for zb in range(NZB):
            for c in range(components):
                xq[2 * (x + 1) + zb, c * width_y : (c + 1) * width_y, :] = a_ref[c, x, :, zb * half : (zb + 1) * half].astype(jnp.bfloat16)
        return carry

    for zb in range(NZB):
        for c in range(components):
            xq[zb, c * width_y : (c + 1) * width_y, :] = w_ref[c, 0, :, zb * half : (zb + 1) * half].astype(jnp.bfloat16)
            xq[2 * (width_x + 1) + zb, c * width_y : (c + 1) * width_y, :] = e_ref[c, 0, :, zb * half : (zb + 1) * half].astype(jnp.bfloat16)
    lax.fori_loop(0, width_x, fill_plane, 0)

    def eddy_block(p, carry):
        acc = jnp.zeros((components * width_y, half), jnp.float32)
        for k in range(0, KB, 2):
            pair = jnp.concatenate([xq[cols_ref[p, k]], xq[cols_ref[p, k + 1]]], axis=1)
            acc = acc + jnp.dot(pair, eddy_ref[k // 2], preferred_element_type=jnp.float32)
        prod[p] = acc
        return carry

    lax.fori_loop(0, width_x * NZB, eddy_block, 0)
    if exchange:
        first = pltpu.make_async_remote_copy(
            src_ref=near.at[pl.ds(0, group - 1)], dst_ref=near.at[pl.ds(0, group - 1)],
            send_sem=sems.at[0], recv_sem=sems.at[1], device_id=near_device(1), device_id_type=MESH,
        )
        first.wait_send()
        first.wait_recv()
        far[me // group] = jnp.sum(near[...], axis=0)

        def send_far(i, carry):
            pltpu.make_async_remote_copy(
                src_ref=far.at[me // group], dst_ref=far.at[me // group], send_sem=sems.at[2],
                recv_sem=sems.at[3], device_id=far_device(i), device_id_type=MESH,
            ).start()
            return carry

        lax.fori_loop(1, groups, send_far, 0)

    row = lax.broadcasted_iota(jnp.int32, (width_y, height), 0)
    lane = lax.broadcasted_iota(jnp.int32, (width_y, height), 1)

    def plane(x, west_of, east_of):
        u0 = u_ref[0, x].astype(jnp.float32)
        u1 = u_ref[1, x].astype(jnp.float32)
        u2 = u_ref[2, x].astype(jnp.float32)
        viscous = (TIME_STEP * EDDY_COEF) * jnp.sqrt(1.0 + (u0 * u0 + u1 * u1 + u2 * u2))
        diffuse = TIME_STEP * BASE_VISC
        carry_x, carry_y, carry_z = (0.5 * TIME_STEP) * u0, (0.5 * TIME_STEP) * u1, (0.5 * TIME_STEP) * u2
        east_weight, west_weight = diffuse + carry_x, diffuse - carry_x
        north_weight, south_weight = diffuse + carry_y, diffuse - carry_y
        upper_weight = jnp.where(lane == height - 1, 0.0, diffuse + carry_z)
        lower_weight = jnp.where(lane == 0, 0.0, diffuse - carry_z)
        centre_weight = 1.0 - 6.0 * diffuse
        drag = TIME_STEP * drag_ref[x] * u0
        scale = fringe_ref[x]
        for c in range(components):
            center = a_ref[c, x]
            north = jnp.where(row == width_y - 1, jnp.broadcast_to(n_ref[c, x], (width_y, height)), pltpu.roll(center, width_y - 1, 0))
            south = jnp.where(row == 0, jnp.broadcast_to(s_ref[c, x], (width_y, height)), pltpu.roll(center, 1, 0))
            product = jnp.concatenate(
                [prod[2 * x + zb, c * width_y : (c + 1) * width_y, :] for zb in range(NZB)], axis=1
            )
            update = (
                centre_weight * center
                + east_weight * east_of(c)
                + west_weight * west_of(c)
                + north_weight * north
                + south_weight * south
                + upper_weight * pltpu.roll(center, height - 1, 1)
                + lower_weight * pltpu.roll(center, 1, 1)
                + viscous * product
            )
            if c == 0:
                update = update - drag * center
            final = update if exchange else update * scale
            out_ref[c, x] = final
            first_row[c, x] = final[0:1, :]
            last_row[c, x] = final[width_y - 1 :, :]
            if isinstance(x, int) and x == 0:
                first_plane[c, 0] = final
            if isinstance(x, int) and x == width_x - 1:
                last_plane[c, 0] = final

    plane(0, lambda c: w_ref[c, 0], lambda c: a_ref[c, 1])

    def inner_plane(x, carry):
        plane(x, lambda c: a_ref[c, x - 1], lambda c: a_ref[c, x + 1])
        return carry

    lax.fori_loop(1, width_x - 1, inner_plane, 0)
    plane(width_x - 1, lambda c: a_ref[c, width_x - 2], lambda c: e_ref[c, 0])
    if exchange:
        second = pltpu.make_async_remote_copy(
            src_ref=far.at[pl.ds(0, groups - 1)], dst_ref=far.at[pl.ds(0, groups - 1)],
            send_sem=sems.at[2], recv_sem=sems.at[3], device_id=far_device(1), device_id_type=MESH,
        )
        second.wait_send()
        second.wait_recv()
        sum_ref[...] = jnp.sum(far[...], axis=0)


def advance(adjoint, west, east, south, north, forward, columns, eddy_blocks, drag_field, fringe_scale, turbine, prior, exchange):
    components, width_x, width_y, height = adjoint.shape
    vmem = pl.BlockSpec(memory_space=pltpu.VMEM)
    smem = pl.BlockSpec(memory_space=pltpu.SMEM)
    count_y = lax.axis_size("gy")
    total = lax.axis_size("gx") * count_y
    group = 8 if total % 8 == 0 and total > 8 else total // 2
    paired = eddy_blocks.reshape(KB // 2, 2 * eddy_blocks.shape[1], eddy_blocks.shape[2])
    operands = [columns, fringe_scale, adjoint, west, east, south, north, forward, drag_field, paired]
    operands += list(turbine) + [prior]
    out_shape = (
        jax.ShapeDtypeStruct(adjoint.shape, jnp.float32),
        jax.ShapeDtypeStruct(prior.shape, jnp.float32),
        jax.ShapeDtypeStruct((components, 1, width_y, height), jnp.float32),
        jax.ShapeDtypeStruct((components, 1, width_y, height), jnp.float32),
        jax.ShapeDtypeStruct((components, width_x, 1, height), jnp.float32),
        jax.ShapeDtypeStruct((components, width_x, 1, height), jnp.float32),
    )
    scratch = [
        pltpu.VMEM(((width_x + 2) * NZB, components * width_y, height // NZB), jnp.bfloat16),
        pltpu.VMEM((width_x * NZB, components * width_y, height // NZB), jnp.float32),
    ]
    params = dict(vmem_limit_bytes=48 * 1024 * 1024)
    if exchange:
        scratch += [
            pltpu.VMEM((group,) + prior.shape, jnp.float32),
            pltpu.VMEM((total // group,) + prior.shape, jnp.float32),
            pltpu.SemaphoreType.DMA((4,)),
        ]
        params.update(collective_id=0, has_side_effects=True)
    return pl.pallas_call(
        functools.partial(advance_kernel, count_y, group, exchange),
        out_shape=out_shape,
        in_specs=[smem, smem] + [vmem] * (len(operands) - 2),
        out_specs=tuple([vmem] * len(out_shape)),
        scratch_shapes=scratch,
        compiler_params=pltpu.CompilerParams(**params),
    )(*operands)


def turbine_tables(owned_mask, plan_kernel, along_z, width_x, width_y):
    lanes = 128
    count = plan_kernel.shape[0]
    weights = (plan_kernel * owned_mask[:, None]).T.reshape(width_x, width_y, count)
    weights = jnp.zeros((width_x, width_y, lanes), jnp.float32).at[:, :, :count].set(weights)
    column = jnp.zeros((along_z.shape[1], lanes), jnp.float32).at[:, :count].set(along_z.T)
    high = lax.reduce_precision(column, exponent_bits=8, mantissa_bits=7)
    low = column - high
    return weights, jnp.stack([high, low]).astype(jnp.bfloat16)


def halo(first, last, axis):
    count = lax.axis_size(axis)
    forward = [(i, (i + 1) % count) for i in range(count)]
    backward = [(target, source) for source, target in forward]
    return lax.ppermute(last, axis, forward), lax.ppermute(first, axis, backward)


def shards(
    adjoint_in,
    checkpoints,
    send_owner,
    receive_rows,
    block_columns,
    eddy_blocks,
    thrust,
    yaw_angle,
    turbine_place,
    turbine_tile,
    fringe_rows,
):
    count_x = lax.axis_size("gx")
    count_y = lax.axis_size("gy")
    tile_count = count_x * count_y
    tile_index = lax.axis_index("gx") * count_y + lax.axis_index("gy")
    components, width_x, width_y, height = adjoint_in.shape
    steps_total = checkpoints.shape[0]
    block_shape = checkpoints.shape[2:]
    owner_ids = jnp.arange(tile_count, dtype=jnp.int32)
    onehot = (send_owner[:, None] == owner_ids[None, :]).astype(jnp.int32)
    slot_rank = jnp.sum(jnp.cumsum(onehot, axis=0) * onehot, axis=1) - 1
    position = send_owner * CAP + slot_rank
    slots = send_owner.shape[0]
    row_ids = jnp.arange(tile_count * CAP, dtype=jnp.int32)
    pack_table = (row_ids[:, None] == position[None, :]).astype(jnp.bfloat16)
    pack_table = pack_table.reshape(tile_count, CAP, slots)
    pick_table = (receive_rows[:, None] == row_ids[None, :]).astype(jnp.bfloat16)
    pick_table = pick_table.reshape(receive_rows.shape[0], tile_count, CAP)
    rows_x = lax.axis_index("gx") * width_x + jnp.arange(width_x, dtype=jnp.int32)
    fringe_hit = jnp.any(rows_x[:, None] == fringe_rows[None, :], axis=1)
    fringe_scale = jnp.where(fringe_hit, FRINGE_KEEP, 1.0).astype(jnp.float32)
    owned_mask, plan_kernel, along_z, drag_field = turbine_terms(
        tile_index, thrust, yaw_angle, turbine_place, turbine_tile, width_x, width_y, height
    )
    turbine = turbine_tables(owned_mask, plan_kernel, along_z, width_x, width_y)
    adjoint = adjoint_in
    gradient_block = jnp.zeros((8, 128), jnp.float32)
    edges = (
        (adjoint[:, :1], adjoint[:, -1:]),
        (adjoint[:, :, :1], adjoint[:, :, -1:]),
    )
    for step_index in range(steps_total):
        stored = checkpoints[steps_total - 1 - step_index]
        packed = jnp.einsum(
            "drs,scb->dcrb", pack_table, stored, preferred_element_type=jnp.float32
        ).astype(jnp.bfloat16)
        arrived = lax.all_to_all(packed, ("gx", "gy"), split_axis=0, concat_axis=0, tiled=True)
        forward = jnp.einsum(
            "jsr,scrb->cjb", pick_table, arrived, preferred_element_type=jnp.float32
        ).astype(jnp.bfloat16)
        forward = forward.reshape(components, width_x, width_y, height)
        west, east = halo(*edges[0], "gx")
        south, north = halo(*edges[1], "gy")
        adjoint, gradient_block, first_plane, last_plane, first_row, last_row = advance(
            adjoint, west, east, south, north, forward, block_columns, eddy_blocks, drag_field, fringe_scale,
            turbine, gradient_block, step_index == steps_total - 1,
        )
        edges = ((first_plane, last_plane), (first_row, last_row))
    adjoint = adjoint * fringe_scale[None, :, None, None]
    gradient_sum = gradient_block[0, : thrust.shape[0]]
    cosine = jnp.cos(yaw_angle)
    sine = jnp.sin(yaw_angle)
    control_gradient = jnp.stack(
        [
            -0.5 * TIME_STEP * cosine * cosine * gradient_sum,
            TIME_STEP * thrust * sine * cosine * gradient_sum,
        ]
    )
    return (adjoint, control_gradient)


def solution(mesh):
    return jax.shard_map(
        shards,
        mesh=mesh,
        in_specs=(
            P(None, "gx", "gy", None),
            P(None, ("gx", "gy"), None, None),
            P(("gx", "gy")),
            P(("gx", "gy")),
            P(("gx", "gy"), None),
            P(),
            P(),
            P(),
            P(),
            P(),
            P(),
        ),
        out_specs=(P(None, "gx", "gy", None), P()),
        check_vma=False,
    )
```

```python
import functools

import jax
import jax.numpy as jnp
from jax import lax
from jax.experimental import pallas as pl
from jax.experimental.pallas import tpu as pltpu
from jax.sharding import PartitionSpec as P

MESH = pl.DeviceIdType.MESH

PB = 128
KB = 8
CAP = 2
NZB = 2


TIME_STEP = 0.25
BASE_VISC = 0.1
EDDY_COEF = 0.5
KERNEL_WIDTH = 1.5
FRINGE_KEEP = 0.5


def turbine_terms(
    tile_index, thrust, yaw_angle, turbine_place, turbine_tile, width_x, width_y, height
):
    owned_mask = (turbine_tile == tile_index).astype(jnp.float32)
    spread = 2.0 * KERNEL_WIDTH * KERNEL_WIDTH
    along_x = jnp.exp(
        -(
            (jnp.arange(width_x, dtype=jnp.float32)[None, :] - turbine_place[0][:, None] * width_x)
            ** 2
        )
        / spread
    )
    along_y = jnp.exp(
        -(
            (jnp.arange(width_y, dtype=jnp.float32)[None, :] - turbine_place[1][:, None] * width_y)
            ** 2
        )
        / spread
    )
    along_z = jnp.exp(
        -(
            (
                jnp.arange(height, dtype=jnp.float32)[None, :]
                - turbine_place[2][:, None] * (0.5 * height)
            )
            ** 2
        )
        / spread
    )
    plan_kernel = (along_x[:, :, None] * along_y[:, None, :]).reshape(
        along_x.shape[0], width_x * width_y
    )
    cosine = jnp.cos(yaw_angle)
    loading = owned_mask * thrust * cosine * cosine
    drag_field = jnp.dot(
        (plan_kernel * loading[:, None]).T, along_z, precision=lax.Precision.HIGHEST
    )
    return (owned_mask, plan_kernel, along_z, drag_field.reshape(width_x, width_y, height))


def advance_kernel(count_y, group, exchange, *refs):
    (cols_ref, fringe_ref, a_ref, w_ref, e_ref, s_ref, n_ref, u_ref, drag_ref, eddy_ref, pk_ref, azh_ref,
     prior_ref, out_ref, sum_ref, first_plane, last_plane, first_row, last_row, xq, prod) = refs[:21]
    components, width_x, width_y, height = a_ref.shape
    if exchange:
        near, far, sems = refs[21:]
        total = lax.axis_size("gx") * count_y
        groups = total // group
        me = lax.axis_index("gx") * count_y + lax.axis_index("gy")
        mine, base = me % group, me - me % group

        def near_device(i):
            other = base + lax.rem(mine + i, group)
            return (other // count_y, other % count_y)

        def far_device(i):
            other = lax.rem(me + i * group, total)
            return (other // count_y, other % count_y)

        barrier = pltpu.get_barrier_semaphore()

        def greet_near(i, carry):
            pl.semaphore_signal(barrier, inc=1, device_id=near_device(i), device_id_type=MESH)
            return carry

        def greet_far(i, carry):
            pl.semaphore_signal(barrier, inc=1, device_id=far_device(i), device_id_type=MESH)
            return carry

        lax.fori_loop(1, group, greet_near, 0)
        lax.fori_loop(1, groups, greet_far, 0)

    def turbine_plane(x, acc):
        velocity = u_ref[0, x].astype(jnp.float32)
        density = velocity * velocity * a_ref[0, x]
        high = density.astype(jnp.bfloat16)
        low = (density - high.astype(jnp.float32)).astype(jnp.bfloat16)
        projected = (
            jnp.dot(high, azh_ref[0], preferred_element_type=jnp.float32)
            + jnp.dot(high, azh_ref[1], preferred_element_type=jnp.float32)
            + jnp.dot(low, azh_ref[0], preferred_element_type=jnp.float32)
        )
        return acc + pk_ref[x] * projected

    acc = lax.fori_loop(0, width_x, turbine_plane, jnp.zeros(pk_ref.shape[1:], jnp.float32))
    leading_row = lax.broadcasted_iota(jnp.int32, prior_ref.shape, 0) == 0
    part = prior_ref[...] + jnp.where(leading_row, jnp.sum(acc, axis=0, keepdims=True), 0.0)
    if exchange:
        pl.semaphore_wait(barrier, group + groups - 2)
        near[mine] = part

        def send_near(i, carry):
            pltpu.make_async_remote_copy(
                src_ref=near.at[mine], dst_ref=near.at[mine], send_sem=sems.at[0], recv_sem=sems.at[1],
                device_id=near_device(i), device_id_type=MESH,
            ).start()
            return carry

        lax.fori_loop(1, group, send_near, 0)
    else:
        sum_ref[...] = part

    half = height // NZB

    def fill_plane(x, carry):
        for zb in range(NZB):
            for c in range(components):
                xq[2 * (x + 1) + zb, c * width_y : (c + 1) * width_y, :] = a_ref[c, x, :, zb * half : (zb + 1) * half].astype(jnp.bfloat16)
        return carry

    for zb in range(NZB):
        for c in range(components):
            xq[zb, c * width_y : (c + 1) * width_y, :] = w_ref[c, 0, :, zb * half : (zb + 1) * half].astype(jnp.bfloat16)
            xq[2 * (width_x + 1) + zb, c * width_y : (c + 1) * width_y, :] = e_ref[c, 0, :, zb * half : (zb + 1) * half].astype(jnp.bfloat16)
    lax.fori_loop(0, width_x, fill_plane, 0)

    def eddy_block(p, carry):
        acc = jnp.zeros((components * width_y, half), jnp.float32)
        for k in range(0, KB, 2):
            pair = jnp.concatenate([xq[cols_ref[p, k]], xq[cols_ref[p, k + 1]]], axis=1)
            acc = acc + jnp.dot(pair, eddy_ref[k // 2], preferred_element_type=jnp.float32)
        prod[p] = acc
        return carry

    lax.fori_loop(0, width_x * NZB, eddy_block, 0)
    if exchange:
        first = pltpu.make_async_remote_copy(
            src_ref=near.at[pl.ds(0, group - 1)], dst_ref=near.at[pl.ds(0, group - 1)],
            send_sem=sems.at[0], recv_sem=sems.at[1], device_id=near_device(1), device_id_type=MESH,
        )
        first.wait_send()
        first.wait_recv()
        far[me // group] = jnp.sum(near[...], axis=0)

        def send_far(i, carry):
            pltpu.make_async_remote_copy(
                src_ref=far.at[me // group], dst_ref=far.at[me // group], send_sem=sems.at[2],
                recv_sem=sems.at[3], device_id=far_device(i), device_id_type=MESH,
            ).start()
            return carry

        lax.fori_loop(1, groups, send_far, 0)

    row = lax.broadcasted_iota(jnp.int32, (width_y, height), 0)
    lane = lax.broadcasted_iota(jnp.int32, (width_y, height), 1)

    def plane(x, west_of, east_of):
        u0 = u_ref[0, x].astype(jnp.float32)
        u1 = u_ref[1, x].astype(jnp.float32)
        u2 = u_ref[2, x].astype(jnp.float32)
        viscous = (TIME_STEP * EDDY_COEF) * jnp.sqrt(1.0 + (u0 * u0 + u1 * u1 + u2 * u2))
        diffuse = TIME_STEP * BASE_VISC
        carry_x, carry_y, carry_z = (0.5 * TIME_STEP) * u0, (0.5 * TIME_STEP) * u1, (0.5 * TIME_STEP) * u2
        east_weight, west_weight = diffuse + carry_x, diffuse - carry_x
        north_weight, south_weight = diffuse + carry_y, diffuse - carry_y
        upper_weight = jnp.where(lane == height - 1, 0.0, diffuse + carry_z)
        lower_weight = jnp.where(lane == 0, 0.0, diffuse - carry_z)
        centre_weight = 1.0 - 6.0 * diffuse
        drag = TIME_STEP * drag_ref[x] * u0
        scale = fringe_ref[x]
        for c in range(components):
            center = a_ref[c, x]
            north = jnp.where(row == width_y - 1, jnp.broadcast_to(n_ref[c, x], (width_y, height)), pltpu.roll(center, width_y - 1, 0))
            south = jnp.where(row == 0, jnp.broadcast_to(s_ref[c, x], (width_y, height)), pltpu.roll(center, 1, 0))
            product = jnp.concatenate(
                [prod[2 * x + zb, c * width_y : (c + 1) * width_y, :] for zb in range(NZB)], axis=1
            )
            update = (
                centre_weight * center
                + east_weight * east_of(c)
                + west_weight * west_of(c)
                + north_weight * north
                + south_weight * south
                + upper_weight * pltpu.roll(center, height - 1, 1)
                + lower_weight * pltpu.roll(center, 1, 1)
                + viscous * product
            )
            if c == 0:
                update = update - drag * center
            final = update if exchange else update * scale
            out_ref[c, x] = final
            first_row[c, x] = final[0:1, :]
            last_row[c, x] = final[width_y - 1 :, :]
            if isinstance(x, int) and x == 0:
                first_plane[c, 0] = final
            if isinstance(x, int) and x == width_x - 1:
                last_plane[c, 0] = final

    plane(0, lambda c: w_ref[c, 0], lambda c: a_ref[c, 1])

    def inner_plane(x, carry):
        plane(x, lambda c: a_ref[c, x - 1], lambda c: a_ref[c, x + 1])
        return carry

    lax.fori_loop(1, width_x - 1, inner_plane, 0)
    plane(width_x - 1, lambda c: a_ref[c, width_x - 2], lambda c: e_ref[c, 0])
    if exchange:
        second = pltpu.make_async_remote_copy(
            src_ref=far.at[pl.ds(0, groups - 1)], dst_ref=far.at[pl.ds(0, groups - 1)],
            send_sem=sems.at[2], recv_sem=sems.at[3], device_id=far_device(1), device_id_type=MESH,
        )
        second.wait_send()
        second.wait_recv()
        sum_ref[...] = jnp.sum(far[...], axis=0)


def advance(adjoint, west, east, south, north, forward, columns, eddy_blocks, drag_field, fringe_scale, turbine, prior, exchange):
    components, width_x, width_y, height = adjoint.shape
    vmem = pl.BlockSpec(memory_space=pltpu.VMEM)
    smem = pl.BlockSpec(memory_space=pltpu.SMEM)
    count_y = lax.axis_size("gy")
    total = lax.axis_size("gx") * count_y
    group = 8 if total % 8 == 0 and total > 8 else total // 2
    paired = eddy_blocks.reshape(KB // 2, 2 * eddy_blocks.shape[1], eddy_blocks.shape[2])
    operands = [columns, fringe_scale, adjoint, west, east, south, north, forward, drag_field, paired]
    operands += list(turbine) + [prior]
    out_shape = (
        jax.ShapeDtypeStruct(adjoint.shape, jnp.float32),
        jax.ShapeDtypeStruct(prior.shape, jnp.float32),
        jax.ShapeDtypeStruct((components, 1, width_y, height), jnp.float32),
        jax.ShapeDtypeStruct((components, 1, width_y, height), jnp.float32),
        jax.ShapeDtypeStruct((components, width_x, 1, height), jnp.float32),
        jax.ShapeDtypeStruct((components, width_x, 1, height), jnp.float32),
    )
    scratch = [
        pltpu.VMEM(((width_x + 2) * NZB, components * width_y, height // NZB), jnp.bfloat16),
        pltpu.VMEM((width_x * NZB, components * width_y, height // NZB), jnp.float32),
    ]
    params = dict(vmem_limit_bytes=48 * 1024 * 1024)
    if exchange:
        scratch += [
            pltpu.VMEM((group,) + prior.shape, jnp.float32),
            pltpu.VMEM((total // group,) + prior.shape, jnp.float32),
            pltpu.SemaphoreType.DMA((4,)),
        ]
        params.update(collective_id=0, has_side_effects=True)
    return pl.pallas_call(
        functools.partial(advance_kernel, count_y, group, exchange),
        out_shape=out_shape,
        in_specs=[smem, smem] + [vmem] * (len(operands) - 2),
        out_specs=tuple([vmem] * len(out_shape)),
        scratch_shapes=scratch,
        compiler_params=pltpu.CompilerParams(**params),
    )(*operands)


def turbine_tables(owned_mask, plan_kernel, along_z, width_x, width_y):
    lanes = 128
    count = plan_kernel.shape[0]
    weights = (plan_kernel * owned_mask[:, None]).T.reshape(width_x, width_y, count)
    weights = jnp.zeros((width_x, width_y, lanes), jnp.float32).at[:, :, :count].set(weights)
    column = jnp.zeros((along_z.shape[1], lanes), jnp.float32).at[:, :count].set(along_z.T)
    high = lax.reduce_precision(column, exponent_bits=8, mantissa_bits=7)
    low = column - high
    return weights, jnp.stack([high, low]).astype(jnp.bfloat16)


def halo(first, last, axis):
    count = lax.axis_size(axis)
    forward = [(i, (i + 1) % count) for i in range(count)]
    backward = [(target, source) for source, target in forward]
    return lax.ppermute(last, axis, forward), lax.ppermute(first, axis, backward)


def shards(
    adjoint_in,
    checkpoints,
    send_owner,
    receive_rows,
    block_columns,
    eddy_blocks,
    thrust,
    yaw_angle,
    turbine_place,
    turbine_tile,
    fringe_rows,
):
    count_x = lax.axis_size("gx")
    count_y = lax.axis_size("gy")
    tile_count = count_x * count_y
    tile_index = lax.axis_index("gx") * count_y + lax.axis_index("gy")
    components, width_x, width_y, height = adjoint_in.shape
    steps_total = checkpoints.shape[0]
    block_shape = checkpoints.shape[2:]
    owner_ids = jnp.arange(tile_count, dtype=jnp.int32)
    onehot = (send_owner[:, None] == owner_ids[None, :]).astype(jnp.int32)
    slot_rank = jnp.sum(jnp.cumsum(onehot, axis=0) * onehot, axis=1) - 1
    position = send_owner * CAP + slot_rank
    slots = send_owner.shape[0]
    row_ids = jnp.arange(tile_count * CAP, dtype=jnp.int32)
    pack_table = (row_ids[:, None] == position[None, :]).astype(jnp.bfloat16)
    pack_table = pack_table.reshape(tile_count, CAP, slots)
    pick_table = (receive_rows[:, None] == row_ids[None, :]).astype(jnp.bfloat16)
    pick_table = pick_table.reshape(receive_rows.shape[0], tile_count, CAP)
    rows_x = lax.axis_index("gx") * width_x + jnp.arange(width_x, dtype=jnp.int32)
    fringe_hit = jnp.any(rows_x[:, None] == fringe_rows[None, :], axis=1)
    fringe_scale = jnp.where(fringe_hit, FRINGE_KEEP, 1.0).astype(jnp.float32)
    owned_mask, plan_kernel, along_z, drag_field = turbine_terms(
        tile_index, thrust, yaw_angle, turbine_place, turbine_tile, width_x, width_y, height
    )
    turbine = turbine_tables(owned_mask, plan_kernel, along_z, width_x, width_y)
    adjoint = adjoint_in
    gradient_block = jnp.zeros((8, 128), jnp.float32)
    edges = (
        (adjoint[:, :1], adjoint[:, -1:]),
        (adjoint[:, :, :1], adjoint[:, :, -1:]),
    )
    for step_index in range(steps_total):
        stored = checkpoints[steps_total - 1 - step_index]
        packed = jnp.einsum(
            "drs,scb->dcrb", pack_table, stored, preferred_element_type=jnp.float32
        ).astype(jnp.bfloat16)
        arrived = lax.all_to_all(packed, ("gx", "gy"), split_axis=0, concat_axis=0, tiled=True)
        forward = jnp.einsum(
            "scrb,jsr->cjb", arrived, pick_table, preferred_element_type=jnp.float32
        )
        forward = forward.reshape(components, width_x, width_y, height).astype(jnp.bfloat16)
        west, east = halo(*edges[0], "gx")
        south, north = halo(*edges[1], "gy")
        adjoint, gradient_block, first_plane, last_plane, first_row, last_row = advance(
            adjoint, west, east, south, north, forward, block_columns, eddy_blocks, drag_field, fringe_scale,
            turbine, gradient_block, step_index == steps_total - 1,
        )
        edges = ((first_plane, last_plane), (first_row, last_row))
    adjoint = adjoint * fringe_scale[None, :, None, None]
    gradient_sum = gradient_block[0, : thrust.shape[0]]
    cosine = jnp.cos(yaw_angle)
    sine = jnp.sin(yaw_angle)
    control_gradient = jnp.stack(
        [
            -0.5 * TIME_STEP * cosine * cosine * gradient_sum,
            TIME_STEP * thrust * sine * cosine * gradient_sum,
        ]
    )
    return (adjoint, control_gradient)


def solution(mesh):
    return jax.shard_map(
        shards,
        mesh=mesh,
        in_specs=(
            P(None, "gx", "gy", None),
            P(None, ("gx", "gy"), None, None),
            P(("gx", "gy")),
            P(("gx", "gy")),
            P(("gx", "gy"), None),
            P(),
            P(),
            P(),
            P(),
            P(),
            P(),
        ),
        out_specs=(P(None, "gx", "gy", None), P()),
        check_vma=False,
    )
```
